32 devices in a mesh: tile: 8 (over z, x), chan: 4 (over y, core).
Axes of the slice: x: 2, y: 2, z: 4, core: 2. Of those that a mesh axis runs over, the one named last changes fastest.
Arguments:
- tokens: bfloat16 [512, 512], P('tile', 'chan'), may hold values from -6 to 6
- cell_source: int32 [8, 64], replicated, may hold values from 0 to 511, as said below
- gain: float32 [512], P('chan'), may hold values from 0.5 to 1.5
- shift: float32 [512], P('chan'), may hold values from -3 to 3
- weight: bfloat16 [27, 512, 512], P(None, None, 'chan'), may hold values from -0.0546875 to 0.0546875
- bias: float32 [512], P('chan'), may hold values from -3 to 3
- cotangent: bfloat16 [8, 2, 8, 16, 512], P('tile', None, None, None, 'chan'), may hold values from -6 to 6
Outputs:
- decoded: bfloat16 [8, 2, 8, 16, 512], P('tile', None, None, None, 'chan')
- token_grad: bfloat16 [512, 512], P('tile', 'chan')
The draws below stay inside these ranges and needn't reach their ends.
Inputs may be any that keep to these rules, and one draw needn't show every extreme that they name: `cell_source`: every token fills exactly one cell. Token t is held by owner t // 64. A tile takes either none or exactly 16 of its cells from an owner, and those 16 tokens are consecutive in the owner's order starting at a multiple of 16; the set of differences (tile - owner) mod 8 from which a tile takes cells is the same for every tile.
All inputs are finite; a program needn't handle non-finite values.
Results may differ from the reference program's by a relative error of at most 0.0041.
Values may be sent and summed in bfloat16 or wider, within the bound.
No kernel may reach another device: no remote copies, remote signals or barrier semaphores. Data moves between devices by JAX's collectives and lax.ppermute only.
A program may use at most 64 MiB of HBM per device.

```python
import jax
import jax.numpy as jnp
from jax import lax

CHANNELS = 512
GROUPS = 32
FRAMES = 2
TILE_H = 4
TILE_W = 8
TILES = 8
TILE_COLS = 8
TILE_ROWS = 1
CELLS = 64
TOKENS = 512
CAP = 16


def draw_cell_source(key, part):
    first_key, second_key = jax.random.split(jax.random.fold_in(key, 11))
    blocks = CELLS // CAP
    ranking = jax.random.permutation(first_key, TILES).astype(jnp.int32)
    candidates = jnp.arange(TILES, dtype=jnp.int32)
    priority = jnp.where(candidates == 1, -3, jnp.where(candidates == TILES - 1, -2, jnp.where(candidates == TILES // 2, -1, ranking)))
    offsets = jnp.argsort(priority)[:blocks].astype(jnp.int32)
    tile_ids = jnp.arange(TILES, dtype=jnp.int32)[:, None, None]
    block_ids = jnp.arange(blocks, dtype=jnp.int32)[None, :, None]
    within = jnp.arange(CAP, dtype=jnp.int32)[None, None, :]
    owners = (tile_ids - offsets[None, :, None]) % TILES
    ordered = (owners * CELLS + block_ids * CAP + within).reshape(TILES, CELLS)
    scores = jax.random.randint(second_key, (TILES, CELLS), 0, CELLS) * CELLS + jnp.arange(CELLS, dtype=jnp.int32)[None, :]
    placing = jnp.argsort(scores, axis=1)
    return jnp.take_along_axis(ordered, placing, axis=1).astype(jnp.int32)


def block_scale(own_key, extent, pieces, smallest, high):
    def one(dim, parts):
        draws = jax.random.uniform(jax.random.fold_in(jax.random.fold_in(own_key, 6), dim), (parts,), jnp.float32, smallest / len(pieces), high / len(pieces))
        return jnp.repeat(jnp.exp(draws), extent[dim] // parts).reshape((-1,) + (1,) * (len(extent) - dim - 1))

    loudness = one(*pieces[0])
    for cut in pieces[1:]:
        loudness = loudness * one(*cut)
    return loudness


def bell_draw(own_key, dims, deviation, reach, shards=(), kind=jnp.bfloat16):
    result = jax.random.normal(own_key, dims, jnp.float32) * deviation
    if len(shards) > 0:
        result = block_scale(own_key, dims, shards, -0.22, 0.18) * result
    return jnp.clip(result, min=-reach, max=reach).astype(kind)


def setup_inputs(seed: int = 0) -> dict:
    key_list = jax.random.split(jax.random.key(seed), 8)
    return {
        "tokens": bell_draw(key_list[0], (TOKENS, CHANNELS), 1.0, 6.0, ((0, 8), (1, 4))),
        "cell_source": draw_cell_source(jax.random.fold_in(key_list[7], 71), 0),
        "gain": jnp.clip(0.5 + 1.0 * jax.random.uniform(key_list[2], (CHANNELS,), jnp.float32) ** block_scale(key_list[2], (CHANNELS,), ((0, 4),), -0.2, 0.2), 0.5, 1.5),
        "shift": bell_draw(key_list[3], (CHANNELS,), 0.5, 3.0, ((0, 4),), jnp.float32),
        "weight": bell_draw(key_list[4], (27, CHANNELS, CHANNELS), (27 * CHANNELS) ** -0.5, 0.0546875, ((2, 4),)),
        "bias": bell_draw(key_list[5], (CHANNELS,), 0.5, 3.0, ((0, 4),), jnp.float32),
        "cotangent": bell_draw(key_list[6], (TILES, FRAMES, 2 * TILE_H, 2 * TILE_W, CHANNELS), 1.0, 6.0, ((0, 8), (4, 4))),
    }


def normalize(values, gain, shift):
    group = CHANNELS // GROUPS
    grouped = values.reshape(values.shape[0], values.shape[1], values.shape[2] // group, group)
    center = lax.optimization_barrier(jnp.mean(grouped, axis=(1, 3), keepdims=True))
    centred = grouped - center
    spread = lax.optimization_barrier(jnp.mean(centred * centred, axis=(1, 3), keepdims=True))
    normed = (centred * lax.rsqrt(spread + 1e-06)).reshape(values.shape) * gain + shift
    return jax.nn.silu(normed)

def to_grid(tiled):
    high, wide = (tiled.shape[2], tiled.shape[3])
    shaped = tiled.reshape(TILE_ROWS, TILE_COLS, FRAMES, high, wide, CHANNELS)
    return shaped.transpose(2, 0, 3, 1, 4, 5).reshape(FRAMES, TILE_ROWS * high, TILE_COLS * wide, CHANNELS)

def to_tiles(grid, high, wide):
    shaped = grid.reshape(FRAMES, TILE_ROWS, high, TILE_COLS, wide, CHANNELS)
    return shaped.transpose(1, 3, 0, 2, 4, 5).reshape(TILES, FRAMES, high, wide, CHANNELS)

def reference(tokens, cell_source, gain, shift, weight, bias, cotangent):
    flat_index = cell_source.reshape(-1)
    features = tokens[flat_index].astype(jnp.float32).reshape(TILES, CELLS, CHANNELS)
    activated = normalize(features, gain, shift).astype(jnp.bfloat16)
    grid = to_grid(activated.reshape(TILES, FRAMES, TILE_H, TILE_W, CHANNELS))
    upsampled = jnp.repeat(jnp.repeat(grid, 2, axis=1), 2, axis=2)
    spaced = jnp.pad(upsampled, ((0, 0), (1, 1), (1, 1), (0, 0)))
    time_padded = jnp.concatenate([spaced[:1], spaced[:1], spaced], axis=0).astype(jnp.float32)
    out_h = 2 * TILE_H * TILE_ROWS
    out_w = 2 * TILE_W * TILE_COLS
    summed = jnp.zeros((FRAMES * out_h * out_w, CHANNELS), jnp.float32)
    for offset in range(27):
        time_lag, row_shift, col_shift = (offset // 9, offset // 3 % 3, offset % 3)
        window = time_padded[time_lag:time_lag + FRAMES, row_shift:row_shift + out_h, col_shift:col_shift + out_w]
        summed = summed + jnp.dot(window.reshape(-1, CHANNELS), weight[offset].astype(jnp.float32), preferred_element_type=jnp.float32, precision=lax.Precision.HIGHEST)
    decoded_grid = (summed + bias).astype(jnp.bfloat16).reshape(FRAMES, out_h, out_w, CHANNELS)
    decoded = to_tiles(decoded_grid, 2 * TILE_H, 2 * TILE_W)
    grads = to_grid(cotangent).astype(jnp.float32).reshape(-1, CHANNELS)
    accum = jnp.zeros(time_padded.shape, jnp.float32)
    for offset in range(27):
        time_lag, row_shift, col_shift = (offset // 9, offset // 3 % 3, offset % 3)
        term = jnp.dot(grads, weight[offset].astype(jnp.float32).T, preferred_element_type=jnp.float32, precision=lax.Precision.HIGHEST)
        accum = accum.at[time_lag:time_lag + FRAMES, row_shift:row_shift + out_h, col_shift:col_shift + out_w].add(term.reshape(FRAMES, out_h, out_w, CHANNELS))
    frames_back = accum[2:].at[0].add(accum[0] + accum[1])[:, 1:-1, 1:-1]
    folded = frames_back.reshape(FRAMES, out_h // 2, 2, out_w // 2, 2, CHANNELS).sum(axis=(2, 4))
    adjoint = to_tiles(folded, TILE_H, TILE_W).reshape(TILES, CELLS, CHANNELS)
    unused, pullback = jax.vjp(lambda values: normalize(values, gain, shift), features)
    d_features, = pullback(adjoint)
    token_grad = jnp.zeros((TOKENS, CHANNELS), jnp.float32).at[flat_index].set(d_features.reshape(-1, CHANNELS)).astype(jnp.bfloat16)
    return (decoded, token_grad)
```

```python
import functools

import jax
import jax.numpy as jnp
from jax import lax
from jax.experimental import pallas as pl
from jax.experimental.pallas import tpu as pltpu
from jax.sharding import PartitionSpec as P

CHANNELS = 512
GROUP = 16
FRAMES = 2
TILE_H = 4
TILE_W = 8
CELLS = FRAMES * TILE_H * TILE_W
ROWS = FRAMES * TILE_H
EPS = 1e-06
F32 = jnp.float32
BF16 = jnp.bfloat16
VMEM = pl.BlockSpec(memory_space=pltpu.VMEM)
HIGHEST = lax.Precision.HIGHEST


def call(kernel, outs, args, scratch=(), flops=0):
    moved = sum(a.size * a.dtype.itemsize for a in args)
    moved += sum(o.size * o.dtype.itemsize for o in outs)
    return pl.pallas_call(
        kernel,
        out_shape=outs,
        in_specs=[VMEM] * len(args),
        out_specs=[VMEM] * len(outs),
        scratch_shapes=list(scratch),
        compiler_params=pltpu.CompilerParams(vmem_limit_bytes=48 * 2**20),
        cost_estimate=pl.CostEstimate(flops=flops, bytes_accessed=moved, transcendentals=0),
    )(*args)


def across_tiles():
    return min(lax.axis_size("tile"), 16)


def along_row(block, step):
    count, across = lax.axis_size("tile"), across_tiles()
    route = [(i, i + step) for i in range(count) if 0 <= i % across + step < across]
    return lax.ppermute(block, "tile", route)


def along_column(block, step):
    count, across = lax.axis_size("tile"), across_tiles()
    route = [(i, i + step * across) for i in range(count) if 0 <= i + step * across < count]
    return lax.ppermute(block, "tile", route)


def row_index(shape):
    return lax.broadcasted_iota(jnp.int32, shape, 0)


def from_row_above(x):
    keep = row_index(x.shape) % TILE_H != 0
    return jnp.where(keep, pltpu.roll(x, 1, 0), 0.0)


def from_row_below(x):
    keep = row_index(x.shape) % TILE_H != TILE_H - 1
    return jnp.where(keep, pltpu.roll(x, x.shape[0] - 1, 0), 0.0)


def dgrad_kernel(multi, *refs):
    if multi:
        e_ref, l_ref, r_ref, a_ref, b_ref, w_ref, out_ref, grid, sides = refs
    else:
        e_ref, l_ref, r_ref, w_ref, out_ref, grid, sides = refs
    wide = 2 * TILE_W
    grid[...] = e_ref[...].astype(F32)
    sides[: 2 * ROWS] = l_ref[...].astype(F32)
    sides[2 * ROWS :] = r_ref[...].astype(F32)

    def column(p, x):
        if x < 0:
            return sides[pl.ds(p, ROWS, stride=2), :]
        if x >= wide:
            return sides[pl.ds(2 * ROWS + p, ROWS, stride=2), :]
        return grid[pl.ds(p * wide + x, ROWS, stride=2 * wide), :]

    columns = [[column(p, x) for x in range(-1, wide + 1)] for p in range(2)]

    def fold(parts, e):
        pairs = [parts[2 * s + 2 - e] + parts[2 * s + 3 - e] for s in range(TILE_W)]
        return jnp.concatenate(pairs, axis=0)

    total = jnp.zeros((CELLS, CHANNELS), F32)
    latest = []
    for e in range(3):
        even, odd = fold(columns[0], e), fold(columns[1], e)
        below, above = from_row_below(even), from_row_above(odd)
        if multi:
            low = [b_ref[x].astype(F32) for x in range(wide + 2)]
            high = [a_ref[x].astype(F32) for x in range(wide + 2)]
            below, above = below + fold(low, e), above + fold(high, e)
        for b, folded in enumerate((odd + below, even + odd, above + even)):
            tap = 3 * b + e
            first = row_index(folded.shape) % ROWS < TILE_H
            both = folded + pltpu.roll(folded, CELLS - TILE_H, 0)
            both = jnp.where(first, both, 0.0).astype(BF16)
            latest.append((folded.astype(BF16), tap + 18))
            total = total + contract(both, tap, both, tap + 9, w_ref)
            if len(latest) == 2:
                (x, i), (y, j) = latest
                total = total + contract(x, i, y, j, w_ref)
                latest = []
    for x, i in latest:
        total = total + lax.dot_general(
            x, w_ref[i], (((1,), (1,)), ((), ())), preferred_element_type=F32
        )
    out_ref[...] = total


def contract(x, i, y, j, w_ref):
    left = jnp.concatenate([x, y], axis=1)
    right = jnp.concatenate([w_ref[i], w_ref[j]], axis=1)
    return lax.dot_general(left, right, (((1,), (1,)), ((), ())), preferred_element_type=F32)


def group_mean(sums):
    lanes = sums.shape[1]
    left = lax.broadcasted_iota(jnp.int32, (lanes, lanes), 0) // GROUP
    right = lax.broadcasted_iota(jnp.int32, (lanes, lanes), 1) // GROUP
    same = (left == right).astype(F32)
    whole = jnp.dot(sums, same, preferred_element_type=F32, precision=HIGHEST)
    return whole * (1.0 / (CELLS * GROUP))


def column_sums(x):
    return jnp.sum(x, axis=0, keepdims=True)


def norm_kernel(members, across, swapped, neighbours, peers, *refs):
    pieces = refs[:-12]
    source_ref, gain_ref, shift_ref, partial_ref = refs[-12:-8]
    mine_ref, hat_ref, slope_ref, scale_ref = refs[-8:-4]
    sends, own_ref = refs[-4:-1], refs[-1]
    tile = lax.axis_index("tile")
    chan = lax.axis_index("chan")
    tokens = jnp.concatenate([p[...] for p in pieces], axis=0) if len(pieces) > 1 else pieces[0][...]
    total = tokens.shape[0]
    own = total // members
    lanes = tokens.shape[1]
    source = source_ref[...]
    lane = lax.broadcasted_iota(jnp.int32, source.shape, 1)
    gain, shift = gain_ref[...], shift_ref[...]
    place = lax.broadcasted_iota(jnp.int32, (CELLS, total), 1)
    columns, there = [], []
    for dr, dc in neighbours:
        col, row = tile % across + dc, tile // across + dr
        there.append((col >= 0) & (col < across) & (row >= 0) & (row < members // across))
        wanted = jnp.sum(
            jnp.where(lane == tile + dr * across + dc, source, 0), axis=1, keepdims=True
        )
        if swapped:
            wanted = wanted ^ (tile * own)
        columns.append((place == wanted).astype(BF16))
    chosen = jnp.concatenate(columns, axis=0)
    features = jnp.dot(chosen, tokens, preferred_element_type=F32)
    features = [features[i * CELLS : (i + 1) * CELLS] for i in range(len(neighbours))]
    means = group_mean(stacked([column_sums(f) for f in features]))
    centred = [f - means[i : i + 1] for i, f in enumerate(features)]
    spreads = group_mean(stacked([column_sums(c * c) for c in centred]))
    scales = lax.rsqrt(spreads + EPS)
    blocks = {}
    for i, (dr, dc) in enumerate(neighbours):
        c = centred[i]
        if dc == -1:
            c = c[-ROWS:]
        elif dc == 1:
            c = c[:ROWS]
        hat = c * scales[i : i + 1]
        value = hat * gain + shift
        gate = 1.0 / (1.0 + jnp.exp(-value))
        active = value * gate
        if (dr, dc) == (0, 0):
            hat_ref[...] = hat
            slope_ref[...] = gate * (1.0 + value * (1.0 - gate)) * gain
            scale_ref[...] = scales[i : i + 1]
        else:
            active = jnp.where(there[i], active, 0.0)
        blocks[dr, dc] = active
    parts = [blocks[0, dc] for dc in (-1, 0, 1)]
    if len(neighbours) == 9:
        rows = CELLS + 2 * ROWS
        line = row_index((rows, lanes)) % TILE_H
        for dr, take, keep in ((-1, rows - TILE_H + 1, 0), (1, TILE_H - 1, TILE_H - 1)):
            block = jnp.concatenate([blocks[dr, dc] for dc in (-1, 0, 1)], axis=0)
            parts.append(jnp.where(line == keep, pltpu.roll(block, take, 0), 0.0))
    packed = jnp.concatenate(parts, axis=0).astype(BF16)
    own_ref[...] = packed
    size = packed.shape[0]
    for k, send in enumerate(sends):
        send[:size] = packed
        begin = pl.multiple_of((chan ^ (k + 1)) * lanes, 128)
        send[size:] = partial_ref[:, pl.ds(begin, lanes)].astype(BF16)
    mine_ref[...] = partial_ref[:, pl.ds(pl.multiple_of(chan * lanes, 128), lanes)]


def stacked(rows):
    lanes = rows[0].shape[1]
    pad = -len(rows) % 8
    if pad:
        rows = rows + [jnp.zeros((pad, lanes), F32)]
    return jnp.concatenate(rows, axis=0)


def back_kernel(own, capacity, size, *refs):
    mine_ref, hat_ref, slope_ref, scale_ref, source_ref = refs[:5]
    received, out_ref = refs[5:-1], refs[-1]
    tile = lax.axis_index("tile")
    grad = mine_ref[...]
    for r in received:
        grad = grad + r[size:].astype(F32)
    grad = grad * slope_ref[...]
    hat = hat_ref[...]
    means = group_mean(stacked([column_sums(grad), column_sums(grad * hat)]))
    result = scale_ref[...] * (grad - means[0:1] - hat * means[1:2])
    source = source_ref[pl.ds(tile, 1), :]
    slot = source // own * capacity + source % capacity
    place = row_index((out_ref.shape[0], CELLS))
    chosen = (place == slot).astype(BF16)
    packed = jnp.dot(chosen, result.astype(BF16), preferred_element_type=F32)
    out_ref[...] = packed.astype(BF16)


def conv_kernel(multi, *refs):
    own_ref, r1_ref, r2_ref, r3_ref, w_ref, bias_ref, out_ref, grid = refs
    chan = lax.axis_index("chan")
    rows = CELLS + 2 * ROWS
    lanes = own_ref.shape[1]
    size = own_ref.shape[0]
    grid_in = []
    received = [own_ref[...], r1_ref[:size], r2_ref[:size], r3_ref[:size]]
    for c in range(4):
        piece = received[3]
        for k in range(3):
            piece = jnp.where(chan ^ k == c, received[k], piece)
        grid_in.append(piece)
    cells = jnp.concatenate(grid_in, axis=1).astype(F32)
    line = row_index(cells.shape) % ROWS < TILE_H
    early = jnp.where(line, cells, pltpu.roll(cells, TILE_H, 0)).astype(BF16)
    cells = cells.astype(BF16)

    def products(taps, begin):
        x = cells[begin : begin + rows]
        y = early[begin : begin + rows]
        made = {}
        for at in range(0, len(taps), 2):
            pair = taps[at : at + 2]
            acc = None
            for a, left in ((0, y), (9, y), (18, x)):
                right = jnp.concatenate([w_ref[a + t] for t in pair], axis=1)
                term = jnp.dot(left, right, preferred_element_type=F32)
                acc = term if acc is None else acc + term
            for n, t in enumerate(pair):
                made[t] = acc[:, n * lanes : (n + 1) * lanes]
        return made

    def spread(made, b, q):
        first, middle, last = (made[3 * b + e] for e in range(3))
        if q == 0:
            return first[:CELLS] + middle[ROWS:-ROWS] + last[ROWS:-ROWS]
        return first[ROWS:-ROWS] + middle[ROWS:-ROWS] + last[2 * ROWS :]

    made = products(list(range(9)), 0)
    if multi:
        made_above = products([0, 1, 2], rows)
        made_below = products([6, 7, 8], 2 * rows)
    wide = 2 * TILE_W
    for q in range(2):
        top, middle, bottom = (spread(made, b, q) for b in range(3))
        above, below = from_row_above(top), from_row_below(bottom)
        if multi:
            above = above + spread(made_above, 0, q)
            below = below + spread(made_below, 2, q)
        for p, value in enumerate((above + middle + bottom, top + middle + below)):
            value = value + bias_ref[...]
            for j in range(TILE_W):
                grid[pl.ds(p * wide + 2 * j + q, ROWS, stride=2 * wide), :] = value[
                    j * ROWS : (j + 1) * ROWS
                ]
    out_ref[...] = grid[...].astype(BF16)


def place_kernel(returned_ref, slots_ref, out_ref):
    place = row_index((out_ref.shape[0], slots_ref.shape[1]))
    chosen = (place == slots_ref[...]).astype(BF16)
    out_ref[...] = jnp.dot(chosen, returned_ref[...], preferred_element_type=F32).astype(BF16)


def gathered_tokens(tokens):
    members = lax.axis_size("tile")
    if members != 8:
        return [lax.all_gather(tokens, "tile", axis=0, tiled=True)], False

    def swap(block, k):
        return lax.ppermute(block, "tile", [(i, i ^ k) for i in range(members)])

    pair = jnp.concatenate([tokens, swap(tokens, 1)], axis=0)
    return [pair] + [swap(pair, k) for k in (2, 4, 6)], True


def local(tokens, cell_source, gain, shift, weight, bias, cotangent):
    members = lax.axis_size("tile")
    device = lax.axis_index("tile")
    peers = lax.axis_size("chan")
    own, lanes = tokens.shape
    across = across_tiles()
    multi = members > across
    capacity = max(2, own // (members // 2))
    high, wide = 2 * TILE_H, 2 * TILE_W
    shape = jax.ShapeDtypeStruct

    grads = cotangent.reshape(FRAMES, high, wide, lanes)
    from_left = along_row(grads[:, :, -1:], 1)
    from_right = along_row(grads[:, :, :1], -1)
    pieces, swapped = gathered_tokens(tokens)
    args = [
        grads.reshape(-1, lanes),
        from_left.reshape(-1, lanes),
        from_right.reshape(-1, lanes),
    ]
    if multi:
        widened = jnp.concatenate([from_left, grads, from_right], axis=2)
        for edge, step, line in ((widened[:, -1], 1, 0), (widened[:, 0], -1, TILE_H - 1)):
            rim = along_column(edge, step).transpose(1, 0, 2)
            spaced = jnp.zeros((wide + 2, FRAMES, TILE_H, lanes), BF16).at[:, :, line].set(rim)
            args.append(spaced.reshape(wide + 2, ROWS, lanes))
    (partial,) = call(
        functools.partial(dgrad_kernel, multi),
        [shape((CELLS, CHANNELS), F32)],
        args + [weight],
        [pltpu.VMEM((high * wide * FRAMES, lanes), F32), pltpu.VMEM((4 * ROWS, lanes), F32)],
        flops=2 * 27 * CELLS * lanes * CHANNELS,
    )

    by_cell = cell_source.reshape(members, FRAMES, TILE_H, TILE_W).transpose(0, 3, 1, 2)
    by_cell = by_cell.reshape(members, CELLS)
    neighbours = [(0, -1), (0, 0), (0, 1)]
    if multi:
        neighbours = [(r, c) for r in (-1, 0, 1) for c in (-1, 0, 1)]
    size = (CELLS + 2 * ROWS) * (3 if multi else 1)
    cell = shape((CELLS, lanes), F32)
    mine, hat, slope, scale, *sends, packed = call(
        functools.partial(norm_kernel, members, across, swapped, neighbours, peers),
        [cell, cell, cell, shape((1, lanes), F32)]
        + [shape((size + CELLS, lanes), BF16)] * 3
        + [shape((size, lanes), BF16)],
        pieces + [by_cell.T, gain.reshape(1, -1), shift.reshape(1, -1), partial],
        flops=2 * len(neighbours) * CELLS * members * own * lanes,
    )
    received = [
        lax.ppermute(block, "chan", [(i, i ^ (k + 1)) for i in range(peers)])
        for k, block in enumerate(sends)
    ]
    (returning,) = call(
        functools.partial(back_kernel, own, capacity, size),
        [shape((members * capacity, lanes), BF16)],
        [mine, hat, slope, scale, by_cell] + received,
    )
    returned = lax.all_to_all(returning, "tile", split_axis=0, concat_axis=0, tiled=True)
    (decoded,) = call(
        functools.partial(conv_kernel, multi),
        [shape((FRAMES * high * wide, lanes), BF16)],
        [packed] + received + [weight, bias.reshape(1, -1)],
        [pltpu.VMEM((FRAMES * high * wide, lanes), F32)],
        flops=2 * 27 * (CELLS + 2 * ROWS) * lanes * CHANNELS,
    )
    mine_here = cell_source // own == device
    first = jnp.max(jnp.where(mine_here, cell_source % own, -capacity), axis=1) // capacity
    slots = first[:, None] * capacity + jnp.arange(capacity, dtype=jnp.int32)[None, :]
    (token_grad,) = call(
        place_kernel, [shape((own, lanes), BF16)], [returned, slots.reshape(1, -1)]
    )
    return decoded.reshape(1, FRAMES, high, wide, lanes), token_grad


def solution(mesh):
    in_specs = (
        P("tile", "chan"),
        P(),
        P("chan"),
        P("chan"),
        P(None, None, "chan"),
        P("chan"),
        P("tile", None, None, None, "chan"),
    )
    out_specs = (P("tile", None, None, None, "chan"), P("tile", "chan"))
    return jax.shard_map(local, mesh=mesh, in_specs=in_specs, out_specs=out_specs, check_vma=False)
```

```python
import functools

import jax
import jax.numpy as jnp
from jax import lax
from jax.experimental import pallas as pl
from jax.experimental.pallas import tpu as pltpu
from jax.sharding import PartitionSpec as P

CHANNELS = 512
GROUP = 16
FRAMES = 2
TILE_H = 4
TILE_W = 8
CELLS = FRAMES * TILE_H * TILE_W
ROWS = FRAMES * TILE_H
EPS = 1e-06
VMEM_LIMIT = 12 * 2**20
F32 = jnp.float32
BF16 = jnp.bfloat16
VMEM = pl.BlockSpec(memory_space=pltpu.VMEM)
ANY = pl.BlockSpec(memory_space=pl.ANY)
HIGHEST = lax.Precision.HIGHEST


def call(kernel, outs, args, scratch=(), flops=0, loose=()):
    moved = sum(a.size * a.dtype.itemsize for a in args)
    moved += sum(o.size * o.dtype.itemsize for o in outs)
    return pl.pallas_call(
        kernel,
        out_shape=outs,
        in_specs=[ANY if i in loose else VMEM for i in range(len(args))],
        out_specs=[VMEM] * len(outs),
        scratch_shapes=list(scratch),
        compiler_params=pltpu.CompilerParams(vmem_limit_bytes=VMEM_LIMIT),
        cost_estimate=pl.CostEstimate(flops=flops, bytes_accessed=moved, transcendentals=0),
    )(*args)


def across_tiles():
    return min(lax.axis_size("tile"), 16)


def along_row(block, step):
    count, across = lax.axis_size("tile"), across_tiles()
    route = [(i, i + step) for i in range(count) if 0 <= i % across + step < across]
    return lax.ppermute(block, "tile", route)


def along_column(block, step):
    count, across = lax.axis_size("tile"), across_tiles()
    route = [(i, i + step * across) for i in range(count) if 0 <= i + step * across < count]
    return lax.ppermute(block, "tile", route)


def row_index(shape):
    return lax.broadcasted_iota(jnp.int32, shape, 0)


def from_row_above(x):
    keep = row_index(x.shape) % TILE_H != 0
    return jnp.where(keep, pltpu.roll(x, 1, 0), 0.0)


def from_row_below(x):
    keep = row_index(x.shape) % TILE_H != TILE_H - 1
    return jnp.where(keep, pltpu.roll(x, x.shape[0] - 1, 0), 0.0)


def dgrad(lines, left, right, rims, w_ref, grid, sides):
    multi = len(rims) > 0
    wide = 2 * TILE_W
    grid[...] = lines.astype(F32)
    sides[: 2 * ROWS] = left.astype(F32)
    sides[2 * ROWS :] = right.astype(F32)

    def column(p, x):
        if x < 0:
            return sides[pl.ds(p, ROWS, stride=2), :]
        if x >= wide:
            return sides[pl.ds(2 * ROWS + p, ROWS, stride=2), :]
        return grid[pl.ds(p * wide + x, ROWS, stride=2 * wide), :]

    columns = [[column(p, x) for x in range(-1, wide + 1)] for p in range(2)]

    def fold(parts, e):
        pairs = [parts[2 * s + 2 - e] + parts[2 * s + 3 - e] for s in range(TILE_W)]
        return jnp.concatenate(pairs, axis=0)

    total = jnp.zeros((CELLS, CHANNELS), F32)
    latest = []
    for e in range(3):
        even, odd = fold(columns[0], e), fold(columns[1], e)
        below, above = from_row_below(even), from_row_above(odd)
        if multi:
            high = [rims[0][x].astype(F32) for x in range(wide + 2)]
            low = [rims[1][x].astype(F32) for x in range(wide + 2)]
            below, above = below + fold(low, e), above + fold(high, e)
        for b, folded in enumerate((odd + below, even + odd, above + even)):
            tap = 3 * b + e
            first = row_index(folded.shape) % ROWS < TILE_H
            both = folded + pltpu.roll(folded, CELLS - TILE_H, 0)
            both = jnp.where(first, both, 0.0).astype(BF16)
            latest.append((folded.astype(BF16), tap + 18))
            total = total + contract(both, tap, both, tap + 9, w_ref)
            if len(latest) == 2:
                (x, i), (y, j) = latest
                total = total + contract(x, i, y, j, w_ref)
                latest = []
    for x, i in latest:
        total = total + lax.dot_general(
            x, w_ref[i], (((1,), (1,)), ((), ())), preferred_element_type=F32
        )
    return total


def contract(x, i, y, j, w_ref):
    left = jnp.concatenate([x, y], axis=1)
    right = jnp.concatenate([w_ref[i], w_ref[j]], axis=1)
    return lax.dot_general(left, right, (((1,), (1,)), ((), ())), preferred_element_type=F32)


def group_mean(sums):
    lanes = sums.shape[1]
    left = lax.broadcasted_iota(jnp.int32, (lanes, lanes), 0) // GROUP
    right = lax.broadcasted_iota(jnp.int32, (lanes, lanes), 1) // GROUP
    same = (left == right).astype(F32)
    whole = jnp.dot(sums, same, preferred_element_type=F32, precision=HIGHEST)
    return whole * (1.0 / (CELLS * GROUP))


def column_sums(x):
    return jnp.sum(x, axis=0, keepdims=True)


def main_kernel(members, across, woven, neighbours, count, *refs):
    pieces, refs = refs[:count], refs[count:]
    lines_ref, w_ref, take_ref, gain_ref, shift_ref = refs[:5]
    others, refs = refs[5:-11], refs[-11:]
    mine_ref, hat_ref, slope_ref, scale_ref = refs[:4]
    sends, own_ref = refs[4:7], refs[7]
    partial_ref, grid, sides = refs[8:11]
    tile = lax.axis_index("tile")
    chan = lax.axis_index("chan")
    if woven:
        near = others[0][: 2 * ROWS]
        far = jnp.zeros_like(near)
        column = tile % 2
        wanted = tile // 2 + 2 * column - 1
        for k in range(1, count):
            far = jnp.where(wanted == tile // 2 ^ k, pieces[k][-2 * ROWS :], far)
        left = jnp.where(column == 1, near, far)
        right = jnp.where(column == 1, far, near)
        tokens = jnp.concatenate([p[: -2 * ROWS] for p in pieces], axis=0)
        rims = ()
    else:
        left, right = others[0][...], others[1][...]
        tokens = pieces[0][...]
        rims = others[2:]
    partial_ref[...] = dgrad(lines_ref[...], left, right, rims, w_ref, grid, sides)
    lanes = tokens.shape[1]
    gain, shift = gain_ref[...], shift_ref[...]
    there = []
    for dr, dc in neighbours:
        col, row = tile % across + dc, tile // across + dr
        there.append((col >= 0) & (col < across) & (row >= 0) & (row < members // across))
    chosen = take_ref[...]
    features = jnp.dot(chosen, tokens, preferred_element_type=F32)
    features = [features[i * CELLS : (i + 1) * CELLS] for i in range(len(neighbours))]
    means = group_mean(stacked([column_sums(f) for f in features]))
    centred = [f - means[i : i + 1] for i, f in enumerate(features)]
    spreads = group_mean(stacked([column_sums(c * c) for c in centred]))
    scales = lax.rsqrt(spreads + EPS)
    blocks = {}
    for i, (dr, dc) in enumerate(neighbours):
        c = centred[i]
        if dc == -1:
            c = c[-ROWS:]
        elif dc == 1:
            c = c[:ROWS]
        hat = c * scales[i : i + 1]
        value = hat * gain + shift
        gate = 1.0 / (1.0 + jnp.exp(-value))
        active = value * gate
        if (dr, dc) == (0, 0):
            hat_ref[...] = hat
            slope_ref[...] = gate * (1.0 + value * (1.0 - gate)) * gain
            scale_ref[...] = scales[i : i + 1]
        else:
            active = jnp.where(there[i], active, 0.0)
        blocks[dr, dc] = active
    parts = [blocks[0, dc] for dc in (-1, 0, 1)]
    if len(neighbours) == 9:
        rows = CELLS + 2 * ROWS
        line = row_index((rows, lanes)) % TILE_H
        for dr, take, keep in ((-1, rows - TILE_H + 1, 0), (1, TILE_H - 1, TILE_H - 1)):
            block = jnp.concatenate([blocks[dr, dc] for dc in (-1, 0, 1)], axis=0)
            parts.append(jnp.where(line == keep, pltpu.roll(block, take, 0), 0.0))
    packed = jnp.concatenate(parts, axis=0).astype(BF16)
    own_ref[...] = packed
    size = packed.shape[0]
    for k, send in enumerate(sends):
        send[:size] = packed
        begin = pl.multiple_of((chan ^ (k + 1)) * lanes, 128)
        send[size:] = partial_ref[:, pl.ds(begin, lanes)].astype(BF16)
    mine_ref[...] = partial_ref[:, pl.ds(pl.multiple_of(chan * lanes, 128), lanes)]


def stacked(rows):
    lanes = rows[0].shape[1]
    pad = -len(rows) % 8
    if pad:
        rows = rows + [jnp.zeros((pad, lanes), F32)]
    return jnp.concatenate(rows, axis=0)


def fetch(copies):
    for copy in copies:
        copy.start()
    for copy in copies:
        copy.wait()


def back_kernel(size, *refs):
    mine_ref, hat_ref, slope_ref, scale_ref, pack_ref = refs[:5]
    received, outs = refs[5:8], refs[8:-2]
    space, sems = refs[-2:]
    copies = [
        pltpu.make_async_copy(r.at[pl.ds(size, CELLS)], space.at[k], sems.at[k])
        for k, r in enumerate(received)
    ]
    fetch(copies)
    grad = mine_ref[...]
    for k in range(3):
        grad = grad + space[k].astype(F32)
    grad = grad * slope_ref[...]
    hat = hat_ref[...]
    means = group_mean(stacked([column_sums(grad), column_sums(grad * hat)]))
    result = scale_ref[...] * (grad - means[0:1] - hat * means[1:2])
    packed = jnp.dot(pack_ref[...], result.astype(BF16), preferred_element_type=F32).astype(BF16)
    begin = 0
    for out in outs:
        out[...] = packed[begin : begin + out.shape[0]]
        begin += out.shape[0]


def route_kernel(kept_ref, came_ref, *outs):
    some = outs[0].shape[0] // 2
    for k, out in enumerate(outs):
        out[:some] = kept_ref[k * some : (k + 1) * some]
        out[some:] = came_ref[k * some : (k + 1) * some]


def join_kernel(tokens_ref, peer_ref, edges_ref, out_ref):
    own = tokens_ref.shape[0]
    out_ref[:own] = tokens_ref[...]
    out_ref[own : 2 * own] = peer_ref[...]
    out_ref[2 * own :] = edges_ref[2 * ROWS :]


def edge_kernel(lines_ref, out_ref, grid):
    wide = 2 * TILE_W
    grid[...] = lines_ref[...].astype(F32)
    first = grid[pl.ds(0, 2 * ROWS, stride=wide), :]
    last = grid[pl.ds(wide - 1, 2 * ROWS, stride=wide), :]
    odd = lax.axis_index("tile") % 2 == 1
    out_ref[: 2 * ROWS] = jnp.where(odd, first, last).astype(BF16)
    out_ref[2 * ROWS :] = jnp.where(odd, last, first).astype(BF16)


def conv_kernel(multi, *refs):
    own_ref, *received, hbm_ref, bias_ref, out_ref, grid, space, w_ref, sems = refs
    chan = lax.axis_index("chan")
    rows = CELLS + 2 * ROWS
    lanes = own_ref.shape[1]
    size = own_ref.shape[0]
    copies = [
        pltpu.make_async_copy(r.at[pl.ds(0, size)], space.at[k], sems.at[k])
        for k, r in enumerate(received)
    ]
    copies.append(pltpu.make_async_copy(hbm_ref, w_ref, sems.at[3]))
    fetch(copies)
    grid_in = []
    received = [own_ref[...], space[0], space[1], space[2]]
    for c in range(4):
        piece = received[3]
        for k in range(3):
            piece = jnp.where(chan ^ k == c, received[k], piece)
        grid_in.append(piece)
    cells = jnp.concatenate(grid_in, axis=1).astype(F32)
    line = row_index(cells.shape) % ROWS < TILE_H
    early = jnp.where(line, cells, pltpu.roll(cells, TILE_H, 0)).astype(BF16)
    cells = cells.astype(BF16)

    def products(taps, begin):
        x = cells[begin : begin + rows]
        y = early[begin : begin + rows]
        made = {}
        for at in range(0, len(taps), 2):
            pair = taps[at : at + 2]
            acc = None
            for a, left in ((0, y), (9, y), (18, x)):
                right = jnp.concatenate([w_ref[a + t] for t in pair], axis=1)
                term = jnp.dot(left, right, preferred_element_type=F32)
                acc = term if acc is None else acc + term
            for n, t in enumerate(pair):
                made[t] = acc[:, n * lanes : (n + 1) * lanes]
        return made

    def spread(made, b, q):
        first, middle, last = (made[3 * b + e] for e in range(3))
        if q == 0:
            return first[:CELLS] + middle[ROWS:-ROWS] + last[ROWS:-ROWS]
        return first[ROWS:-ROWS] + middle[ROWS:-ROWS] + last[2 * ROWS :]

    made = products(list(range(9)), 0)
    if multi:
        made_above = products([0, 1, 2], rows)
        made_below = products([6, 7, 8], 2 * rows)
    wide = 2 * TILE_W
    for q in range(2):
        top, middle, bottom = (spread(made, b, q) for b in range(3))
        above, below = from_row_above(top), from_row_below(bottom)
        if multi:
            above = above + spread(made_above, 0, q)
            below = below + spread(made_below, 2, q)
        for p, value in enumerate((above + middle + bottom, top + middle + below)):
            value = value + bias_ref[...]
            for j in range(TILE_W):
                grid[pl.ds(p * wide + 2 * j + q, ROWS, stride=2 * wide), :] = value[
                    j * ROWS : (j + 1) * ROWS
                ]
    out_ref[...] = grid[...].astype(BF16)


def place_kernel(put_ref, *refs):
    returned, out_ref = refs[:-1], refs[-1]
    values = [r[...] for r in returned]
    values = jnp.concatenate(values, axis=0) if len(values) > 1 else values[0]
    placed = jnp.dot(put_ref[...], values, preferred_element_type=F32)
    out_ref[...] = placed.astype(BF16)


def cell_of(place):
    return place % ROWS // TILE_H * (TILE_H * TILE_W) + place % TILE_H * TILE_W + place // ROWS


def index_kernel(across, woven, neighbours, own, capacity, source_ref, take_ref, pack_ref, put_ref):
    tile = lax.axis_index("tile")
    source = source_ref[...]
    members = source.shape[0]
    square = (CELLS, CELLS)
    left = lax.broadcasted_iota(jnp.int32, square, 0)
    right = lax.broadcasted_iota(jnp.int32, square, 1)
    place = lax.broadcasted_iota(jnp.int32, (CELLS, members * own), 1)
    for i, (dr, dc) in enumerate(neighbours):
        other = jnp.clip(tile + dr * across + dc, 0, members - 1)
        line = source_ref[pl.ds(other, 1), :]
        wanted = jnp.sum(jnp.where(cell_of(left) == right, line, 0), axis=1, keepdims=True)
        if (dr, dc) == (0, 0):
            owner = wanted // own
            if woven:
                owner = owner ^ tile
                owner = owner // 2 + owner % 2 * (members // 2)
            slot = owner * capacity + wanted % capacity
            slot = jnp.sum(jnp.where(left == right, slot, 0), axis=0, keepdims=True)
        if woven:
            wanted = wanted ^ (tile * own)
        take_ref[i * CELLS : (i + 1) * CELLS] = (place == wanted).astype(F32).astype(BF16)
    pack_ref[...] = (row_index(pack_ref.shape) == slot).astype(F32).astype(BF16)
    mine = source // own == tile
    first = jnp.where(mine, source % own, -capacity)
    first = jnp.max(first, axis=1, keepdims=True) // capacity * capacity
    wide = (members, members * capacity)
    spot = lax.broadcasted_iota(jnp.int32, wide, 1)
    sender = spot // capacity
    if woven:
        sender = sender ^ tile
    meant = jnp.where(sender == row_index(wide), first + spot % capacity, 0)
    meant = jnp.sum(meant, axis=0, keepdims=True)
    put_ref[...] = (row_index(put_ref.shape) == meant).astype(F32).astype(BF16)


def swapped(block, axis, k):
    return lax.ppermute(block, axis, [(i, i ^ k) for i in range(lax.axis_size(axis))])


def local(tokens, cell_source, gain, shift, weight, bias, cotangent):
    members = lax.axis_size("tile")
    own, lanes = tokens.shape
    across = across_tiles()
    multi = members > across
    woven = members == 8
    capacity = max(2, own // (members // 2))
    slots = members * capacity
    high, wide = 2 * TILE_H, 2 * TILE_W
    area = FRAMES * high * wide
    shape = jax.ShapeDtypeStruct

    def block(rows):
        return shape((rows, lanes), BF16)

    neighbours = [(0, -1), (0, 0), (0, 1)]
    if multi:
        neighbours = [(r, c) for r in (-1, 0, 1) for c in (-1, 0, 1)]
    take, pack, put = call(
        functools.partial(index_kernel, across, woven, neighbours, own, capacity),
        [
            shape((len(neighbours) * CELLS, members * own), BF16),
            shape((slots, CELLS), BF16),
            shape((own, slots), BF16),
        ],
        [cell_source],
    )
    lines = cotangent.reshape(area, lanes)
    spread = pltpu.VMEM((area, lanes), F32)
    if woven:
        peer = swapped(tokens, "tile", 1)
        (edges,) = call(edge_kernel, [block(4 * ROWS)], [lines], [spread])
        edges = swapped(edges, "tile", 1)
        (pair,) = call(join_kernel, [block(2 * own + 2 * ROWS)], [tokens, peer, edges])
        pieces = [pair] + [swapped(pair, "tile", k) for k in (2, 4, 6)]
        others = [edges]
    else:
        pieces = [lax.all_gather(tokens, "tile", axis=0, tiled=True)]
        others = [along_row(lines[wide - 1 :: wide], 1), along_row(lines[::wide], -1)]
    if multi:
        side = (FRAMES, high, 1, lanes)
        widened = [others[0].reshape(side), lines.reshape(FRAMES, high, wide, lanes)]
        widened = jnp.concatenate(widened + [others[1].reshape(side)], axis=2)
        for edge, step, line in ((widened[:, -1], 1, 0), (widened[:, 0], -1, TILE_H - 1)):
            rim = along_column(edge, step).transpose(1, 0, 2)
            spaced = jnp.zeros((wide + 2, FRAMES, TILE_H, lanes), BF16).at[:, :, line].set(rim)
            others.append(spaced.reshape(wide + 2, ROWS, lanes))

    size = (CELLS + 2 * ROWS) * (3 if multi else 1)
    cell = shape((CELLS, lanes), F32)
    mine, hat, slope, scale, *sends, packed = call(
        functools.partial(main_kernel, members, across, woven, neighbours, len(pieces)),
        [cell, cell, cell, shape((1, lanes), F32)] + [block(size + CELLS)] * 3 + [block(size)],
        pieces + [lines, weight, take, gain.reshape(1, -1), shift.reshape(1, -1)] + others,
        [pltpu.VMEM((CELLS, CHANNELS), F32), spread, pltpu.VMEM((4 * ROWS, lanes), F32)],
        flops=2 * 27 * CELLS * lanes * CHANNELS,
    )
    received = [swapped(send, "chan", k + 1) for k, send in enumerate(sends)]
    halves = [block(slots // 2)] * 2 if woven else [block(slots)]
    returning = call(
        functools.partial(back_kernel, size),
        halves,
        [mine, hat, slope, scale, pack] + received,
        [pltpu.VMEM((3, CELLS, lanes), BF16), pltpu.SemaphoreType.DMA((3,))],
        loose=(5, 6, 7),
    )
    if woven:
        came = swapped(returning[1], "tile", 1)
        routed = call(route_kernel, [block(2 * capacity)] * 4, [returning[0], came])
        returned = [routed[0]] + [swapped(r, "tile", 2 * k + 2) for k, r in enumerate(routed[1:])]
    else:
        returned = [lax.all_to_all(returning[0], "tile", split_axis=0, concat_axis=0, tiled=True)]
    (decoded,) = call(
        functools.partial(conv_kernel, multi),
        [block(area)],
        [packed] + received + [weight, bias.reshape(1, -1)],
        [
            spread,
            pltpu.VMEM((3, size, lanes), BF16),
            pltpu.VMEM(weight.shape, BF16),
            pltpu.SemaphoreType.DMA((4,)),
        ],
        flops=2 * 27 * (CELLS + 2 * ROWS) * lanes * CHANNELS,
        loose=(1, 2, 3, 4),
    )
    (token_grad,) = call(place_kernel, [block(own)], [put] + returned)
    return decoded.reshape(1, FRAMES, high, wide, lanes), token_grad


def solution(mesh):
    in_specs = (
        P("tile", "chan"),
        P(),
        P("chan"),
        P("chan"),
        P(None, None, "chan"),
        P("chan"),
        P("tile", None, None, None, "chan"),
    )
    out_specs = (P("tile", None, None, None, "chan"), P("tile", "chan"))
    return jax.shard_map(local, mesh=mesh, in_specs=in_specs, out_specs=out_specs, check_vma=False)
```

```python
import functools

import jax
import jax.numpy as jnp
from jax import lax
from jax.experimental import pallas as pl
from jax.experimental.pallas import tpu as pltpu
from jax.sharding import PartitionSpec as P

CHANNELS = 512
GROUP = 16
FRAMES = 2
TILE_H = 4
TILE_W = 8
CELLS = FRAMES * TILE_H * TILE_W
ROWS = FRAMES * TILE_H
EPS = 1e-06
VMEM_LIMIT = 12 * 2**20
F32 = jnp.float32
BF16 = jnp.bfloat16
VMEM = pl.BlockSpec(memory_space=pltpu.VMEM)
FAR = pl.BlockSpec(memory_space=pltpu.HBM)
HIGHEST = lax.Precision.HIGHEST


def call(kernel, outs, args, scratch=(), flops=0, loose=()):
    args = [
        pltpu.with_memory_space_constraint(a, pltpu.HBM) if i in loose else a
        for i, a in enumerate(args)
    ]
    moved = sum(a.size * a.dtype.itemsize for a in args)
    moved += sum(o.size * o.dtype.itemsize for o in outs)
    return pl.pallas_call(
        kernel,
        out_shape=outs,
        in_specs=[FAR if i in loose else VMEM for i in range(len(args))],
        out_specs=[VMEM] * len(outs),
        scratch_shapes=list(scratch),
        compiler_params=pltpu.CompilerParams(vmem_limit_bytes=VMEM_LIMIT),
        cost_estimate=pl.CostEstimate(flops=flops, bytes_accessed=moved, transcendentals=0),
    )(*args)


def across_tiles():
    return min(lax.axis_size("tile"), 16)


def along_row(block, step):
    count, across = lax.axis_size("tile"), across_tiles()
    route = [(i, i + step) for i in range(count) if 0 <= i % across + step < across]
    return lax.ppermute(block, "tile", route)


def along_column(block, step):
    count, across = lax.axis_size("tile"), across_tiles()
    route = [(i, i + step * across) for i in range(count) if 0 <= i + step * across < count]
    return lax.ppermute(block, "tile", route)


def row_index(shape):
    return lax.broadcasted_iota(jnp.int32, shape, 0)


def from_row_above(x):
    keep = row_index(x.shape) % TILE_H != 0
    return jnp.where(keep, pltpu.roll(x, 1, 0), 0.0)


def from_row_below(x):
    keep = row_index(x.shape) % TILE_H != TILE_H - 1
    return jnp.where(keep, pltpu.roll(x, x.shape[0] - 1, 0), 0.0)


def dgrad(grid, left, right, rims, w_ref, sides):
    multi = len(rims) > 0
    wide = 2 * TILE_W
    sides[: 2 * ROWS] = left.astype(F32)
    sides[2 * ROWS :] = right.astype(F32)

    def column(p, x):
        if x < 0:
            return sides[pl.ds(p, ROWS, stride=2), :]
        if x >= wide:
            return sides[pl.ds(2 * ROWS + p, ROWS, stride=2), :]
        return grid[pl.ds(p * wide + x, ROWS, stride=2 * wide), :]

    columns = [[column(p, x) for x in range(-1, wide + 1)] for p in range(2)]

    def fold(parts, e):
        pairs = [parts[2 * s + 2 - e] + parts[2 * s + 3 - e] for s in range(TILE_W)]
        return jnp.concatenate(pairs, axis=0)

    total = jnp.zeros((CELLS, CHANNELS), F32)
    latest = []
    for e in range(3):
        even, odd = fold(columns[0], e), fold(columns[1], e)
        below, above = from_row_below(even), from_row_above(odd)
        if multi:
            high = [rims[0][x].astype(F32) for x in range(wide + 2)]
            low = [rims[1][x].astype(F32) for x in range(wide + 2)]
            below, above = below + fold(low, e), above + fold(high, e)
        for b, folded in enumerate((odd + below, even + odd, above + even)):
            tap = 3 * b + e
            first = row_index(folded.shape) % ROWS < TILE_H
            both = folded + pltpu.roll(folded, CELLS - TILE_H, 0)
            both = jnp.where(first, both, 0.0).astype(BF16)
            latest.append((folded.astype(BF16), tap + 18))
            total = total + contract(both, tap, both, tap + 9, w_ref)
            if len(latest) == 2:
                (x, i), (y, j) = latest
                total = total + contract(x, i, y, j, w_ref)
                latest = []
    for x, i in latest:
        total = total + lax.dot_general(
            x, w_ref[i], (((1,), (1,)), ((), ())), preferred_element_type=F32
        )
    return total


def contract(x, i, y, j, w_ref):
    left = jnp.concatenate([x, y], axis=1)
    right = jnp.concatenate([w_ref[i], w_ref[j]], axis=1)
    return lax.dot_general(left, right, (((1,), (1,)), ((), ())), preferred_element_type=F32)


def group_mean(sums):
    lanes = sums.shape[1]
    left = lax.broadcasted_iota(jnp.int32, (lanes, lanes), 0) // GROUP
    right = lax.broadcasted_iota(jnp.int32, (lanes, lanes), 1) // GROUP
    same = (left == right).astype(F32)
    whole = jnp.dot(sums, same, preferred_element_type=F32, precision=HIGHEST)
    return whole * (1.0 / (CELLS * GROUP))


def column_sums(x):
    return jnp.sum(x, axis=0, keepdims=True)


def main_kernel(members, across, woven, neighbours, count, *refs):
    pieces, refs = refs[:count], refs[count:]
    lines_ref, w_ref, take_ref, gain_ref, shift_ref = refs[:5]
    others, refs = refs[5:-10], refs[-10:]
    mine_ref, hat_ref, slope_ref, scale_ref = refs[:4]
    sends, own_ref = refs[4:7], refs[7]
    partial_ref, sides = refs[8:10]
    tile = lax.axis_index("tile")
    chan = lax.axis_index("chan")
    if woven:
        near = others[0][-4 * ROWS : -2 * ROWS]
        far = jnp.zeros_like(near)
        column = tile % 2
        wanted = tile // 2 + 2 * column - 1
        for k in range(1, count):
            far = jnp.where(wanted == tile // 2 ^ k, pieces[k][-2 * ROWS :], far)
        left = jnp.where(column == 1, near, far)
        right = jnp.where(column == 1, far, near)
        tokens = jnp.concatenate([p[: -2 * ROWS] for p in pieces], axis=0)
        rims = ()
    else:
        left, right = others[0][...], others[1][...]
        tokens = pieces[0][...]
        rims = others[2:]
    partial_ref[...] = dgrad(lines_ref, left, right, rims, w_ref, sides)
    lanes = tokens.shape[1]
    gain, shift = gain_ref[...], shift_ref[...]
    there = []
    for dr, dc in neighbours:
        col, row = tile % across + dc, tile // across + dr
        there.append((col >= 0) & (col < across) & (row >= 0) & (row < members // across))
    chosen = take_ref[...]
    features = jnp.dot(chosen, tokens, preferred_element_type=F32)
    features = [features[i * CELLS : (i + 1) * CELLS] for i in range(len(neighbours))]
    means = group_mean(stacked([column_sums(f) for f in features]))
    centred = [f - means[i : i + 1] for i, f in enumerate(features)]
    spreads = group_mean(stacked([column_sums(c * c) for c in centred]))
    scales = lax.rsqrt(spreads + EPS)
    blocks = {}
    for i, (dr, dc) in enumerate(neighbours):
        c = centred[i]
        if dc == -1:
            c = c[-ROWS:]
        elif dc == 1:
            c = c[:ROWS]
        hat = c * scales[i : i + 1]
        value = hat * gain + shift
        gate = 1.0 / (1.0 + jnp.exp(-value))
        active = value * gate
        if (dr, dc) == (0, 0):
            hat_ref[...] = hat
            slope_ref[...] = gate * (1.0 + value * (1.0 - gate)) * gain
            scale_ref[...] = scales[i : i + 1]
        else:
            active = jnp.where(there[i], active, 0.0)
        blocks[dr, dc] = active
    parts = [blocks[0, dc] for dc in (-1, 0, 1)]
    if len(neighbours) == 9:
        rows = CELLS + 2 * ROWS
        line = row_index((rows, lanes)) % TILE_H
        for dr, take, keep in ((-1, rows - TILE_H + 1, 0), (1, TILE_H - 1, TILE_H - 1)):
            block = jnp.concatenate([blocks[dr, dc] for dc in (-1, 0, 1)], axis=0)
            parts.append(jnp.where(line == keep, pltpu.roll(block, take, 0), 0.0))
    packed = jnp.concatenate(parts, axis=0).astype(BF16)
    own_ref[...] = packed
    size = packed.shape[0]
    for k, send in enumerate(sends):
        send[:size] = packed
        begin = pl.multiple_of((chan ^ (k + 1)) * lanes, 128)
        send[size:] = partial_ref[:, pl.ds(begin, lanes)].astype(BF16)
    mine_ref[...] = partial_ref[:, pl.ds(pl.multiple_of(chan * lanes, 128), lanes)]


def stacked(rows):
    lanes = rows[0].shape[1]
    pad = -len(rows) % 8
    if pad:
        rows = rows + [jnp.zeros((pad, lanes), F32)]
    return jnp.concatenate(rows, axis=0)


def fetch(copies):
    for copy in copies:
        copy.start()
    for copy in copies:
        copy.wait()


def back_kernel(size, *refs):
    mine_ref, hat_ref, slope_ref, scale_ref, pack_ref = refs[:5]
    received, outs = refs[5:8], refs[8:]
    grad = mine_ref[...]
    for r in received:
        grad = grad + r[size:].astype(F32)
    grad = grad * slope_ref[...]
    hat = hat_ref[...]
    means = group_mean(stacked([column_sums(grad), column_sums(grad * hat)]))
    result = scale_ref[...] * (grad - means[0:1] - hat * means[1:2])
    packed = jnp.dot(pack_ref[...], result.astype(BF16), preferred_element_type=F32).astype(BF16)
    begin = 0
    for out in outs:
        out[...] = packed[begin : begin + out.shape[0]]
        begin += out.shape[0]


def route_kernel(kept_ref, came_ref, *outs):
    some = outs[0].shape[0] // 2
    for k, out in enumerate(outs):
        out[:some] = kept_ref[k * some : (k + 1) * some]
        out[some:] = came_ref[k * some : (k + 1) * some]


def early_kernel(tokens_ref, lines_ref, out_ref, grid, space, sems):
    own = tokens_ref.shape[0]
    first_copy = pltpu.make_async_copy(lines_ref, space, sems.at[0])
    other_copy = pltpu.make_async_copy(tokens_ref, out_ref.at[pl.ds(0, own)], sems.at[1])
    fetch([first_copy, other_copy])
    wide = 2 * TILE_W
    grid[...] = space[...].astype(F32)
    first = grid[pl.ds(0, 2 * ROWS, stride=wide), :]
    last = grid[pl.ds(wide - 1, 2 * ROWS, stride=wide), :]
    odd = lax.axis_index("tile") % 2 == 1
    out_ref[own : own + 2 * ROWS] = jnp.where(odd, first, last).astype(BF16)
    out_ref[own + 2 * ROWS :] = jnp.where(odd, last, first).astype(BF16)


def join_kernel(mine_ref, peer_ref, out_ref):
    own = mine_ref.shape[0] - 4 * ROWS
    out_ref[:own] = mine_ref[:own]
    out_ref[own : 2 * own] = peer_ref[:own]
    out_ref[2 * own :] = peer_ref[own + 2 * ROWS :]


def conv_kernel(multi, *refs):
    own_ref, *received, w_ref, bias_ref, out_ref, grid = refs
    chan = lax.axis_index("chan")
    rows = CELLS + 2 * ROWS
    lanes = own_ref.shape[1]
    size = own_ref.shape[0]
    grid_in = []
    received = [own_ref[...]] + [r[:size] for r in received]
    for c in range(4):
        piece = received[3]
        for k in range(3):
            piece = jnp.where(chan ^ k == c, received[k], piece)
        grid_in.append(piece)
    cells = jnp.concatenate(grid_in, axis=1).astype(F32)
    line = row_index(cells.shape) % ROWS < TILE_H
    early = jnp.where(line, cells, pltpu.roll(cells, TILE_H, 0)).astype(BF16)
    cells = cells.astype(BF16)

    def products(taps, begin):
        x = cells[begin : begin + rows]
        y = early[begin : begin + rows]
        made = {}
        for at in range(0, len(taps), 2):
            pair = taps[at : at + 2]
            acc = None
            for a, left in ((0, y), (9, y), (18, x)):
                right = jnp.concatenate([w_ref[a + t] for t in pair], axis=1)
                term = jnp.dot(left, right, preferred_element_type=F32)
                acc = term if acc is None else acc + term
            for n, t in enumerate(pair):
                made[t] = acc[:, n * lanes : (n + 1) * lanes]
        return made

    def spread(made, b, q):
        first, middle, last = (made[3 * b + e] for e in range(3))
        if q == 0:
            return first[:CELLS] + middle[ROWS:-ROWS] + last[ROWS:-ROWS]
        return first[ROWS:-ROWS] + middle[ROWS:-ROWS] + last[2 * ROWS :]

    made = products(list(range(9)), 0)
    if multi:
        made_above = products([0, 1, 2], rows)
        made_below = products([6, 7, 8], 2 * rows)
    wide = 2 * TILE_W
    for q in range(2):
        top, middle, bottom = (spread(made, b, q) for b in range(3))
        above, below = from_row_above(top), from_row_below(bottom)
        if multi:
            above = above + spread(made_above, 0, q)
            below = below + spread(made_below, 2, q)
        for p, value in enumerate((above + middle + bottom, top + middle + below)):
            value = value + bias_ref[...]
            for j in range(TILE_W):
                grid[pl.ds(p * wide + 2 * j + q, ROWS, stride=2 * wide), :] = value[
                    j * ROWS : (j + 1) * ROWS
                ]
    out_ref[...] = grid[...].astype(BF16)


def place_kernel(put_ref, *refs):
    returned, out_ref = refs[:-1], refs[-1]
    values = [r[...] for r in returned]
    values = jnp.concatenate(values, axis=0) if len(values) > 1 else values[0]
    placed = jnp.dot(put_ref[...], values, preferred_element_type=F32)
    out_ref[...] = placed.astype(BF16)


def cell_of(place):
    return place % ROWS // TILE_H * (TILE_H * TILE_W) + place % TILE_H * TILE_W + place // ROWS


def prep_kernel(across, woven, neighbours, own, capacity, *refs):
    ins, (take_ref, pack_ref, put_ref, *outs), (source_ref, space, sems) = refs[:6], refs[6:-3], refs[-3:]
    copies = [
        pltpu.make_async_copy(hbm, vmem, sems.at[k])
        for k, (hbm, vmem) in enumerate(zip(ins, [source_ref, space] + outs[1:]))
    ]
    for copy in copies:
        copy.start()
    copies[0].wait()
    tile = lax.axis_index("tile")
    source = source_ref[...]
    members = source.shape[0]
    square = (CELLS, CELLS)
    left = lax.broadcasted_iota(jnp.int32, square, 0)
    right = lax.broadcasted_iota(jnp.int32, square, 1)
    place = lax.broadcasted_iota(jnp.int32, (CELLS, members * own), 1)
    for i, (dr, dc) in enumerate(neighbours):
        other = jnp.clip(tile + dr * across + dc, 0, members - 1)
        line = source_ref[pl.ds(other, 1), :]
        wanted = jnp.sum(jnp.where(cell_of(left) == right, line, 0), axis=1, keepdims=True)
        if (dr, dc) == (0, 0):
            owner = wanted // own
            if woven:
                owner = owner ^ tile
                owner = owner // 2 + owner % 2 * (members // 2)
            slot = owner * capacity + wanted % capacity
            slot = jnp.sum(jnp.where(left == right, slot, 0), axis=0, keepdims=True)
        if woven:
            wanted = wanted ^ (tile * own)
        take_ref[i * CELLS : (i + 1) * CELLS] = (place == wanted).astype(F32).astype(BF16)
    pack_ref[...] = (row_index(pack_ref.shape) == slot).astype(F32).astype(BF16)
    mine = source // own == tile
    first = jnp.where(mine, source % own, -capacity)
    first = jnp.max(first, axis=1, keepdims=True) // capacity * capacity
    wide = (members, members * capacity)
    spot = lax.broadcasted_iota(jnp.int32, wide, 1)
    sender = spot // capacity
    if woven:
        sender = sender ^ tile
    meant = jnp.where(sender == row_index(wide), first + spot % capacity, 0)
    meant = jnp.sum(meant, axis=0, keepdims=True)
    put_ref[...] = (row_index(put_ref.shape) == meant).astype(F32).astype(BF16)
    copies[1].wait()
    outs[0][...] = space[...].astype(F32)
    for copy in copies[2:]:
        copy.wait()


def swapped(block, axis, k):
    return lax.ppermute(block, axis, [(i, i ^ k) for i in range(lax.axis_size(axis))])


def local(tokens, cell_source, gain, shift, weight, bias, cotangent):
    members = lax.axis_size("tile")
    own, lanes = tokens.shape
    across = across_tiles()
    multi = members > across
    woven = members == 8
    capacity = max(2, own // (members // 2))
    slots = members * capacity
    high, wide = 2 * TILE_H, 2 * TILE_W
    area = FRAMES * high * wide
    shape = jax.ShapeDtypeStruct

    def block(rows):
        return shape((rows, lanes), BF16)

    neighbours = [(0, -1), (0, 0), (0, 1)]
    if multi:
        neighbours = [(r, c) for r in (-1, 0, 1) for c in (-1, 0, 1)]
    lines = cotangent.reshape(area, lanes)
    spread = pltpu.VMEM((area, lanes), F32)
    flat = [v.reshape(1, lanes) for v in (gain, shift, bias)]
    ins = [cell_source, lines, weight] + flat
    take, pack, put, grid, weight, gain, shift, bias = call(
        functools.partial(prep_kernel, across, woven, neighbours, own, capacity),
        [
            shape((len(neighbours) * CELLS, members * own), BF16),
            shape((slots, CELLS), BF16),
            shape((own, slots), BF16),
            shape((area, lanes), F32),
        ]
        + [shape(v.shape, v.dtype) for v in ins[2:]],
        ins,
        [
            pltpu.VMEM(cell_source.shape, jnp.int32),
            pltpu.VMEM(lines.shape, BF16),
            pltpu.SemaphoreType.DMA((len(ins),)),
        ],
        loose=range(len(ins)),
    )
    if woven:
        (early,) = call(
            early_kernel,
            [block(own + 4 * ROWS)],
            [tokens, lines],
            [spread, pltpu.VMEM((area, lanes), BF16), pltpu.SemaphoreType.DMA((2,))],
            loose=(0, 1),
        )
        peer = swapped(early, "tile", 1)
        (pair,) = call(join_kernel, [block(2 * own + 2 * ROWS)], [early, peer])
        pieces = [pair] + [swapped(pair, "tile", k) for k in (2, 4, 6)]
        others = [peer]
    else:
        pieces = [lax.all_gather(tokens, "tile", axis=0, tiled=True)]
        others = [along_row(lines[wide - 1 :: wide], 1), along_row(lines[::wide], -1)]
    if multi:
        side = (FRAMES, high, 1, lanes)
        widened = [others[0].reshape(side), lines.reshape(FRAMES, high, wide, lanes)]
        widened = jnp.concatenate(widened + [others[1].reshape(side)], axis=2)
        for edge, step, line in ((widened[:, -1], 1, 0), (widened[:, 0], -1, TILE_H - 1)):
            rim = along_column(edge, step).transpose(1, 0, 2)
            spaced = jnp.zeros((wide + 2, FRAMES, TILE_H, lanes), BF16).at[:, :, line].set(rim)
            others.append(spaced.reshape(wide + 2, ROWS, lanes))

    size = (CELLS + 2 * ROWS) * (3 if multi else 1)
    cell = shape((CELLS, lanes), F32)
    mine, hat, slope, scale, *sends, packed = call(
        functools.partial(main_kernel, members, across, woven, neighbours, len(pieces)),
        [cell, cell, cell, shape((1, lanes), F32)] + [block(size + CELLS)] * 3 + [block(size)],
        pieces + [grid, weight, take, gain, shift] + others,
        [pltpu.VMEM((CELLS, CHANNELS), F32), pltpu.VMEM((4 * ROWS, lanes), F32)],
        flops=2 * 27 * CELLS * lanes * CHANNELS,
    )
    received = [swapped(send, "chan", k + 1) for k, send in enumerate(sends)]
    halves = [block(slots // 2)] * 2 if woven else [block(slots)]
    returning = call(
        functools.partial(back_kernel, size),
        halves,
        [mine, hat, slope, scale, pack] + received,
    )
    if woven:
        came = swapped(returning[1], "tile", 1)
        routed = call(route_kernel, [block(2 * capacity)] * 4, [returning[0], came])
        returned = [routed[0]] + [swapped(r, "tile", 2 * k + 2) for k, r in enumerate(routed[1:])]
    else:
        returned = [lax.all_to_all(returning[0], "tile", split_axis=0, concat_axis=0, tiled=True)]
    (decoded,) = call(
        functools.partial(conv_kernel, multi),
        [block(area)],
        [packed] + received + [weight, bias],
        [spread],
        flops=2 * 27 * (CELLS + 2 * ROWS) * lanes * CHANNELS,
    )
    (token_grad,) = call(place_kernel, [block(own)], [put] + returned)
    return decoded.reshape(1, FRAMES, high, wide, lanes), token_grad


def solution(mesh):
    in_specs = (
        P("tile", "chan"),
        P(),
        P("chan"),
        P("chan"),
        P(None, None, "chan"),
        P("chan"),
        P("tile", None, None, None, "chan"),
    )
    out_specs = (P("tile", None, None, None, "chan"), P("tile", "chan"))
    return jax.shard_map(local, mesh=mesh, in_specs=in_specs, out_specs=out_specs, check_vma=False)
```

```python
import functools

import jax
import jax.numpy as jnp
from jax import lax
from jax.experimental import pallas as pl
from jax.experimental.pallas import tpu as pltpu
from jax.sharding import PartitionSpec as P

CHANNELS = 512
GROUP = 16
FRAMES = 2
TILE_H = 4
TILE_W = 8
CELLS = FRAMES * TILE_H * TILE_W
ROWS = FRAMES * TILE_H
EPS = 1e-06
VMEM_LIMIT = 12 * 2**20
F32 = jnp.float32
BF16 = jnp.bfloat16
VMEM = pl.BlockSpec(memory_space=pltpu.VMEM)
FAR = pl.BlockSpec(memory_space=pltpu.HBM)
HIGHEST = lax.Precision.HIGHEST


def call(kernel, outs, args, scratch=(), flops=0, loose=()):
    args = [
        pltpu.with_memory_space_constraint(a, pltpu.HBM) if i in loose else a
        for i, a in enumerate(args)
    ]
    moved = sum(a.size * a.dtype.itemsize for a in args)
    moved += sum(o.size * o.dtype.itemsize for o in outs)
    return pl.pallas_call(
        kernel,
        out_shape=outs,
        in_specs=[FAR if i in loose else VMEM for i in range(len(args))],
        out_specs=[VMEM] * len(outs),
        scratch_shapes=list(scratch),
        compiler_params=pltpu.CompilerParams(vmem_limit_bytes=VMEM_LIMIT),
        cost_estimate=pl.CostEstimate(flops=flops, bytes_accessed=moved, transcendentals=0),
    )(*args)


def across_tiles():
    return min(lax.axis_size("tile"), 16)


def along_row(block, step):
    count, across = lax.axis_size("tile"), across_tiles()
    route = [(i, i + step) for i in range(count) if 0 <= i % across + step < across]
    return lax.ppermute(block, "tile", route)


def along_column(block, step):
    count, across = lax.axis_size("tile"), across_tiles()
    route = [(i, i + step * across) for i in range(count) if 0 <= i + step * across < count]
    return lax.ppermute(block, "tile", route)


def row_index(shape):
    return lax.broadcasted_iota(jnp.int32, shape, 0)


def from_row_above(x):
    keep = row_index(x.shape) % TILE_H != 0
    return jnp.where(keep, pltpu.roll(x, 1, 0), 0.0)


def from_row_below(x):
    keep = row_index(x.shape) % TILE_H != TILE_H - 1
    return jnp.where(keep, pltpu.roll(x, x.shape[0] - 1, 0), 0.0)


def folded_columns(grid, cut, wide, left=None, right=None):
    def column(p, x):
        if x < 0:
            return left(p)
        if x >= wide:
            return right(p)
        return grid[pl.ds(x // cut * (FRAMES * 2 * TILE_H * cut) + p * cut + x % cut, ROWS, stride=2 * cut), :]

    return [[column(p, x) for x in range(-1, wide + 1)] for p in range(2)]


def fold(parts, e):
    pairs = [parts[2 * s + 2 - e] + parts[2 * s + 3 - e] for s in range(len(parts) // 2 - 1)]
    return jnp.concatenate(pairs, axis=0)


def fold_taps(columns, rims=()):
    taps = [None] * 9
    for e in range(3):
        even, odd = fold(columns[0], e), fold(columns[1], e)
        below, above = from_row_below(even), from_row_above(odd)
        if rims:
            high = [rims[0][x].astype(F32) for x in range(len(columns[0]))]
            low = [rims[1][x].astype(F32) for x in range(len(columns[0]))]
            below, above = below + fold(low, e), above + fold(high, e)
        taps[e], taps[3 + e], taps[6 + e] = odd + below, even + odd, above + even
    return taps


def adjoint(taps, w_ref):
    rows = taps[0].shape[0]
    total = jnp.zeros((rows, CHANNELS), F32)
    first = row_index(taps[0].shape) % ROWS < TILE_H
    latest = []
    for tap, value in enumerate(taps):
        both = value + pltpu.roll(value, rows - TILE_H, 0)
        both = jnp.where(first, both, 0.0).astype(BF16)
        latest.append((value.astype(BF16), tap + 18))
        total = total + contract(both, tap, both, tap + 9, w_ref)
        if len(latest) == 2:
            (x, i), (y, j) = latest
            total = total + contract(x, i, y, j, w_ref)
            latest = []
    for x, i in latest:
        total = total + lax.dot_general(
            x, w_ref[i], (((1,), (1,)), ((), ())), preferred_element_type=F32
        )
    return total


def share(partial_ref, outs):
    lanes = outs[0].shape[1]
    chan = lax.axis_index("chan")
    for k, out in enumerate(outs):
        begin = pl.multiple_of((chan ^ k) * lanes, 128)
        out[...] = partial_ref[:, pl.ds(begin, lanes)].astype(out.dtype)


def contract(x, i, y, j, w_ref):
    left = jnp.concatenate([x, y], axis=1)
    right = jnp.concatenate([w_ref[i], w_ref[j]], axis=1)
    return lax.dot_general(left, right, (((1,), (1,)), ((), ())), preferred_element_type=F32)


def group_mean(sums):
    lanes = sums.shape[1]
    left = lax.broadcasted_iota(jnp.int32, (lanes, lanes), 0) // GROUP
    right = lax.broadcasted_iota(jnp.int32, (lanes, lanes), 1) // GROUP
    same = (left == right).astype(F32)
    whole = jnp.dot(sums, same, preferred_element_type=F32, precision=HIGHEST)
    return whole * (1.0 / (CELLS * GROUP))


def column_sums(x):
    return jnp.sum(x, axis=0, keepdims=True)


def silu_parts(hat, gain, shift):
    value = hat * gain + shift
    gate = 1.0 / (1.0 + jnp.exp(-value))
    return value * gate, gate * (1.0 + value * (1.0 - gate)) * gain


def standardized(features):
    means = group_mean(stacked([column_sums(f) for f in features]))
    centred = [f - means[i : i + 1] for i, f in enumerate(features)]
    spreads = group_mean(stacked([column_sums(c * c) for c in centred]))
    scales = lax.rsqrt(spreads + EPS)
    return [c * scales[i : i + 1] for i, c in enumerate(centred)], scales


def tile_adjoint_kernel(grid_ref, w_ref, left_ref, right_ref, *refs):
    rims, outs, (partial_ref, sides) = refs[:-6], refs[-6:-2], refs[-2:]
    wide = 2 * TILE_W
    sides[: 2 * ROWS] = left_ref[...].astype(F32)
    sides[2 * ROWS :] = right_ref[...].astype(F32)
    columns = folded_columns(
        grid_ref,
        wide,
        wide,
        lambda p: sides[pl.ds(p, ROWS, stride=2), :],
        lambda p: sides[pl.ds(2 * ROWS + p, ROWS, stride=2), :],
    )
    partial_ref[...] = adjoint(fold_taps(columns, rims), w_ref)
    share(partial_ref, outs)


def tile_norm_kernel(members, across, neighbours, *refs):
    tokens_ref, take_ref, gain_ref, shift_ref = refs[:4]
    hat_ref, slope_ref, scale_ref, own_ref = refs[4:]
    tile = lax.axis_index("tile")
    tokens = tokens_ref[...]
    lanes = tokens.shape[1]
    gain, shift = gain_ref[...], shift_ref[...]
    there = []
    for dr, dc in neighbours:
        col, row = tile % across + dc, tile // across + dr
        there.append((col >= 0) & (col < across) & (row >= 0) & (row < members // across))
    chosen = take_ref[...]
    features = jnp.dot(chosen, tokens, preferred_element_type=F32)
    features = [features[i * CELLS : (i + 1) * CELLS] for i in range(len(neighbours))]
    hats, scales = standardized(features)
    blocks = {}
    for i, (dr, dc) in enumerate(neighbours):
        hat = hats[i][-ROWS:] if dc == -1 else hats[i][:ROWS] if dc == 1 else hats[i]
        active, slope = silu_parts(hat, gain, shift)
        if (dr, dc) == (0, 0):
            hat_ref[...] = hat
            slope_ref[...] = slope
            scale_ref[...] = scales[i : i + 1]
        else:
            active = jnp.where(there[i], active, 0.0)
        blocks[dr, dc] = active
    parts = [blocks[0, dc] for dc in (-1, 0, 1)]
    if len(neighbours) == 9:
        rows = CELLS + 2 * ROWS
        line = row_index((rows, lanes)) % TILE_H
        for dr, take, keep in ((-1, rows - TILE_H + 1, 0), (1, TILE_H - 1, TILE_H - 1)):
            block = jnp.concatenate([blocks[dr, dc] for dc in (-1, 0, 1)], axis=0)
            parts.append(jnp.where(line == keep, pltpu.roll(block, take, 0), 0.0))
    own_ref[...] = jnp.concatenate(parts, axis=0).astype(BF16)


def pair_adjoint_kernel(taps_ref, w_ref, *refs):
    pieces, outs, (partial_ref, sides) = refs[:4], refs[4:8], refs[8:]
    place = lax.axis_index("tile") // 2
    zero = jnp.zeros((2 * ROWS, taps_ref.shape[2]), BF16)
    left, right = zero, zero
    for k in range(1, 4):
        edges = pieces[k][-4 * ROWS :]
        left = jnp.where(place ^ k == place - 1, edges[2 * ROWS :], left)
        right = jnp.where(place ^ k == place + 1, edges[: 2 * ROWS], right)
    sides[: 2 * ROWS] = left.astype(F32)
    sides[2 * ROWS :] = right.astype(F32)
    rims = []
    for begin in (0, 2 * ROWS):
        even, odd = (sides[pl.ds(begin + p, ROWS, stride=2), :] for p in range(2))
        below, above = from_row_below(even), from_row_above(odd)
        rims.append((odd + below, even + odd, above + even))
    taps = []
    for tap in range(9):
        value, b, e = taps_ref[tap], tap // 3, tap % 3
        if e == 0:
            value = jnp.concatenate([value[:-ROWS], value[-ROWS:] + rims[1][b]], axis=0)
        if e == 2:
            value = jnp.concatenate([value[:ROWS] + rims[0][b], value[ROWS:]], axis=0)
        taps.append(value)
    partial_ref[...] = adjoint(taps, w_ref)
    share(partial_ref, outs)


def pair_norm_kernel(*refs):
    pieces, (take_ref, gain_ref, shift_ref) = refs[:4], refs[4:7]
    hat_ref, slope_ref, scale_ref, own_ref = refs[7:]
    tile = lax.axis_index("tile")
    odd = tile % 2 == 1
    tokens = jnp.concatenate([p[: -4 * ROWS] for p in pieces], axis=0)
    features = jnp.dot(take_ref[...], tokens, preferred_element_type=F32)
    hats, scales = standardized([features[i * CELLS : (i + 1) * CELLS] for i in range(3)])
    hat = jnp.concatenate(hats[:2], axis=0)
    active, slope = silu_parts(hat, gain_ref[...], shift_ref[...])
    hat_ref[...] = hat
    slope_ref[...] = slope
    scale_ref[...] = scales[:2]
    outer = jnp.where(odd, hats[2][:ROWS], hats[2][-ROWS:])
    outer, _ = silu_parts(outer, gain_ref[...], shift_ref[...])
    outer = jnp.where((tile == 0) | (tile == 7), 0.0, outer)
    own_ref[:ROWS] = jnp.where(odd, active[CELLS - ROWS : CELLS], outer).astype(BF16)
    own_ref[ROWS:-ROWS] = jnp.where(odd, active[CELLS:], active[:CELLS]).astype(BF16)
    own_ref[-ROWS:] = jnp.where(odd, outer, active[CELLS : CELLS + ROWS]).astype(BF16)


def stacked(rows):
    lanes = rows[0].shape[1]
    pad = -len(rows) % 8
    if pad:
        rows = rows + [jnp.zeros((pad, lanes), F32)]
    return jnp.concatenate(rows, axis=0)


def fetch(copies):
    for copy in copies:
        copy.start()
    for copy in copies:
        copy.wait()


def back_kernel(*refs):
    mine_ref, hat_ref, slope_ref, scale_ref, pack_ref = refs[:5]
    received, outs = refs[5:8], refs[8:]
    grad = mine_ref[...]
    for r in received:
        grad = grad + r[...].astype(F32)
    grad = grad * slope_ref[...]
    hat = hat_ref[...]
    tiles = grad.shape[0] // CELLS
    spans = [slice(i * CELLS, (i + 1) * CELLS) for i in range(tiles)]
    sums = [column_sums(grad[c]) for c in spans] + [column_sums(grad[c] * hat[c]) for c in spans]
    means = group_mean(stacked(sums))
    result = []
    for i, c in enumerate(spans):
        value = grad[c] - means[i : i + 1] - hat[c] * means[tiles + i : tiles + i + 1]
        result.append(scale_ref[i : i + 1] * value)
    result = (jnp.concatenate(result, axis=0) if tiles > 1 else result[0]).astype(BF16)
    packed = jnp.dot(pack_ref[...], result, preferred_element_type=F32).astype(BF16)
    begin = 0
    for out in outs:
        out[...] = packed[begin : begin + out.shape[0]]
        begin += out.shape[0]


def fetch(copies):
    for copy in copies:
        copy.start()
    for copy in copies:
        copy.wait()


def early_kernel(tokens_ref, lines_ref, own_ref, grid_ref, space, sems):
    fetch(
        [
            pltpu.make_async_copy(tokens_ref, own_ref, sems.at[0]),
            pltpu.make_async_copy(lines_ref, space, sems.at[1]),
        ]
    )
    grid_ref[...] = space[...].astype(F32)


def join_kernel(own_ref, peer_ref, grid_ref, lines_ref, out_ref, pair_ref):
    own, area = own_ref.shape[0], grid_ref.shape[0]
    odd = lax.axis_index("tile") % 2
    wide = 2 * TILE_W
    out_ref[pl.ds(pl.multiple_of(odd * own, own), own), :] = own_ref[...]
    out_ref[pl.ds(pl.multiple_of((1 - odd) * own, own), own), :] = peer_ref[...]
    pair_ref[pl.ds(pl.multiple_of(odd * area, area), area), :] = grid_ref[...]
    pair_ref[pl.ds(pl.multiple_of((1 - odd) * area, area), area), :] = lines_ref[...].astype(F32)
    left = pair_ref[pl.ds(0, 2 * ROWS, stride=wide), :]
    right = pair_ref[pl.ds(area + wide - 1, 2 * ROWS, stride=wide), :]
    out_ref[2 * own : 2 * own + 2 * ROWS] = left.astype(BF16)
    out_ref[2 * own + 2 * ROWS :] = right.astype(BF16)


def conv_kernel(multi, *refs):
    own_ref, *received, w_ref, bias_ref, out_ref, grid = refs
    chan = lax.axis_index("chan")
    rows = CELLS + 2 * ROWS
    lanes = own_ref.shape[1]
    grid_in = []
    received = [own_ref[...]] + [r[...] for r in received]
    for c in range(4):
        piece = received[3]
        for k in range(3):
            piece = jnp.where(chan ^ k == c, received[k], piece)
        grid_in.append(piece)
    cells = jnp.concatenate(grid_in, axis=1).astype(F32)
    line = row_index(cells.shape) % ROWS < TILE_H
    early = jnp.where(line, cells, pltpu.roll(cells, TILE_H, 0)).astype(BF16)
    cells = cells.astype(BF16)

    def products(taps, begin):
        x = cells[begin : begin + rows]
        y = early[begin : begin + rows]
        made = {}
        for at in range(0, len(taps), 2):
            pair = taps[at : at + 2]
            acc = None
            for a, left in ((0, y), (9, y), (18, x)):
                right = jnp.concatenate([w_ref[a + t] for t in pair], axis=1)
                term = jnp.dot(left, right, preferred_element_type=F32)
                acc = term if acc is None else acc + term
            for n, t in enumerate(pair):
                made[t] = acc[:, n * lanes : (n + 1) * lanes]
        return made

    def spread(made, b, q):
        first, middle, last = (made[3 * b + e] for e in range(3))
        if q == 0:
            return first[:CELLS] + middle[ROWS:-ROWS] + last[ROWS:-ROWS]
        return first[ROWS:-ROWS] + middle[ROWS:-ROWS] + last[2 * ROWS :]

    made = products(list(range(9)), 0)
    if multi:
        made_above = products([0, 1, 2], rows)
        made_below = products([6, 7, 8], 2 * rows)
    wide = 2 * TILE_W
    for q in range(2):
        top, middle, bottom = (spread(made, b, q) for b in range(3))
        above, below = from_row_above(top), from_row_below(bottom)
        if multi:
            above = above + spread(made_above, 0, q)
            below = below + spread(made_below, 2, q)
        for p, value in enumerate((above + middle + bottom, top + middle + below)):
            value = value + bias_ref[...]
            for j in range(TILE_W):
                grid[pl.ds(p * wide + 2 * j + q, ROWS, stride=2 * wide), :] = value[
                    j * ROWS : (j + 1) * ROWS
                ]
    out_ref[...] = grid[...].astype(BF16)


def place_kernel(put_ref, *refs):
    returned, out_ref = refs[:-1], refs[-1]
    values = [r[...] for r in returned]
    values = jnp.concatenate(values, axis=0) if len(values) > 1 else values[0]
    placed = jnp.dot(put_ref[...], values, preferred_element_type=F32)
    out_ref[...] = placed.astype(BF16)


def cell_of(place):
    return place % ROWS // TILE_H * (TILE_H * TILE_W) + place % TILE_H * TILE_W + place // ROWS


def sources_of(source_ref, tile):
    square = (CELLS, CELLS)
    left = lax.broadcasted_iota(jnp.int32, square, 0)
    right = lax.broadcasted_iota(jnp.int32, square, 1)
    line = source_ref[pl.ds(tile, 1), :]
    column = jnp.sum(jnp.where(cell_of(left) == right, line, 0), axis=1, keepdims=True)
    return column, jnp.sum(jnp.where(left == right, column, 0), axis=0, keepdims=True)


def one_hot(match):
    return match.astype(F32).astype(BF16)


def first_places(source, own, capacity, sender):
    members = source.shape[0]
    first = jnp.where(source // own == lax.axis_index("tile"), source % own, -capacity)
    first = jnp.max(first, axis=1, keepdims=True) // capacity * capacity
    wide = (members, members * capacity)
    spot = lax.broadcasted_iota(jnp.int32, wide, 1)
    match = sender(spot // capacity) == row_index(wide)
    return jnp.sum(jnp.where(match, first + spot % capacity, 0), axis=0, keepdims=True)


def load_all(ins, outs, sems):
    copies = [
        pltpu.make_async_copy(hbm, vmem, sems.at[k]) for k, (hbm, vmem) in enumerate(zip(ins, outs))
    ]
    for copy in copies:
        copy.start()
    return copies


def tile_prep_kernel(across, neighbours, own, capacity, *refs):
    ins, (take_ref, pack_ref, put_ref, grid_ref, *outs) = refs[:6], refs[6:-3]
    source_ref, space, sems = refs[-3:]
    copies = load_all(ins, [source_ref, space] + outs, sems)
    for copy in copies:
        copy.wait()
    tile = lax.axis_index("tile")
    members = source_ref.shape[0]
    place = lax.broadcasted_iota(jnp.int32, (CELLS, members * own), 1)
    for i, (dr, dc) in enumerate(neighbours):
        other = jnp.clip(tile + dr * across + dc, 0, members - 1)
        column, row = sources_of(source_ref, other)
        if (dr, dc) == (0, 0):
            slot = row // own * capacity + row % capacity
            pack_ref[...] = one_hot(row_index(pack_ref.shape) == slot)
        take_ref[i * CELLS : (i + 1) * CELLS] = one_hot(place == column)
    spots = first_places(source_ref[...], own, capacity, lambda sender: sender)
    put_ref[...] = one_hot(row_index(put_ref.shape) == spots)
    grid_ref[...] = space[...].astype(F32)


def pair_prep_kernel(own, capacity, pair_ref, *refs):
    ins, (take_ref, pack_ref, put_ref, taps_ref, *outs), (source_ref, sems) = refs[:5], refs[5:-2], refs[-2:]
    copies = load_all(ins, [source_ref] + outs, sems)
    wide = 2 * TILE_W
    zero = jnp.zeros((ROWS, pair_ref.shape[1]), F32)
    columns = folded_columns(pair_ref, wide, 2 * wide, lambda p: zero, lambda p: zero)
    for tap, value in enumerate(fold_taps(columns)):
        taps_ref[tap] = value
    copies[0].wait()
    tile = lax.axis_index("tile")
    z, x = tile // 2, tile % 2
    members = source_ref.shape[0]
    place = lax.broadcasted_iota(jnp.int32, (CELLS, members * own), 1)
    outer = jnp.clip(tile + 2 * x - 1, 0, members - 1)
    for i, other in enumerate((2 * z, 2 * z + 1, outer)):
        column, row = sources_of(source_ref, other)
        take_ref[i * CELLS : (i + 1) * CELLS] = one_hot(place == column ^ (2 * z * own))
        if i < 2:
            owner = row // own
            slot = (owner // 2 ^ z) * (2 * capacity) + i * capacity + row % capacity
            slot = jnp.where(owner % 2 == x, slot, -1)
            shape = (pack_ref.shape[0], CELLS)
            pack_ref[:, i * CELLS : (i + 1) * CELLS] = one_hot(row_index(shape) == slot)
    spots = first_places(source_ref[...], own, capacity, lambda k: (k // 2 ^ z) * 2 + k % 2)
    put_ref[...] = one_hot(row_index(put_ref.shape) == spots)
    for copy in copies[1:]:
        copy.wait()


def swapped(block, axis, k):
    return lax.ppermute(block, axis, [(i, i ^ k) for i in range(lax.axis_size(axis))])


def shape(rows, lanes, kind=BF16):
    return jax.ShapeDtypeStruct((rows, lanes), kind)


def chan_swaps(blocks):
    return [swapped(block, "chan", k + 1) for k, block in enumerate(blocks)]


def pair_plan(tokens, cell_source, gain, shift, weight, bias, lines):
    own, lanes = tokens.shape
    members = lax.axis_size("tile")
    capacity = max(2, own // (members // 2))
    slots = members * capacity
    area = lines.shape[0]
    peer = swapped(tokens, "tile", 1)
    other = swapped(lines, "tile", 1)
    kept, grid = call(
        early_kernel,
        [shape(own, lanes), shape(area, lanes, F32)],
        [tokens, lines],
        [pltpu.VMEM((area, lanes), BF16), pltpu.SemaphoreType.DMA((2,))],
        loose=(0, 1),
    )
    block, pair = call(
        join_kernel,
        [shape(2 * own + 4 * ROWS, lanes), shape(2 * area, lanes, F32)],
        [kept, peer, grid, other],
    )
    pieces = [block] + [swapped(block, "tile", k) for k in (2, 4, 6)]
    ins = [cell_source, weight] + [v.reshape(1, lanes) for v in (gain, shift, bias)]
    take, pack, put, taps, weight, gain, shift, bias = call(
        functools.partial(pair_prep_kernel, own, capacity),
        [
            shape(3 * CELLS, members * own),
            shape(slots, 2 * CELLS),
            shape(own, slots),
            jax.ShapeDtypeStruct((9, 2 * CELLS, lanes), F32),
        ]
        + [jax.ShapeDtypeStruct(v.shape, v.dtype) for v in ins[1:]],
        [pair] + ins,
        [pltpu.VMEM(cell_source.shape, jnp.int32), pltpu.SemaphoreType.DMA((len(ins),))],
        loose=range(1, 6),
    )
    cell = shape(2 * CELLS, lanes, F32)
    mine, *sends = call(
        pair_adjoint_kernel,
        [cell] + [shape(2 * CELLS, lanes)] * 3,
        [taps, weight] + pieces,
        [pltpu.VMEM((2 * CELLS, CHANNELS), F32), pltpu.VMEM((4 * ROWS, lanes), F32)],
        flops=4 * 27 * CELLS * lanes * CHANNELS,
    )
    sends = chan_swaps(sends)
    hat, slope, scale, cells = call(
        pair_norm_kernel,
        [cell, cell, shape(2, lanes, F32), shape(CELLS + 2 * ROWS, lanes)],
        pieces + [take, gain, shift],
        flops=6 * CELLS * members * own * lanes,
    )
    received = chan_swaps([cells] * 3)
    routed = call(
        back_kernel,
        [shape(2 * capacity, lanes)] * 4,
        [mine, hat, slope, scale, pack] + sends,
    )
    returned = [routed[0]] + [swapped(r, "tile", 2 * k + 2) for k, r in enumerate(routed[1:])]
    return cells, received, weight, bias, put, returned


def tile_plan(tokens, cell_source, gain, shift, weight, bias, lines):
    own, lanes = tokens.shape
    members = lax.axis_size("tile")
    across = across_tiles()
    multi = members > across
    capacity = max(2, own // (members // 2))
    slots = members * capacity
    high, wide = 2 * TILE_H, 2 * TILE_W
    area = lines.shape[0]
    neighbours = [(0, -1), (0, 0), (0, 1)]
    if multi:
        neighbours = [(r, c) for r in (-1, 0, 1) for c in (-1, 0, 1)]
    gathered = lax.all_gather(tokens, "tile", axis=0, tiled=True)
    others = [along_row(lines[wide - 1 :: wide], 1), along_row(lines[::wide], -1)]
    if multi:
        side = (FRAMES, high, 1, lanes)
        widened = [others[0].reshape(side), lines.reshape(FRAMES, high, wide, lanes)]
        widened = jnp.concatenate(widened + [others[1].reshape(side)], axis=2)
        for edge, step, line in ((widened[:, -1], 1, 0), (widened[:, 0], -1, TILE_H - 1)):
            rim = along_column(edge, step).transpose(1, 0, 2)
            spaced = jnp.zeros((wide + 2, FRAMES, TILE_H, lanes), BF16).at[:, :, line].set(rim)
            others.append(spaced.reshape(wide + 2, ROWS, lanes))
    ins = [cell_source, lines, weight] + [v.reshape(1, lanes) for v in (gain, shift, bias)]
    take, pack, put, grid, weight, gain, shift, bias = call(
        functools.partial(tile_prep_kernel, across, neighbours, own, capacity),
        [
            shape(len(neighbours) * CELLS, members * own),
            shape(slots, CELLS),
            shape(own, slots),
            shape(area, lanes, F32),
        ]
        + [jax.ShapeDtypeStruct(v.shape, v.dtype) for v in ins[2:]],
        ins,
        [
            pltpu.VMEM(cell_source.shape, jnp.int32),
            pltpu.VMEM(lines.shape, BF16),
            pltpu.SemaphoreType.DMA((len(ins),)),
        ],
        loose=range(len(ins)),
    )
    cell = shape(CELLS, lanes, F32)
    mine, *sends = call(
        tile_adjoint_kernel,
        [cell] + [shape(CELLS, lanes)] * 3,
        [grid, weight] + others,
        [pltpu.VMEM((CELLS, CHANNELS), F32), pltpu.VMEM((4 * ROWS, lanes), F32)],
        flops=2 * 27 * CELLS * lanes * CHANNELS,
    )
    sends = chan_swaps(sends)
    size = (CELLS + 2 * ROWS) * (3 if multi else 1)
    hat, slope, scale, cells = call(
        functools.partial(tile_norm_kernel, members, across, neighbours),
        [cell, cell, shape(1, lanes, F32), shape(size, lanes)],
        [gathered, take, gain, shift],
        flops=2 * len(neighbours) * CELLS * members * own * lanes,
    )
    received = chan_swaps([cells] * 3)
    (packed,) = call(back_kernel, [shape(slots, lanes)], [mine, hat, slope, scale, pack] + sends)
    returned = lax.all_to_all(packed, "tile", split_axis=0, concat_axis=0, tiled=True)
    return cells, received, weight, bias, put, [returned]


def local(tokens, cell_source, gain, shift, weight, bias, cotangent):
    own, lanes = tokens.shape
    lines = cotangent.reshape(-1, lanes)
    members = lax.axis_size("tile")
    plan = pair_plan if members == 8 else tile_plan
    cells, received, weight, bias, put, returned = plan(
        tokens, cell_source, gain, shift, weight, bias, lines
    )
    (decoded,) = call(
        functools.partial(conv_kernel, members > across_tiles()),
        [shape(lines.shape[0], lanes)],
        [cells] + received + [weight, bias],
        [pltpu.VMEM(lines.shape, F32)],
        flops=2 * 27 * (CELLS + 2 * ROWS) * lanes * CHANNELS,
    )
    (token_grad,) = call(place_kernel, [shape(own, lanes)], [put] + returned)
    return decoded.reshape(cotangent.shape), token_grad


def solution(mesh):
    in_specs = (
        P("tile", "chan"),
        P(),
        P("chan"),
        P("chan"),
        P(None, None, "chan"),
        P("chan"),
        P("tile", None, None, None, "chan"),
    )
    out_specs = (P("tile", None, None, None, "chan"), P("tile", "chan"))
    return jax.shard_map(local, mesh=mesh, in_specs=in_specs, out_specs=out_specs, check_vma=False)
```

```python
import functools

import jax
import jax.numpy as jnp
from jax import lax
from jax.experimental import pallas as pl
from jax.experimental.pallas import tpu as pltpu
from jax.sharding import PartitionSpec as P

CHANNELS = 512
GROUP = 16
FRAMES = 2
TILE_H = 4
TILE_W = 8
CELLS = FRAMES * TILE_H * TILE_W
ROWS = FRAMES * TILE_H
EPS = 1e-06
VMEM_LIMIT = 12 * 2**20
F32 = jnp.float32
BF16 = jnp.bfloat16
VMEM = pl.BlockSpec(memory_space=pltpu.VMEM)
FAR = pl.BlockSpec(memory_space=pltpu.HBM)
HIGHEST = lax.Precision.HIGHEST


def call(kernel, outs, args, scratch=(), flops=0, loose=()):
    args = [
        pltpu.with_memory_space_constraint(a, pltpu.HBM) if i in loose else a
        for i, a in enumerate(args)
    ]
    moved = sum(a.size * a.dtype.itemsize for a in args)
    moved += sum(o.size * o.dtype.itemsize for o in outs)
    return pl.pallas_call(
        kernel,
        out_shape=outs,
        in_specs=[FAR if i in loose else VMEM for i in range(len(args))],
        out_specs=[VMEM] * len(outs),
        scratch_shapes=list(scratch),
        compiler_params=pltpu.CompilerParams(vmem_limit_bytes=VMEM_LIMIT),
        cost_estimate=pl.CostEstimate(flops=flops, bytes_accessed=moved, transcendentals=0),
    )(*args)


def across_tiles():
    return min(lax.axis_size("tile"), 16)


def along_row(block, step):
    count, across = lax.axis_size("tile"), across_tiles()
    route = [(i, i + step) for i in range(count) if 0 <= i % across + step < across]
    return lax.ppermute(block, "tile", route)


def along_column(block, step):
    count, across = lax.axis_size("tile"), across_tiles()
    route = [(i, i + step * across) for i in range(count) if 0 <= i + step * across < count]
    return lax.ppermute(block, "tile", route)


def row_index(shape):
    return lax.broadcasted_iota(jnp.int32, shape, 0)


def from_row_above(x):
    keep = row_index(x.shape) % TILE_H != 0
    return jnp.where(keep, pltpu.roll(x, 1, 0), 0.0)


def from_row_below(x):
    keep = row_index(x.shape) % TILE_H != TILE_H - 1
    return jnp.where(keep, pltpu.roll(x, x.shape[0] - 1, 0), 0.0)


def folded_columns(grid, cut, wide, left=None, right=None):
    def column(p, x):
        if x < 0:
            return left(p)
        if x >= wide:
            return right(p)
        return grid[pl.ds(x // cut * (FRAMES * 2 * TILE_H * cut) + p * cut + x % cut, ROWS, stride=2 * cut), :]

    return [[column(p, x) for x in range(-1, wide + 1)] for p in range(2)]


def fold(parts, e):
    pairs = [parts[2 * s + 2 - e] + parts[2 * s + 3 - e] for s in range(len(parts) // 2 - 1)]
    return jnp.concatenate(pairs, axis=0)


def fold_taps(columns, rims=()):
    taps = [None] * 9
    for e in range(3):
        even, odd = fold(columns[0], e), fold(columns[1], e)
        below, above = from_row_below(even), from_row_above(odd)
        if rims:
            high = [rims[0][x].astype(F32) for x in range(len(columns[0]))]
            low = [rims[1][x].astype(F32) for x in range(len(columns[0]))]
            below, above = below + fold(low, e), above + fold(high, e)
        taps[e], taps[3 + e], taps[6 + e] = odd + below, even + odd, above + even
    return taps


def adjoint(taps, w_ref):
    rows = taps[0].shape[0]
    total = jnp.zeros((rows, CHANNELS), F32)
    first = row_index(taps[0].shape) % ROWS < TILE_H
    latest = []
    for tap, value in enumerate(taps):
        both = value + pltpu.roll(value, rows - TILE_H, 0)
        both = jnp.where(first, both, 0.0).astype(BF16)
        latest.append((value.astype(BF16), tap + 18))
        total = total + contract(both, tap, both, tap + 9, w_ref)
        if len(latest) == 2:
            (x, i), (y, j) = latest
            total = total + contract(x, i, y, j, w_ref)
            latest = []
    for x, i in latest:
        total = total + lax.dot_general(
            x, w_ref[i], (((1,), (1,)), ((), ())), preferred_element_type=F32
        )
    return total


def share(partial_ref, outs):
    lanes = outs[0].shape[1]
    chan = lax.axis_index("chan")
    for k, out in enumerate(outs):
        begin = pl.multiple_of((chan ^ k) * lanes, 128)
        out[...] = partial_ref[:, pl.ds(begin, lanes)].astype(out.dtype)


def contract(x, i, y, j, w_ref):
    left = jnp.concatenate([x, y], axis=1)
    right = jnp.concatenate([w_ref[i], w_ref[j]], axis=1)
    return lax.dot_general(left, right, (((1,), (1,)), ((), ())), preferred_element_type=F32)


def group_mean(sums):
    lanes = sums.shape[1]
    left = lax.broadcasted_iota(jnp.int32, (lanes, lanes), 0) // GROUP
    right = lax.broadcasted_iota(jnp.int32, (lanes, lanes), 1) // GROUP
    same = (left == right).astype(F32)
    whole = jnp.dot(sums, same, preferred_element_type=F32, precision=HIGHEST)
    return whole * (1.0 / (CELLS * GROUP))


def column_sums(x):
    return jnp.sum(x, axis=0, keepdims=True)


def silu_parts(hat, gain, shift):
    value = hat * gain + shift
    gate = 1.0 / (1.0 + jnp.exp(-value))
    return value * gate, gate * (1.0 + value * (1.0 - gate)) * gain


def standardized(features):
    means = group_mean(stacked([column_sums(f) for f in features]))
    centred = [f - means[i : i + 1] for i, f in enumerate(features)]
    spreads = group_mean(stacked([column_sums(c * c) for c in centred]))
    scales = lax.rsqrt(spreads + EPS)
    return [c * scales[i : i + 1] for i, c in enumerate(centred)], scales


def tile_adjoint_kernel(grid_ref, w_ref, left_ref, right_ref, *refs):
    rims, outs, (partial_ref, sides) = refs[:-6], refs[-6:-2], refs[-2:]
    wide = 2 * TILE_W
    sides[: 2 * ROWS] = left_ref[...].astype(F32)
    sides[2 * ROWS :] = right_ref[...].astype(F32)
    columns = folded_columns(
        grid_ref,
        wide,
        wide,
        lambda p: sides[pl.ds(p, ROWS, stride=2), :],
        lambda p: sides[pl.ds(2 * ROWS + p, ROWS, stride=2), :],
    )
    partial_ref[...] = adjoint(fold_taps(columns, rims), w_ref)
    share(partial_ref, outs)


def tile_norm_kernel(members, across, neighbours, *refs):
    tokens_ref, take_ref, gain_ref, shift_ref = refs[:4]
    hat_ref, slope_ref, scale_ref, own_ref = refs[4:]
    tile = lax.axis_index("tile")
    tokens = tokens_ref[...]
    lanes = tokens.shape[1]
    gain, shift = gain_ref[...], shift_ref[...]
    there = []
    for dr, dc in neighbours:
        col, row = tile % across + dc, tile // across + dr
        there.append((col >= 0) & (col < across) & (row >= 0) & (row < members // across))
    chosen = take_ref[...]
    features = jnp.dot(chosen, tokens, preferred_element_type=F32)
    features = [features[i * CELLS : (i + 1) * CELLS] for i in range(len(neighbours))]
    hats, scales = standardized(features)
    blocks = {}
    for i, (dr, dc) in enumerate(neighbours):
        hat = hats[i][-ROWS:] if dc == -1 else hats[i][:ROWS] if dc == 1 else hats[i]
        active, slope = silu_parts(hat, gain, shift)
        if (dr, dc) == (0, 0):
            hat_ref[...] = hat
            slope_ref[...] = slope
            scale_ref[...] = scales[i : i + 1]
        else:
            active = jnp.where(there[i], active, 0.0)
        blocks[dr, dc] = active
    parts = [blocks[0, dc] for dc in (-1, 0, 1)]
    if len(neighbours) == 9:
        rows = CELLS + 2 * ROWS
        line = row_index((rows, lanes)) % TILE_H
        for dr, take, keep in ((-1, rows - TILE_H + 1, 0), (1, TILE_H - 1, TILE_H - 1)):
            block = jnp.concatenate([blocks[dr, dc] for dc in (-1, 0, 1)], axis=0)
            parts.append(jnp.where(line == keep, pltpu.roll(block, take, 0), 0.0))
    own_ref[...] = jnp.concatenate(parts, axis=0).astype(BF16)


def pair_adjoint_kernel(taps_ref, w_ref, *refs):
    pieces, outs, (partial_ref, sides) = refs[:4], refs[4:8], refs[8:]
    place = lax.axis_index("tile") // 2
    zero = jnp.zeros((2 * ROWS, taps_ref.shape[2]), BF16)
    left, right = zero, zero
    for k in range(1, 4):
        edges = pieces[k][-4 * ROWS :]
        left = jnp.where(place ^ k == place - 1, edges[2 * ROWS :], left)
        right = jnp.where(place ^ k == place + 1, edges[: 2 * ROWS], right)
    sides[: 2 * ROWS] = left.astype(F32)
    sides[2 * ROWS :] = right.astype(F32)
    rims = []
    for begin in (0, 2 * ROWS):
        even, odd = (sides[pl.ds(begin + p, ROWS, stride=2), :] for p in range(2))
        below, above = from_row_below(even), from_row_above(odd)
        rims.append((odd + below, even + odd, above + even))
    taps = []
    for tap in range(9):
        value, b, e = taps_ref[tap], tap // 3, tap % 3
        if e == 0:
            value = jnp.concatenate([value[:-ROWS], value[-ROWS:] + rims[1][b]], axis=0)
        if e == 2:
            value = jnp.concatenate([value[:ROWS] + rims[0][b], value[ROWS:]], axis=0)
        taps.append(value)
    partial_ref[...] = adjoint(taps, w_ref)
    share(partial_ref, outs)


def pair_norm_kernel(*refs):
    pieces, (take_ref, gain_ref, shift_ref) = refs[:4], refs[4:7]
    hat_ref, slope_ref, scale_ref, own_ref = refs[7:]
    tile = lax.axis_index("tile")
    odd = tile % 2 == 1
    tokens = jnp.concatenate([p[: -4 * ROWS] for p in pieces], axis=0)
    features = jnp.dot(take_ref[...], tokens, preferred_element_type=F32)
    hats, scales = standardized([features[i * CELLS : (i + 1) * CELLS] for i in range(3)])
    hat = jnp.concatenate(hats[:2], axis=0)
    active, slope = silu_parts(hat, gain_ref[...], shift_ref[...])
    hat_ref[...] = hat
    slope_ref[...] = slope
    scale_ref[...] = scales[:2]
    outer = jnp.where(odd, hats[2][:ROWS], hats[2][-ROWS:])
    outer, _ = silu_parts(outer, gain_ref[...], shift_ref[...])
    outer = jnp.where((tile == 0) | (tile == 7), 0.0, outer)
    own_ref[:ROWS] = jnp.where(odd, active[CELLS - ROWS : CELLS], outer).astype(BF16)
    own_ref[ROWS:-ROWS] = jnp.where(odd, active[CELLS:], active[:CELLS]).astype(BF16)
    own_ref[-ROWS:] = jnp.where(odd, outer, active[CELLS : CELLS + ROWS]).astype(BF16)


def stacked(rows):
    lanes = rows[0].shape[1]
    pad = -len(rows) % 8
    if pad:
        rows = rows + [jnp.zeros((pad, lanes), F32)]
    return jnp.concatenate(rows, axis=0)


def fetch(copies):
    for copy in copies:
        copy.start()
    for copy in copies:
        copy.wait()


def back_kernel(*refs):
    mine_ref, hat_ref, slope_ref, scale_ref, pack_ref = refs[:5]
    received, outs = refs[5:8], refs[8:]
    grad = mine_ref[...]
    for r in received:
        grad = grad + r[...].astype(F32)
    grad = grad * slope_ref[...]
    hat = hat_ref[...]
    tiles = grad.shape[0] // CELLS
    spans = [slice(i * CELLS, (i + 1) * CELLS) for i in range(tiles)]
    sums = [column_sums(grad[c]) for c in spans] + [column_sums(grad[c] * hat[c]) for c in spans]
    means = group_mean(stacked(sums))
    result = []
    for i, c in enumerate(spans):
        value = grad[c] - means[i : i + 1] - hat[c] * means[tiles + i : tiles + i + 1]
        result.append(scale_ref[i : i + 1] * value)
    result = (jnp.concatenate(result, axis=0) if tiles > 1 else result[0]).astype(BF16)
    packed = jnp.dot(pack_ref[...], result, preferred_element_type=F32).astype(BF16)
    begin = 0
    for out in outs:
        out[...] = packed[begin : begin + out.shape[0]]
        begin += out.shape[0]


def fetch(copies):
    for copy in copies:
        copy.start()
    for copy in copies:
        copy.wait()


def early_kernel(tokens_ref, lines_ref, own_ref, grid_ref, space, sems):
    fetch(
        [
            pltpu.make_async_copy(tokens_ref, own_ref, sems.at[0]),
            pltpu.make_async_copy(lines_ref, space, sems.at[1]),
        ]
    )
    grid_ref[...] = space[...].astype(F32)


def join_kernel(own_ref, peer_ref, grid_ref, lines_ref, after_ref, out_ref, pair_ref):
    own, area = own_ref.shape[0], grid_ref.shape[0]
    odd = lax.axis_index("tile") % 2
    wide = 2 * TILE_W
    out_ref[pl.ds(pl.multiple_of(odd * own, own), own), :] = own_ref[...]
    out_ref[pl.ds(pl.multiple_of((1 - odd) * own, own), own), :] = peer_ref[...]
    pair_ref[pl.ds(pl.multiple_of(odd * area, area), area), :] = grid_ref[...]
    pair_ref[pl.ds(pl.multiple_of((1 - odd) * area, area), area), :] = lines_ref[...].astype(F32)
    left = pair_ref[pl.ds(0, 2 * ROWS, stride=wide), :]
    right = pair_ref[pl.ds(area + wide - 1, 2 * ROWS, stride=wide), :]
    out_ref[2 * own : 2 * own + 2 * ROWS] = left.astype(BF16)
    out_ref[2 * own + 2 * ROWS :] = right.astype(BF16)


def conv_kernel(multi, *refs):
    own_ref, *received, w_ref, bias_ref, out_ref, grid = refs
    chan = lax.axis_index("chan")
    rows = CELLS + 2 * ROWS
    lanes = own_ref.shape[1]
    grid_in = []
    received = [own_ref[...]] + [r[...] for r in received]
    for c in range(4):
        piece = received[3]
        for k in range(3):
            piece = jnp.where(chan ^ k == c, received[k], piece)
        grid_in.append(piece)
    cells = jnp.concatenate(grid_in, axis=1).astype(F32)
    line = row_index(cells.shape) % ROWS < TILE_H
    early = jnp.where(line, cells, pltpu.roll(cells, TILE_H, 0)).astype(BF16)
    cells = cells.astype(BF16)

    def products(taps, begin):
        x = cells[begin : begin + rows]
        y = early[begin : begin + rows]
        made = {}
        for at in range(0, len(taps), 2):
            pair = taps[at : at + 2]
            acc = None
            for a, left in ((0, y), (9, y), (18, x)):
                right = jnp.concatenate([w_ref[a + t] for t in pair], axis=1)
                term = jnp.dot(left, right, preferred_element_type=F32)
                acc = term if acc is None else acc + term
            for n, t in enumerate(pair):
                made[t] = acc[:, n * lanes : (n + 1) * lanes]
        return made

    def spread(made, b, q):
        first, middle, last = (made[3 * b + e] for e in range(3))
        if q == 0:
            return first[:CELLS] + middle[ROWS:-ROWS] + last[ROWS:-ROWS]
        return first[ROWS:-ROWS] + middle[ROWS:-ROWS] + last[2 * ROWS :]

    made = products(list(range(9)), 0)
    if multi:
        made_above = products([0, 1, 2], rows)
        made_below = products([6, 7, 8], 2 * rows)
    wide = 2 * TILE_W
    for q in range(2):
        top, middle, bottom = (spread(made, b, q) for b in range(3))
        above, below = from_row_above(top), from_row_below(bottom)
        if multi:
            above = above + spread(made_above, 0, q)
            below = below + spread(made_below, 2, q)
        for p, value in enumerate((above + middle + bottom, top + middle + below)):
            value = value + bias_ref[...]
            for j in range(TILE_W):
                grid[pl.ds(p * wide + 2 * j + q, ROWS, stride=2 * wide), :] = value[
                    j * ROWS : (j + 1) * ROWS
                ]
    out_ref[...] = grid[...].astype(BF16)


def place_kernel(put_ref, *refs):
    returned, out_ref = refs[:-1], refs[-1]
    values = [r[...] for r in returned]
    values = jnp.concatenate(values, axis=0) if len(values) > 1 else values[0]
    placed = jnp.dot(put_ref[...], values, preferred_element_type=F32)
    out_ref[...] = placed.astype(BF16)


def cell_of(place):
    return place % ROWS // TILE_H * (TILE_H * TILE_W) + place % TILE_H * TILE_W + place // ROWS


def sources_of(source_ref, tile):
    square = (CELLS, CELLS)
    left = lax.broadcasted_iota(jnp.int32, square, 0)
    right = lax.broadcasted_iota(jnp.int32, square, 1)
    line = source_ref[pl.ds(tile, 1), :]
    column = jnp.sum(jnp.where(cell_of(left) == right, line, 0), axis=1, keepdims=True)
    return column, jnp.sum(jnp.where(left == right, column, 0), axis=0, keepdims=True)


def one_hot(match):
    return match.astype(F32).astype(BF16)


def first_places(source, own, capacity, sender):
    members = source.shape[0]
    first = jnp.where(source // own == lax.axis_index("tile"), source % own, -capacity)
    first = jnp.max(first, axis=1, keepdims=True) // capacity * capacity
    wide = (members, members * capacity)
    spot = lax.broadcasted_iota(jnp.int32, wide, 1)
    match = sender(spot // capacity) == row_index(wide)
    return jnp.sum(jnp.where(match, first + spot % capacity, 0), axis=0, keepdims=True)


def load_all(ins, outs, sems):
    copies = [
        pltpu.make_async_copy(hbm, vmem, sems.at[k]) for k, (hbm, vmem) in enumerate(zip(ins, outs))
    ]
    for copy in copies:
        copy.start()
    return copies


def tile_prep_kernel(across, neighbours, own, capacity, *refs):
    ins, (take_ref, pack_ref, put_ref, grid_ref, *outs) = refs[:6], refs[6:-3]
    source_ref, space, sems = refs[-3:]
    copies = load_all(ins, [source_ref, space] + outs, sems)
    for copy in copies:
        copy.wait()
    tile = lax.axis_index("tile")
    members = source_ref.shape[0]
    place = lax.broadcasted_iota(jnp.int32, (CELLS, members * own), 1)
    for i, (dr, dc) in enumerate(neighbours):
        other = jnp.clip(tile + dr * across + dc, 0, members - 1)
        column, row = sources_of(source_ref, other)
        if (dr, dc) == (0, 0):
            slot = row // own * capacity + row % capacity
            pack_ref[...] = one_hot(row_index(pack_ref.shape) == slot)
        take_ref[i * CELLS : (i + 1) * CELLS] = one_hot(place == column)
    spots = first_places(source_ref[...], own, capacity, lambda sender: sender)
    put_ref[...] = one_hot(row_index(put_ref.shape) == spots)
    grid_ref[...] = space[...].astype(F32)


def pair_prep_kernel(own, capacity, *refs):
    ins, (take_ref, pack_ref, put_ref, *outs) = refs[:5], refs[5:-2]
    source_ref, sems = refs[-2:]
    copies = load_all(ins, [source_ref] + outs, sems)
    copies[0].wait()
    tile = lax.axis_index("tile")
    z, x = tile // 2, tile % 2
    members = source_ref.shape[0]
    place = lax.broadcasted_iota(jnp.int32, (CELLS, members * own), 1)
    outer = jnp.clip(tile + 2 * x - 1, 0, members - 1)
    for i, other in enumerate((2 * z, 2 * z + 1, outer)):
        column, row = sources_of(source_ref, other)
        take_ref[i * CELLS : (i + 1) * CELLS] = one_hot(place == column ^ (2 * z * own))
        if i < 2:
            owner = row // own
            slot = (owner // 2 ^ z) * (2 * capacity) + i * capacity + row % capacity
            slot = jnp.where(owner % 2 == x, slot, -1)
            shape = (pack_ref.shape[0], CELLS)
            pack_ref[:, i * CELLS : (i + 1) * CELLS] = one_hot(row_index(shape) == slot)
    spots = first_places(source_ref[...], own, capacity, lambda k: (k // 2 ^ z) * 2 + k % 2)
    put_ref[...] = one_hot(row_index(put_ref.shape) == spots)
    for copy in copies[1:]:
        copy.wait()


def pair_fold_kernel(pair_ref, taps_ref):
    wide = 2 * TILE_W
    zero = jnp.zeros((ROWS, pair_ref.shape[1]), F32)
    columns = folded_columns(pair_ref, wide, 2 * wide, lambda p: zero, lambda p: zero)
    for tap, value in enumerate(fold_taps(columns)):
        taps_ref[tap] = value


def swapped(block, axis, k):
    return lax.ppermute(block, axis, [(i, i ^ k) for i in range(lax.axis_size(axis))])


def shape(rows, lanes, kind=BF16):
    return jax.ShapeDtypeStruct((rows, lanes), kind)


def chan_swaps(blocks):
    return [swapped(block, "chan", k + 1) for k, block in enumerate(blocks)]


def pair_plan(tokens, cell_source, gain, shift, weight, bias, lines):
    own, lanes = tokens.shape
    members = lax.axis_size("tile")
    capacity = max(2, own // (members // 2))
    slots = members * capacity
    area = lines.shape[0]
    peer = swapped(tokens, "tile", 1)
    other = swapped(lines, "tile", 1)
    kept, grid = call(
        early_kernel,
        [shape(own, lanes), shape(area, lanes, F32)],
        [tokens, lines],
        [pltpu.VMEM((area, lanes), BF16), pltpu.SemaphoreType.DMA((2,))],
        loose=(0, 1),
    )
    ins = [cell_source, weight] + [v.reshape(1, lanes) for v in (gain, shift, bias)]
    take, pack, put, weight, gain, shift, bias = call(
        functools.partial(pair_prep_kernel, own, capacity),
        [
            shape(3 * CELLS, members * own),
            shape(slots, 2 * CELLS),
            shape(own, slots),
        ]
        + [jax.ShapeDtypeStruct(v.shape, v.dtype) for v in ins[1:]],
        ins,
        [pltpu.VMEM(cell_source.shape, jnp.int32), pltpu.SemaphoreType.DMA((len(ins),))],
        loose=range(5),
    )
    block, pair = call(
        join_kernel,
        [shape(2 * own + 4 * ROWS, lanes), shape(2 * area, lanes, F32)],
        [kept, peer, grid, other, put],
    )
    pieces = [block] + [swapped(block, "tile", k) for k in (2, 4, 6)]
    (taps,) = call(pair_fold_kernel, [jax.ShapeDtypeStruct((9, 2 * CELLS, lanes), F32)], [pair])
    cell = shape(2 * CELLS, lanes, F32)
    mine, *sends = call(
        pair_adjoint_kernel,
        [cell] + [shape(2 * CELLS, lanes)] * 3,
        [taps, weight] + pieces,
        [pltpu.VMEM((2 * CELLS, CHANNELS), F32), pltpu.VMEM((4 * ROWS, lanes), F32)],
        flops=4 * 27 * CELLS * lanes * CHANNELS,
    )
    sends = chan_swaps(sends)
    hat, slope, scale, cells = call(
        pair_norm_kernel,
        [cell, cell, shape(2, lanes, F32), shape(CELLS + 2 * ROWS, lanes)],
        pieces + [take, gain, shift],
        flops=6 * CELLS * members * own * lanes,
    )
    received = chan_swaps([cells] * 3)
    routed = call(
        back_kernel,
        [shape(2 * capacity, lanes)] * 4,
        [mine, hat, slope, scale, pack] + sends,
    )
    returned = [routed[0]] + [swapped(r, "tile", 2 * k + 2) for k, r in enumerate(routed[1:])]
    return cells, received, weight, bias, put, returned


def tile_plan(tokens, cell_source, gain, shift, weight, bias, lines):
    own, lanes = tokens.shape
    members = lax.axis_size("tile")
    across = across_tiles()
    multi = members > across
    capacity = max(2, own // (members // 2))
    slots = members * capacity
    high, wide = 2 * TILE_H, 2 * TILE_W
    area = lines.shape[0]
    neighbours = [(0, -1), (0, 0), (0, 1)]
    if multi:
        neighbours = [(r, c) for r in (-1, 0, 1) for c in (-1, 0, 1)]
    gathered = lax.all_gather(tokens, "tile", axis=0, tiled=True)
    others = [along_row(lines[wide - 1 :: wide], 1), along_row(lines[::wide], -1)]
    if multi:
        side = (FRAMES, high, 1, lanes)
        widened = [others[0].reshape(side), lines.reshape(FRAMES, high, wide, lanes)]
        widened = jnp.concatenate(widened + [others[1].reshape(side)], axis=2)
        for edge, step, line in ((widened[:, -1], 1, 0), (widened[:, 0], -1, TILE_H - 1)):
            rim = along_column(edge, step).transpose(1, 0, 2)
            spaced = jnp.zeros((wide + 2, FRAMES, TILE_H, lanes), BF16).at[:, :, line].set(rim)
            others.append(spaced.reshape(wide + 2, ROWS, lanes))
    ins = [cell_source, lines, weight] + [v.reshape(1, lanes) for v in (gain, shift, bias)]
    take, pack, put, grid, weight, gain, shift, bias = call(
        functools.partial(tile_prep_kernel, across, neighbours, own, capacity),
        [
            shape(len(neighbours) * CELLS, members * own),
            shape(slots, CELLS),
            shape(own, slots),
            shape(area, lanes, F32),
        ]
        + [jax.ShapeDtypeStruct(v.shape, v.dtype) for v in ins[2:]],
        ins,
        [
            pltpu.VMEM(cell_source.shape, jnp.int32),
            pltpu.VMEM(lines.shape, BF16),
            pltpu.SemaphoreType.DMA((len(ins),)),
        ],
        loose=range(len(ins)),
    )
    cell = shape(CELLS, lanes, F32)
    mine, *sends = call(
        tile_adjoint_kernel,
        [cell] + [shape(CELLS, lanes)] * 3,
        [grid, weight] + others,
        [pltpu.VMEM((CELLS, CHANNELS), F32), pltpu.VMEM((4 * ROWS, lanes), F32)],
        flops=2 * 27 * CELLS * lanes * CHANNELS,
    )
    sends = chan_swaps(sends)
    size = (CELLS + 2 * ROWS) * (3 if multi else 1)
    hat, slope, scale, cells = call(
        functools.partial(tile_norm_kernel, members, across, neighbours),
        [cell, cell, shape(1, lanes, F32), shape(size, lanes)],
        [gathered, take, gain, shift],
        flops=2 * len(neighbours) * CELLS * members * own * lanes,
    )
    received = chan_swaps([cells] * 3)
    (packed,) = call(back_kernel, [shape(slots, lanes)], [mine, hat, slope, scale, pack] + sends)
    returned = lax.all_to_all(packed, "tile", split_axis=0, concat_axis=0, tiled=True)
    return cells, received, weight, bias, put, [returned]


def local(tokens, cell_source, gain, shift, weight, bias, cotangent):
    own, lanes = tokens.shape
    lines = cotangent.reshape(-1, lanes)
    members = lax.axis_size("tile")
    plan = pair_plan if members == 8 else tile_plan
    cells, received, weight, bias, put, returned = plan(
        tokens, cell_source, gain, shift, weight, bias, lines
    )
    (decoded,) = call(
        functools.partial(conv_kernel, members > across_tiles()),
        [shape(lines.shape[0], lanes)],
        [cells] + received + [weight, bias],
        [pltpu.VMEM(lines.shape, F32)],
        flops=2 * 27 * (CELLS + 2 * ROWS) * lanes * CHANNELS,
    )
    (token_grad,) = call(place_kernel, [shape(own, lanes)], [put] + returned)
    return decoded.reshape(cotangent.shape), token_grad


def solution(mesh):
    in_specs = (
        P("tile", "chan"),
        P(),
        P("chan"),
        P("chan"),
        P(None, None, "chan"),
        P("chan"),
        P("tile", None, None, None, "chan"),
    )
    out_specs = (P("tile", None, None, None, "chan"), P("tile", "chan"))
    return jax.shard_map(local, mesh=mesh, in_specs=in_specs, out_specs=out_specs, check_vma=False)
```

```python
import functools

import jax
import jax.numpy as jnp
from jax import lax
from jax.experimental import pallas as pl
from jax.experimental.pallas import tpu as pltpu
from jax.sharding import PartitionSpec as P

CHANNELS = 512
GROUP = 16
FRAMES = 2
TILE_H = 4
TILE_W = 8
CELLS = FRAMES * TILE_H * TILE_W
ROWS = FRAMES * TILE_H
EPS = 1e-06
VMEM_LIMIT = 12 * 2**20
SPLIT = 240
F32 = jnp.float32
BF16 = jnp.bfloat16
VMEM = pl.BlockSpec(memory_space=pltpu.VMEM)
FAR = pl.BlockSpec(memory_space=pltpu.HBM)
HIGHEST = lax.Precision.HIGHEST


def call(kernel, outs, args, scratch=(), flops=0, loose=()):
    args = [
        pltpu.with_memory_space_constraint(a, pltpu.HBM) if i in loose else a
        for i, a in enumerate(args)
    ]
    moved = sum(a.size * a.dtype.itemsize for a in args)
    moved += sum(o.size * o.dtype.itemsize for o in outs)
    return pl.pallas_call(
        kernel,
        out_shape=outs,
        in_specs=[FAR if i in loose else VMEM for i in range(len(args))],
        out_specs=[VMEM] * len(outs),
        scratch_shapes=list(scratch),
        compiler_params=pltpu.CompilerParams(vmem_limit_bytes=VMEM_LIMIT),
        cost_estimate=pl.CostEstimate(flops=flops, bytes_accessed=moved, transcendentals=0),
    )(*args)


def across_tiles():
    return min(lax.axis_size("tile"), 16)


def along_row(block, step):
    count, across = lax.axis_size("tile"), across_tiles()
    route = [(i, i + step) for i in range(count) if 0 <= i % across + step < across]
    return lax.ppermute(block, "tile", route)


def along_column(block, step):
    count, across = lax.axis_size("tile"), across_tiles()
    route = [(i, i + step * across) for i in range(count) if 0 <= i + step * across < count]
    return lax.ppermute(block, "tile", route)


def row_index(shape):
    return lax.broadcasted_iota(jnp.int32, shape, 0)


def from_row_above(x):
    keep = row_index(x.shape) % TILE_H != 0
    return jnp.where(keep, pltpu.roll(x, 1, 0), 0.0)


def from_row_below(x):
    keep = row_index(x.shape) % TILE_H != TILE_H - 1
    return jnp.where(keep, pltpu.roll(x, x.shape[0] - 1, 0), 0.0)


def folded_columns(grid, cut, wide, left=None, right=None):
    def column(p, x):
        if x < 0:
            return left(p)
        if x >= wide:
            return right(p)
        return grid[pl.ds(x // cut * (FRAMES * 2 * TILE_H * cut) + p * cut + x % cut, ROWS, stride=2 * cut), :]

    return [[column(p, x) for x in range(-1, wide + 1)] for p in range(2)]


def fold(parts, e):
    pairs = [parts[2 * s + 2 - e] + parts[2 * s + 3 - e] for s in range(len(parts) // 2 - 1)]
    return jnp.concatenate(pairs, axis=0)


def fold_taps(columns, rims=()):
    taps = [None] * 9
    for e in range(3):
        even, odd = fold(columns[0], e), fold(columns[1], e)
        below, above = from_row_below(even), from_row_above(odd)
        if rims:
            high = [rims[0][x].astype(F32) for x in range(len(columns[0]))]
            low = [rims[1][x].astype(F32) for x in range(len(columns[0]))]
            below, above = below + fold(low, e), above + fold(high, e)
        taps[e], taps[3 + e], taps[6 + e] = odd + below, even + odd, above + even
    return taps


def adjoint(taps, w_ref):
    rows = taps[0].shape[0]
    total = jnp.zeros((rows, CHANNELS), F32)
    first = row_index(taps[0].shape) % ROWS < TILE_H
    latest = []
    for tap, value in enumerate(taps):
        both = value + pltpu.roll(value, rows - TILE_H, 0)
        both = jnp.where(first, both, 0.0).astype(BF16)
        latest.append((value.astype(BF16), tap + 18))
        total = total + contract(both, tap, both, tap + 9, w_ref)
        if len(latest) == 2:
            (x, i), (y, j) = latest
            total = total + contract(x, i, y, j, w_ref)
            latest = []
    for x, i in latest:
        total = total + lax.dot_general(
            x, w_ref[i], (((1,), (1,)), ((), ())), preferred_element_type=F32
        )
    return total


def share(partial_ref, outs):
    lanes = outs[0].shape[1]
    chan = lax.axis_index("chan")
    for k, out in enumerate(outs):
        begin = pl.multiple_of((chan ^ k) * lanes, 128)
        out[...] = partial_ref[:, pl.ds(begin, lanes)].astype(out.dtype)


def contract(x, i, y, j, w_ref):
    left = jnp.concatenate([x, y], axis=1)
    right = jnp.concatenate([w_ref[i], w_ref[j]], axis=1)
    return lax.dot_general(left, right, (((1,), (1,)), ((), ())), preferred_element_type=F32)


def group_mean(sums):
    lanes = sums.shape[1]
    left = lax.broadcasted_iota(jnp.int32, (lanes, lanes), 0) // GROUP
    right = lax.broadcasted_iota(jnp.int32, (lanes, lanes), 1) // GROUP
    same = (left == right).astype(F32)
    whole = jnp.dot(sums, same, preferred_element_type=F32, precision=HIGHEST)
    return whole * (1.0 / (CELLS * GROUP))


def column_sums(x):
    return jnp.sum(x, axis=0, keepdims=True)


def silu_parts(hat, gain, shift):
    value = hat * gain + shift
    gate = 1.0 / (1.0 + jnp.exp(-value))
    return value * gate, gate * (1.0 + value * (1.0 - gate)) * gain


def standardized(features):
    means = group_mean(stacked([column_sums(f) for f in features]))
    centred = [f - means[i : i + 1] for i, f in enumerate(features)]
    spreads = group_mean(stacked([column_sums(c * c) for c in centred]))
    scales = lax.rsqrt(spreads + EPS)
    return [c * scales[i : i + 1] for i, c in enumerate(centred)], scales


def tile_adjoint_kernel(grid_ref, w_ref, left_ref, right_ref, *refs):
    rims, outs, (partial_ref, sides) = refs[:-6], refs[-6:-2], refs[-2:]
    wide = 2 * TILE_W
    sides[: 2 * ROWS] = left_ref[...].astype(F32)
    sides[2 * ROWS :] = right_ref[...].astype(F32)
    columns = folded_columns(
        grid_ref,
        wide,
        wide,
        lambda p: sides[pl.ds(p, ROWS, stride=2), :],
        lambda p: sides[pl.ds(2 * ROWS + p, ROWS, stride=2), :],
    )
    partial_ref[...] = adjoint(fold_taps(columns, rims), w_ref)
    share(partial_ref, outs)


def tile_norm_kernel(members, across, neighbours, *refs):
    tokens_ref, take_ref, gain_ref, shift_ref = refs[:4]
    hat_ref, slope_ref, scale_ref, own_ref = refs[4:]
    tile = lax.axis_index("tile")
    tokens = tokens_ref[...]
    lanes = tokens.shape[1]
    gain, shift = gain_ref[...], shift_ref[...]
    there = []
    for dr, dc in neighbours:
        col, row = tile % across + dc, tile // across + dr
        there.append((col >= 0) & (col < across) & (row >= 0) & (row < members // across))
    chosen = take_ref[...]
    features = jnp.dot(chosen, tokens, preferred_element_type=F32)
    features = [features[i * CELLS : (i + 1) * CELLS] for i in range(len(neighbours))]
    hats, scales = standardized(features)
    blocks = {}
    for i, (dr, dc) in enumerate(neighbours):
        hat = hats[i][-ROWS:] if dc == -1 else hats[i][:ROWS] if dc == 1 else hats[i]
        active, slope = silu_parts(hat, gain, shift)
        if (dr, dc) == (0, 0):
            hat_ref[...] = hat
            slope_ref[...] = slope
            scale_ref[...] = scales[i : i + 1]
        else:
            active = jnp.where(there[i], active, 0.0)
        blocks[dr, dc] = active
    parts = [blocks[0, dc] for dc in (-1, 0, 1)]
    if len(neighbours) == 9:
        rows = CELLS + 2 * ROWS
        line = row_index((rows, lanes)) % TILE_H
        for dr, take, keep in ((-1, rows - TILE_H + 1, 0), (1, TILE_H - 1, TILE_H - 1)):
            block = jnp.concatenate([blocks[dr, dc] for dc in (-1, 0, 1)], axis=0)
            parts.append(jnp.where(line == keep, pltpu.roll(block, take, 0), 0.0))
    own_ref[...] = jnp.concatenate(parts, axis=0).astype(BF16)


def pair_adjoint_kernel(taps_ref, w_ref, *refs):
    pieces, outs, (partial_ref, sides) = refs[:4], refs[4:8], refs[8:]
    place = lax.axis_index("tile") // 2
    zero = jnp.zeros((2 * ROWS, taps_ref.shape[2]), BF16)
    left, right = zero, zero
    for k in range(1, 4):
        edges = pieces[k][-4 * ROWS :]
        left = jnp.where(place ^ k == place - 1, edges[2 * ROWS :], left)
        right = jnp.where(place ^ k == place + 1, edges[: 2 * ROWS], right)
    sides[: 2 * ROWS] = left.astype(F32)
    sides[2 * ROWS :] = right.astype(F32)
    rims = []
    for begin in (0, 2 * ROWS):
        even, odd = (sides[pl.ds(begin + p, ROWS, stride=2), :] for p in range(2))
        below, above = from_row_below(even), from_row_above(odd)
        rims.append((odd + below, even + odd, above + even))
    taps = []
    for tap in range(9):
        value, b, e = taps_ref[tap], tap // 3, tap % 3
        if e == 0:
            value = jnp.concatenate([value[:-ROWS], value[-ROWS:] + rims[1][b]], axis=0)
        if e == 2:
            value = jnp.concatenate([value[:ROWS] + rims[0][b], value[ROWS:]], axis=0)
        taps.append(value)
    partial_ref[...] = adjoint(taps, w_ref)
    share(partial_ref, outs)


def pair_norm_kernel(*refs):
    pieces, (take_ref, gain_ref, shift_ref) = refs[:4], refs[4:7]
    hat_ref, slope_ref, scale_ref, own_ref = refs[7:]
    tile = lax.axis_index("tile")
    odd = tile % 2 == 1
    tokens = jnp.concatenate([p[: -4 * ROWS] for p in pieces], axis=0)
    features = jnp.dot(take_ref[...], tokens, preferred_element_type=F32)
    hats, scales = standardized([features[i * CELLS : (i + 1) * CELLS] for i in range(3)])
    hat = jnp.concatenate(hats[:2], axis=0)
    active, slope = silu_parts(hat, gain_ref[...], shift_ref[...])
    hat_ref[...] = hat
    slope_ref[...] = slope
    scale_ref[...] = scales[:2]
    outer = jnp.where(odd, hats[2][:ROWS], hats[2][-ROWS:])
    outer, _ = silu_parts(outer, gain_ref[...], shift_ref[...])
    outer = jnp.where((tile == 0) | (tile == 7), 0.0, outer)
    own_ref[:ROWS] = jnp.where(odd, active[CELLS - ROWS : CELLS], outer).astype(BF16)
    own_ref[ROWS:-ROWS] = jnp.where(odd, active[CELLS:], active[:CELLS]).astype(BF16)
    own_ref[-ROWS:] = jnp.where(odd, outer, active[CELLS : CELLS + ROWS]).astype(BF16)


def stacked(rows):
    lanes = rows[0].shape[1]
    pad = -len(rows) % 8
    if pad:
        rows = rows + [jnp.zeros((pad, lanes), F32)]
    return jnp.concatenate(rows, axis=0)


def fetch(copies):
    for copy in copies:
        copy.start()
    for copy in copies:
        copy.wait()


def back_kernel(*refs):
    mine_ref, hat_ref, slope_ref, scale_ref, pack_ref = refs[:5]
    received, outs = refs[5:8], refs[8:]
    grad = mine_ref[...]
    for r in received:
        grad = grad + r[...].astype(F32)
    grad = grad * slope_ref[...]
    hat = hat_ref[...]
    tiles = grad.shape[0] // CELLS
    spans = [slice(i * CELLS, (i + 1) * CELLS) for i in range(tiles)]
    sums = [column_sums(grad[c]) for c in spans] + [column_sums(grad[c] * hat[c]) for c in spans]
    means = group_mean(stacked(sums))
    result = []
    for i, c in enumerate(spans):
        value = grad[c] - means[i : i + 1] - hat[c] * means[tiles + i : tiles + i + 1]
        result.append(scale_ref[i : i + 1] * value)
    result = (jnp.concatenate(result, axis=0) if tiles > 1 else result[0]).astype(BF16)
    packed = jnp.dot(pack_ref[...], result, preferred_element_type=F32).astype(BF16)
    begin = 0
    for out in outs:
        out[...] = packed[begin : begin + out.shape[0]]
        begin += out.shape[0]


def fetch(copies):
    for copy in copies:
        copy.start()
    for copy in copies:
        copy.wait()


def early_kernel(tokens_ref, lines_ref, out_ref, *refs):
    parts, (grid_ref, space, sems) = refs[:-3], refs[-3:]
    own = tokens_ref.shape[0]
    fetch(
        [
            pltpu.make_async_copy(tokens_ref, out_ref.at[pl.ds(0, own)], sems.at[0]),
            pltpu.make_async_copy(lines_ref, space, sems.at[1]),
        ]
    )
    size = parts[0].shape[0]
    parts[0][...] = space[:size]
    out_ref[own + 2 * ROWS :] = space[size:]
    grid_ref[...] = space[...].astype(F32)
    wide = 2 * TILE_W
    first = grid_ref[pl.ds(0, 2 * ROWS, stride=wide), :]
    last = grid_ref[pl.ds(wide - 1, 2 * ROWS, stride=wide), :]
    odd = lax.axis_index("tile") % 2 == 1
    out_ref[own : own + 2 * ROWS] = jnp.where(odd, last, first).astype(BF16)


def join_kernel(mine_ref, peer_ref, after_ref, out_ref):
    own = (out_ref.shape[0] - 4 * ROWS) // 2
    odd = lax.axis_index("tile") % 2 == 1
    mine, peer = mine_ref[...], peer_ref[...]
    even_one, odd_one = jnp.where(odd, peer, mine), jnp.where(odd, mine, peer)
    out_ref[:own] = even_one[:own]
    out_ref[own : 2 * own] = odd_one[:own]
    out_ref[2 * own : 2 * own + 2 * ROWS] = even_one[own : own + 2 * ROWS]
    out_ref[2 * own + 2 * ROWS :] = odd_one[own : own + 2 * ROWS]


def conv_kernel(multi, *refs):
    own_ref, *received, w_ref, bias_ref, out_ref, grid = refs
    chan = lax.axis_index("chan")
    rows = CELLS + 2 * ROWS
    lanes = own_ref.shape[1]
    grid_in = []
    received = [own_ref[...]] + [r[...] for r in received]
    for c in range(4):
        piece = received[3]
        for k in range(3):
            piece = jnp.where(chan ^ k == c, received[k], piece)
        grid_in.append(piece)
    cells = jnp.concatenate(grid_in, axis=1).astype(F32)
    line = row_index(cells.shape) % ROWS < TILE_H
    early = jnp.where(line, cells, pltpu.roll(cells, TILE_H, 0)).astype(BF16)
    cells = cells.astype(BF16)

    def products(taps, begin):
        x = cells[begin : begin + rows]
        y = early[begin : begin + rows]
        made = {}
        for at in range(0, len(taps), 2):
            pair = taps[at : at + 2]
            acc = None
            for a, left in ((0, y), (9, y), (18, x)):
                right = jnp.concatenate([w_ref[a + t] for t in pair], axis=1)
                term = jnp.dot(left, right, preferred_element_type=F32)
                acc = term if acc is None else acc + term
            for n, t in enumerate(pair):
                made[t] = acc[:, n * lanes : (n + 1) * lanes]
        return made

    def spread(made, b, q):
        first, middle, last = (made[3 * b + e] for e in range(3))
        if q == 0:
            return first[:CELLS] + middle[ROWS:-ROWS] + last[ROWS:-ROWS]
        return first[ROWS:-ROWS] + middle[ROWS:-ROWS] + last[2 * ROWS :]

    made = products(list(range(9)), 0)
    if multi:
        made_above = products([0, 1, 2], rows)
        made_below = products([6, 7, 8], 2 * rows)
    wide = 2 * TILE_W
    for q in range(2):
        top, middle, bottom = (spread(made, b, q) for b in range(3))
        above, below = from_row_above(top), from_row_below(bottom)
        if multi:
            above = above + spread(made_above, 0, q)
            below = below + spread(made_below, 2, q)
        for p, value in enumerate((above + middle + bottom, top + middle + below)):
            value = value + bias_ref[...]
            for j in range(TILE_W):
                grid[pl.ds(p * wide + 2 * j + q, ROWS, stride=2 * wide), :] = value[
                    j * ROWS : (j + 1) * ROWS
                ]
    out_ref[...] = grid[...].astype(BF16)


def place_kernel(put_ref, *refs):
    returned, out_ref = refs[:-1], refs[-1]
    values = [r[...] for r in returned]
    values = jnp.concatenate(values, axis=0) if len(values) > 1 else values[0]
    placed = jnp.dot(put_ref[...], values, preferred_element_type=F32)
    out_ref[...] = placed.astype(BF16)


def cell_of(place):
    return place % ROWS // TILE_H * (TILE_H * TILE_W) + place % TILE_H * TILE_W + place // ROWS


def sources_of(source_ref, tile):
    square = (CELLS, CELLS)
    left = lax.broadcasted_iota(jnp.int32, square, 0)
    right = lax.broadcasted_iota(jnp.int32, square, 1)
    line = source_ref[pl.ds(tile, 1), :]
    column = jnp.sum(jnp.where(cell_of(left) == right, line, 0), axis=1, keepdims=True)
    return column, jnp.sum(jnp.where(left == right, column, 0), axis=0, keepdims=True)


def one_hot(match):
    return match.astype(F32).astype(BF16)


def first_places(source, own, capacity, sender):
    members = source.shape[0]
    first = jnp.where(source // own == lax.axis_index("tile"), source % own, -capacity)
    first = jnp.max(first, axis=1, keepdims=True) // capacity * capacity
    wide = (members, members * capacity)
    spot = lax.broadcasted_iota(jnp.int32, wide, 1)
    match = sender(spot // capacity) == row_index(wide)
    return jnp.sum(jnp.where(match, first + spot % capacity, 0), axis=0, keepdims=True)


def load_all(ins, outs, sems):
    copies = [
        pltpu.make_async_copy(hbm, vmem, sems.at[k]) for k, (hbm, vmem) in enumerate(zip(ins, outs))
    ]
    for copy in copies:
        copy.start()
    return copies


def tile_prep_kernel(across, neighbours, own, capacity, *refs):
    ins, (take_ref, pack_ref, put_ref, grid_ref, *outs) = refs[:6], refs[6:-3]
    source_ref, space, sems = refs[-3:]
    copies = load_all(ins, [source_ref, space] + outs, sems)
    for copy in copies:
        copy.wait()
    tile = lax.axis_index("tile")
    members = source_ref.shape[0]
    place = lax.broadcasted_iota(jnp.int32, (CELLS, members * own), 1)
    for i, (dr, dc) in enumerate(neighbours):
        other = jnp.clip(tile + dr * across + dc, 0, members - 1)
        column, row = sources_of(source_ref, other)
        if (dr, dc) == (0, 0):
            slot = row // own * capacity + row % capacity
            pack_ref[...] = one_hot(row_index(pack_ref.shape) == slot)
        take_ref[i * CELLS : (i + 1) * CELLS] = one_hot(place == column)
    spots = first_places(source_ref[...], own, capacity, lambda sender: sender)
    put_ref[...] = one_hot(row_index(put_ref.shape) == spots)
    grid_ref[...] = space[...].astype(F32)


def pair_prep_kernel(own, capacity, *refs):
    ins, (take_ref, pack_ref, put_ref, *outs) = refs[:5], refs[5:-2]
    source_ref, sems = refs[-2:]
    copies = load_all(ins, [source_ref] + outs, sems)
    copies[0].wait()
    tile = lax.axis_index("tile")
    z, x = tile // 2, tile % 2
    members = source_ref.shape[0]
    place = lax.broadcasted_iota(jnp.int32, (CELLS, members * own), 1)
    outer = jnp.clip(tile + 2 * x - 1, 0, members - 1)
    for i, other in enumerate((2 * z, 2 * z + 1, outer)):
        column, row = sources_of(source_ref, other)
        take_ref[i * CELLS : (i + 1) * CELLS] = one_hot(place == column ^ (2 * z * own))
        if i < 2:
            owner = row // own
            slot = (owner // 2 ^ z) * (2 * capacity) + i * capacity + row % capacity
            slot = jnp.where(owner % 2 == x, slot, -1)
            shape = (pack_ref.shape[0], CELLS)
            pack_ref[:, i * CELLS : (i + 1) * CELLS] = one_hot(row_index(shape) == slot)
    spots = first_places(source_ref[...], own, capacity, lambda k: (k // 2 ^ z) * 2 + k % 2)
    put_ref[...] = one_hot(row_index(put_ref.shape) == spots)
    for copy in copies[1:]:
        copy.wait()


def pair_fold_kernel(*refs):
    taps_ref, pair_ref = refs[-2:]
    mine, theirs = refs[:2], refs[2:4]
    area = pair_ref.shape[0] // 2
    size = mine[0].shape[0]
    wide = 2 * TILE_W
    right = lax.axis_index("tile") % 2
    for at, (head, tail) in ((right, mine), (1 - right, theirs)):
        begin = pl.multiple_of(at * area, area)
        pair_ref[pl.ds(begin, size), :] = head[...].astype(F32)
        begin = pl.multiple_of(at * area + size, 16)
        pair_ref[pl.ds(begin, area - size), :] = tail[size - area :].astype(F32)
    zero = jnp.zeros((ROWS, pair_ref.shape[1]), F32)
    columns = folded_columns(pair_ref, wide, 2 * wide, lambda p: zero, lambda p: zero)
    for tap, value in enumerate(fold_taps(columns)):
        taps_ref[tap] = value


def swapped(block, axis, k):
    return lax.ppermute(block, axis, [(i, i ^ k) for i in range(lax.axis_size(axis))])


def shape(rows, lanes, kind=BF16):
    return jax.ShapeDtypeStruct((rows, lanes), kind)


def chan_swaps(blocks):
    return [swapped(block, "chan", k + 1) for k, block in enumerate(blocks)]


def pair_plan(tokens, cell_source, gain, shift, weight, bias, lines):
    own, lanes = tokens.shape
    members = lax.axis_size("tile")
    capacity = max(2, own // (members // 2))
    slots = members * capacity
    area = lines.shape[0]
    early, *parts = call(
        early_kernel,
        [shape(own + 2 * ROWS + area - SPLIT, lanes), shape(SPLIT, lanes)],
        [tokens, lines],
        [
            pltpu.VMEM((area, lanes), F32),
            pltpu.VMEM((area, lanes), BF16),
            pltpu.SemaphoreType.DMA((2,)),
        ],
        loose=(0, 1),
    )
    peer = swapped(early, "tile", 1)
    others = [swapped(part, "tile", 1) for part in parts]
    ins = [cell_source, weight] + [v.reshape(1, lanes) for v in (gain, shift, bias)]
    take, pack, put, weight, gain, shift, bias = call(
        functools.partial(pair_prep_kernel, own, capacity),
        [
            shape(3 * CELLS, members * own),
            shape(slots, 2 * CELLS),
            shape(own, slots),
        ]
        + [jax.ShapeDtypeStruct(v.shape, v.dtype) for v in ins[1:]],
        ins,
        [pltpu.VMEM(cell_source.shape, jnp.int32), pltpu.SemaphoreType.DMA((len(ins),))],
        loose=range(5),
    )
    (block,) = call(join_kernel, [shape(2 * own + 4 * ROWS, lanes)], [early, peer, put])
    pieces = [block] + [swapped(block, "tile", k) for k in (2, 4, 6)]
    (taps,) = call(
        pair_fold_kernel,
        [jax.ShapeDtypeStruct((9, 2 * CELLS, lanes), F32)],
        parts + [early] + others + [peer],
        [pltpu.VMEM((2 * area, lanes), F32)],
    )
    cell = shape(2 * CELLS, lanes, F32)
    mine, *sends = call(
        pair_adjoint_kernel,
        [cell] + [shape(2 * CELLS, lanes)] * 3,
        [taps, weight] + pieces,
        [pltpu.VMEM((2 * CELLS, CHANNELS), F32), pltpu.VMEM((4 * ROWS, lanes), F32)],
        flops=4 * 27 * CELLS * lanes * CHANNELS,
    )
    sends = chan_swaps(sends)
    hat, slope, scale, cells = call(
        pair_norm_kernel,
        [cell, cell, shape(2, lanes, F32), shape(CELLS + 2 * ROWS, lanes)],
        pieces + [take, gain, shift],
        flops=6 * CELLS * members * own * lanes,
    )
    received = chan_swaps([cells] * 3)
    routed = call(
        back_kernel,
        [shape(2 * capacity, lanes)] * 4,
        [mine, hat, slope, scale, pack] + sends,
    )
    returned = [routed[0]] + [swapped(r, "tile", 2 * k + 2) for k, r in enumerate(routed[1:])]
    return cells, received, weight, bias, put, returned


def tile_plan(tokens, cell_source, gain, shift, weight, bias, lines):
    own, lanes = tokens.shape
    members = lax.axis_size("tile")
    across = across_tiles()
    multi = members > across
    capacity = max(2, own // (members // 2))
    slots = members * capacity
    high, wide = 2 * TILE_H, 2 * TILE_W
    area = lines.shape[0]
    neighbours = [(0, -1), (0, 0), (0, 1)]
    if multi:
        neighbours = [(r, c) for r in (-1, 0, 1) for c in (-1, 0, 1)]
    gathered = lax.all_gather(tokens, "tile", axis=0, tiled=True)
    others = [along_row(lines[wide - 1 :: wide], 1), along_row(lines[::wide], -1)]
    if multi:
        side = (FRAMES, high, 1, lanes)
        widened = [others[0].reshape(side), lines.reshape(FRAMES, high, wide, lanes)]
        widened = jnp.concatenate(widened + [others[1].reshape(side)], axis=2)
        for edge, step, line in ((widened[:, -1], 1, 0), (widened[:, 0], -1, TILE_H - 1)):
            rim = along_column(edge, step).transpose(1, 0, 2)
            spaced = jnp.zeros((wide + 2, FRAMES, TILE_H, lanes), BF16).at[:, :, line].set(rim)
            others.append(spaced.reshape(wide + 2, ROWS, lanes))
    ins = [cell_source, lines, weight] + [v.reshape(1, lanes) for v in (gain, shift, bias)]
    take, pack, put, grid, weight, gain, shift, bias = call(
        functools.partial(tile_prep_kernel, across, neighbours, own, capacity),
        [
            shape(len(neighbours) * CELLS, members * own),
            shape(slots, CELLS),
            shape(own, slots),
            shape(area, lanes, F32),
        ]
        + [jax.ShapeDtypeStruct(v.shape, v.dtype) for v in ins[2:]],
        ins,
        [
            pltpu.VMEM(cell_source.shape, jnp.int32),
            pltpu.VMEM(lines.shape, BF16),
            pltpu.SemaphoreType.DMA((len(ins),)),
        ],
        loose=range(len(ins)),
    )
    cell = shape(CELLS, lanes, F32)
    mine, *sends = call(
        tile_adjoint_kernel,
        [cell] + [shape(CELLS, lanes)] * 3,
        [grid, weight] + others,
        [pltpu.VMEM((CELLS, CHANNELS), F32), pltpu.VMEM((4 * ROWS, lanes), F32)],
        flops=2 * 27 * CELLS * lanes * CHANNELS,
    )
    sends = chan_swaps(sends)
    size = (CELLS + 2 * ROWS) * (3 if multi else 1)
    hat, slope, scale, cells = call(
        functools.partial(tile_norm_kernel, members, across, neighbours),
        [cell, cell, shape(1, lanes, F32), shape(size, lanes)],
        [gathered, take, gain, shift],
        flops=2 * len(neighbours) * CELLS * members * own * lanes,
    )
    received = chan_swaps([cells] * 3)
    (packed,) = call(back_kernel, [shape(slots, lanes)], [mine, hat, slope, scale, pack] + sends)
    returned = lax.all_to_all(packed, "tile", split_axis=0, concat_axis=0, tiled=True)
    return cells, received, weight, bias, put, [returned]


def local(tokens, cell_source, gain, shift, weight, bias, cotangent):
    own, lanes = tokens.shape
    lines = cotangent.reshape(-1, lanes)
    members = lax.axis_size("tile")
    plan = pair_plan if members == 8 else tile_plan
    cells, received, weight, bias, put, returned = plan(
        tokens, cell_source, gain, shift, weight, bias, lines
    )
    (decoded,) = call(
        functools.partial(conv_kernel, members > across_tiles()),
        [shape(lines.shape[0], lanes)],
        [cells] + received + [weight, bias],
        [pltpu.VMEM(lines.shape, F32)],
        flops=2 * 27 * (CELLS + 2 * ROWS) * lanes * CHANNELS,
    )
    (token_grad,) = call(place_kernel, [shape(own, lanes)], [put] + returned)
    return decoded.reshape(cotangent.shape), token_grad


def solution(mesh):
    in_specs = (
        P("tile", "chan"),
        P(),
        P("chan"),
        P("chan"),
        P(None, None, "chan"),
        P("chan"),
        P("tile", None, None, None, "chan"),
    )
    out_specs = (P("tile", None, None, None, "chan"), P("tile", "chan"))
    return jax.shard_map(local, mesh=mesh, in_specs=in_specs, out_specs=out_specs, check_vma=False)
```

```python
import functools

import jax
import jax.numpy as jnp
from jax import lax
from jax.experimental import pallas as pl
from jax.experimental.pallas import tpu as pltpu
from jax.sharding import PartitionSpec as P

CHANNELS = 512
GROUP = 16
FRAMES = 2
TILE_H = 4
TILE_W = 8
CELLS = FRAMES * TILE_H * TILE_W
ROWS = FRAMES * TILE_H
EPS = 1e-06
VMEM_LIMIT = 12 * 2**20
SPLIT = 240
F32 = jnp.float32
BF16 = jnp.bfloat16
VMEM = pl.BlockSpec(memory_space=pltpu.VMEM)
FAR = pl.BlockSpec(memory_space=pltpu.HBM)
HIGHEST = lax.Precision.HIGHEST


def call(kernel, outs, args, scratch=(), flops=0, loose=()):
    args = [
        pltpu.with_memory_space_constraint(a, pltpu.HBM) if i in loose else a
        for i, a in enumerate(args)
    ]
    moved = sum(a.size * a.dtype.itemsize for a in args)
    moved += sum(o.size * o.dtype.itemsize for o in outs)
    return pl.pallas_call(
        kernel,
        out_shape=outs,
        in_specs=[FAR if i in loose else VMEM for i in range(len(args))],
        out_specs=[VMEM] * len(outs),
        scratch_shapes=list(scratch),
        compiler_params=pltpu.CompilerParams(vmem_limit_bytes=VMEM_LIMIT),
        cost_estimate=pl.CostEstimate(flops=flops, bytes_accessed=moved, transcendentals=0),
    )(*args)


def across_tiles():
    return min(lax.axis_size("tile"), 16)


def along_row(block, step):
    count, across = lax.axis_size("tile"), across_tiles()
    route = [(i, i + step) for i in range(count) if 0 <= i % across + step < across]
    return lax.ppermute(block, "tile", route)


def along_column(block, step):
    count, across = lax.axis_size("tile"), across_tiles()
    route = [(i, i + step * across) for i in range(count) if 0 <= i + step * across < count]
    return lax.ppermute(block, "tile", route)


def row_index(shape):
    return lax.broadcasted_iota(jnp.int32, shape, 0)


def from_row_above(x):
    keep = row_index(x.shape) % TILE_H != 0
    return jnp.where(keep, pltpu.roll(x, 1, 0), 0.0)


def from_row_below(x):
    keep = row_index(x.shape) % TILE_H != TILE_H - 1
    return jnp.where(keep, pltpu.roll(x, x.shape[0] - 1, 0), 0.0)


def folded_columns(grid, cut, wide, left=None, right=None):
    def column(p, x):
        if x < 0:
            return left(p)
        if x >= wide:
            return right(p)
        return grid[pl.ds(x // cut * (FRAMES * 2 * TILE_H * cut) + p * cut + x % cut, ROWS, stride=2 * cut), :]

    return [[column(p, x) for x in range(-1, wide + 1)] for p in range(2)]


def fold(parts, e):
    pairs = [parts[2 * s + 2 - e] + parts[2 * s + 3 - e] for s in range(len(parts) // 2 - 1)]
    return jnp.concatenate(pairs, axis=0)


def fold_taps(columns, rims=()):
    taps = [None] * 9
    for e in range(3):
        even, odd = fold(columns[0], e), fold(columns[1], e)
        below, above = from_row_below(even), from_row_above(odd)
        if rims:
            high = [rims[0][x].astype(F32) for x in range(len(columns[0]))]
            low = [rims[1][x].astype(F32) for x in range(len(columns[0]))]
            below, above = below + fold(low, e), above + fold(high, e)
        taps[e], taps[3 + e], taps[6 + e] = odd + below, even + odd, above + even
    return taps


def adjoint(taps, w_ref):
    rows = taps[0].shape[0]
    total = jnp.zeros((rows, CHANNELS), F32)
    first = row_index(taps[0].shape) % ROWS < TILE_H
    latest = []
    for tap, value in enumerate(taps):
        both = value + pltpu.roll(value, rows - TILE_H, 0)
        both = jnp.where(first, both, 0.0).astype(BF16)
        latest.append((value.astype(BF16), tap + 18))
        total = total + contract(both, tap, both, tap + 9, w_ref)
        if len(latest) == 2:
            (x, i), (y, j) = latest
            total = total + contract(x, i, y, j, w_ref)
            latest = []
    for x, i in latest:
        total = total + lax.dot_general(
            x, w_ref[i], (((1,), (1,)), ((), ())), preferred_element_type=F32
        )
    return total


def share(partial_ref, outs):
    lanes = outs[0].shape[1]
    chan = lax.axis_index("chan")
    for k, out in enumerate(outs):
        begin = pl.multiple_of((chan ^ k) * lanes, 128)
        out[...] = partial_ref[:, pl.ds(begin, lanes)].astype(out.dtype)


def contract(x, i, y, j, w_ref):
    left = jnp.concatenate([x, y], axis=1)
    right = jnp.concatenate([w_ref[i], w_ref[j]], axis=1)
    return lax.dot_general(left, right, (((1,), (1,)), ((), ())), preferred_element_type=F32)


def group_mean(sums):
    lanes = sums.shape[1]
    left = lax.broadcasted_iota(jnp.int32, (lanes, lanes), 0) // GROUP
    right = lax.broadcasted_iota(jnp.int32, (lanes, lanes), 1) // GROUP
    same = (left == right).astype(F32)
    whole = jnp.dot(sums, same, preferred_element_type=F32, precision=HIGHEST)
    return whole * (1.0 / (CELLS * GROUP))


def column_sums(x):
    return jnp.sum(x, axis=0, keepdims=True)


def silu_parts(hat, gain, shift):
    value = hat * gain + shift
    gate = 1.0 / (1.0 + jnp.exp(-value))
    return value * gate, gate * (1.0 + value * (1.0 - gate)) * gain


def standardized(features):
    means = group_mean(stacked([column_sums(f) for f in features]))
    centred = [f - means[i : i + 1] for i, f in enumerate(features)]
    spreads = group_mean(stacked([column_sums(c * c) for c in centred]))
    scales = lax.rsqrt(spreads + EPS)
    return [c * scales[i : i + 1] for i, c in enumerate(centred)], scales


def tile_adjoint_kernel(grid_ref, w_ref, left_ref, right_ref, *refs):
    rims, outs, (partial_ref, sides) = refs[:-6], refs[-6:-2], refs[-2:]
    wide = 2 * TILE_W
    sides[: 2 * ROWS] = left_ref[...].astype(F32)
    sides[2 * ROWS :] = right_ref[...].astype(F32)
    columns = folded_columns(
        grid_ref,
        wide,
        wide,
        lambda p: sides[pl.ds(p, ROWS, stride=2), :],
        lambda p: sides[pl.ds(2 * ROWS + p, ROWS, stride=2), :],
    )
    partial_ref[...] = adjoint(fold_taps(columns, rims), w_ref)
    share(partial_ref, outs)


def tile_norm_kernel(members, across, neighbours, *refs):
    tokens_ref, take_ref, gain_ref, shift_ref = refs[:4]
    hat_ref, slope_ref, scale_ref, own_ref = refs[4:]
    tile = lax.axis_index("tile")
    tokens = tokens_ref[...]
    lanes = tokens.shape[1]
    gain, shift = gain_ref[...], shift_ref[...]
    there = []
    for dr, dc in neighbours:
        col, row = tile % across + dc, tile // across + dr
        there.append((col >= 0) & (col < across) & (row >= 0) & (row < members // across))
    chosen = take_ref[...]
    features = jnp.dot(chosen, tokens, preferred_element_type=F32)
    features = [features[i * CELLS : (i + 1) * CELLS] for i in range(len(neighbours))]
    hats, scales = standardized(features)
    blocks = {}
    for i, (dr, dc) in enumerate(neighbours):
        hat = hats[i][-ROWS:] if dc == -1 else hats[i][:ROWS] if dc == 1 else hats[i]
        active, slope = silu_parts(hat, gain, shift)
        if (dr, dc) == (0, 0):
            hat_ref[...] = hat
            slope_ref[...] = slope
            scale_ref[...] = scales[i : i + 1]
        else:
            active = jnp.where(there[i], active, 0.0)
        blocks[dr, dc] = active
    parts = [blocks[0, dc] for dc in (-1, 0, 1)]
    if len(neighbours) == 9:
        rows = CELLS + 2 * ROWS
        line = row_index((rows, lanes)) % TILE_H
        for dr, take, keep in ((-1, rows - TILE_H + 1, 0), (1, TILE_H - 1, TILE_H - 1)):
            block = jnp.concatenate([blocks[dr, dc] for dc in (-1, 0, 1)], axis=0)
            parts.append(jnp.where(line == keep, pltpu.roll(block, take, 0), 0.0))
    own_ref[...] = jnp.concatenate(parts, axis=0).astype(BF16)


def pair_adjoint_kernel(taps_ref, w_ref, *refs):
    pieces, outs, (partial_ref, sides) = refs[:4], refs[4:8], refs[8:]
    place = lax.axis_index("tile") // 2
    zero = jnp.zeros((2 * ROWS, taps_ref.shape[2]), BF16)
    left, right = zero, zero
    for k in range(1, 4):
        edges = pieces[k][-4 * ROWS :]
        left = jnp.where(place ^ k == place - 1, edges[2 * ROWS :], left)
        right = jnp.where(place ^ k == place + 1, edges[: 2 * ROWS], right)
    sides[: 2 * ROWS] = left.astype(F32)
    sides[2 * ROWS :] = right.astype(F32)
    rims = []
    for begin in (0, 2 * ROWS):
        even, odd = (sides[pl.ds(begin + p, ROWS, stride=2), :] for p in range(2))
        below, above = from_row_below(even), from_row_above(odd)
        rims.append((odd + below, even + odd, above + even))
    taps = []
    for tap in range(9):
        value, b, e = taps_ref[tap], tap // 3, tap % 3
        if e == 0:
            value = jnp.concatenate([value[:-ROWS], value[-ROWS:] + rims[1][b]], axis=0)
        if e == 2:
            value = jnp.concatenate([value[:ROWS] + rims[0][b], value[ROWS:]], axis=0)
        taps.append(value)
    partial_ref[...] = adjoint(taps, w_ref)
    share(partial_ref, outs)


def pair_norm_kernel(*refs):
    pieces, (take_ref, gain_ref, shift_ref) = refs[:4], refs[4:7]
    hat_ref, slope_ref, scale_ref, own_ref = refs[7:]
    tile = lax.axis_index("tile")
    odd = tile % 2 == 1
    tokens = jnp.concatenate([p[: -4 * ROWS] for p in pieces], axis=0)
    features = jnp.dot(take_ref[...], tokens, preferred_element_type=F32)
    hats, scales = standardized([features[i * CELLS : (i + 1) * CELLS] for i in range(3)])
    hat = jnp.concatenate(hats[:2], axis=0)
    active, slope = silu_parts(hat, gain_ref[...], shift_ref[...])
    hat_ref[...] = hat
    slope_ref[...] = slope
    scale_ref[...] = scales[:2]
    outer = jnp.where(odd, hats[2][:ROWS], hats[2][-ROWS:])
    outer, _ = silu_parts(outer, gain_ref[...], shift_ref[...])
    outer = jnp.where((tile == 0) | (tile == 7), 0.0, outer)
    own_ref[:ROWS] = jnp.where(odd, active[CELLS - ROWS : CELLS], outer).astype(BF16)
    own_ref[ROWS:-ROWS] = jnp.where(odd, active[CELLS:], active[:CELLS]).astype(BF16)
    own_ref[-ROWS:] = jnp.where(odd, outer, active[CELLS : CELLS + ROWS]).astype(BF16)


def stacked(rows):
    lanes = rows[0].shape[1]
    pad = -len(rows) % 8
    if pad:
        rows = rows + [jnp.zeros((pad, lanes), F32)]
    return jnp.concatenate(rows, axis=0)


def fetch(copies):
    for copy in copies:
        copy.start()
    for copy in copies:
        copy.wait()


def back_kernel(*refs):
    mine_ref, hat_ref, slope_ref, scale_ref, pack_ref = refs[:5]
    received, outs = refs[5:8], refs[8:]
    grad = mine_ref[...]
    for r in received:
        grad = grad + r[...].astype(F32)
    grad = grad * slope_ref[...]
    hat = hat_ref[...]
    tiles = grad.shape[0] // CELLS
    spans = [slice(i * CELLS, (i + 1) * CELLS) for i in range(tiles)]
    sums = [column_sums(grad[c]) for c in spans] + [column_sums(grad[c] * hat[c]) for c in spans]
    means = group_mean(stacked(sums))
    result = []
    for i, c in enumerate(spans):
        value = grad[c] - means[i : i + 1] - hat[c] * means[tiles + i : tiles + i + 1]
        result.append(scale_ref[i : i + 1] * value)
    result = (jnp.concatenate(result, axis=0) if tiles > 1 else result[0]).astype(BF16)
    packed = jnp.dot(pack_ref[...], result, preferred_element_type=F32).astype(BF16)
    step = packed.shape[0] // len(outs)
    for k, out in enumerate(outs):
        out[:step] = packed[k * step : (k + 1) * step]


def fetch(copies):
    for copy in copies:
        copy.start()
    for copy in copies:
        copy.wait()


def early_kernel(tokens_ref, lines_ref, out_ref, *refs):
    parts, (grid_ref, space, sems) = refs[:-3], refs[-3:]
    own = tokens_ref.shape[0]
    fetch(
        [
            pltpu.make_async_copy(tokens_ref, out_ref.at[pl.ds(0, own)], sems.at[0]),
            pltpu.make_async_copy(lines_ref, space, sems.at[1]),
        ]
    )
    size = parts[0].shape[0]
    parts[0][...] = space[:size]
    out_ref[own + 2 * ROWS :] = space[size:]
    grid_ref[...] = space[...].astype(F32)
    wide = 2 * TILE_W
    first = grid_ref[pl.ds(0, 2 * ROWS, stride=wide), :]
    last = grid_ref[pl.ds(wide - 1, 2 * ROWS, stride=wide), :]
    odd = lax.axis_index("tile") % 2 == 1
    out_ref[own : own + 2 * ROWS] = jnp.where(odd, last, first).astype(BF16)


def join_kernel(mine_ref, peer_ref, after_ref, out_ref):
    own = (out_ref.shape[0] - 4 * ROWS) // 2
    odd = lax.axis_index("tile") % 2 == 1
    mine, peer = mine_ref[...], peer_ref[...]
    even_one, odd_one = jnp.where(odd, peer, mine), jnp.where(odd, mine, peer)
    out_ref[:own] = even_one[:own]
    out_ref[own : 2 * own] = odd_one[:own]
    out_ref[2 * own : 2 * own + 2 * ROWS] = even_one[own : own + 2 * ROWS]
    out_ref[2 * own + 2 * ROWS :] = odd_one[own : own + 2 * ROWS]


def conv_kernel(multi, *refs):
    own_ref, *received, w_ref, bias_ref, out_ref, grid = refs
    chan = lax.axis_index("chan")
    rows = CELLS + 2 * ROWS
    lanes = own_ref.shape[1]
    grid_in = []
    received = [own_ref[...]] + [r[...] for r in received]
    for c in range(4):
        piece = received[3]
        for k in range(3):
            piece = jnp.where(chan ^ k == c, received[k], piece)
        grid_in.append(piece)
    cells = jnp.concatenate(grid_in, axis=1).astype(F32)
    line = row_index(cells.shape) % ROWS < TILE_H
    early = jnp.where(line, cells, pltpu.roll(cells, TILE_H, 0)).astype(BF16)
    cells = cells.astype(BF16)

    def products(taps, begin):
        x = cells[begin : begin + rows]
        y = early[begin : begin + rows]
        made = {}
        for at in range(0, len(taps), 2):
            pair = taps[at : at + 2]
            acc = None
            for a, left in ((0, y), (9, y), (18, x)):
                right = jnp.concatenate([w_ref[a + t] for t in pair], axis=1)
                term = jnp.dot(left, right, preferred_element_type=F32)
                acc = term if acc is None else acc + term
            for n, t in enumerate(pair):
                made[t] = acc[:, n * lanes : (n + 1) * lanes]
        return made

    def spread(made, b, q):
        first, middle, last = (made[3 * b + e] for e in range(3))
        if q == 0:
            return first[:CELLS] + middle[ROWS:-ROWS] + last[ROWS:-ROWS]
        return first[ROWS:-ROWS] + middle[ROWS:-ROWS] + last[2 * ROWS :]

    made = products(list(range(9)), 0)
    if multi:
        made_above = products([0, 1, 2], rows)
        made_below = products([6, 7, 8], 2 * rows)
    wide = 2 * TILE_W
    for q in range(2):
        top, middle, bottom = (spread(made, b, q) for b in range(3))
        above, below = from_row_above(top), from_row_below(bottom)
        if multi:
            above = above + spread(made_above, 0, q)
            below = below + spread(made_below, 2, q)
        for p, value in enumerate((above + middle + bottom, top + middle + below)):
            value = value + bias_ref[...]
            for j in range(TILE_W):
                grid[pl.ds(p * wide + 2 * j + q, ROWS, stride=2 * wide), :] = value[
                    j * ROWS : (j + 1) * ROWS
                ]
    out_ref[...] = grid[...].astype(BF16)


def place_kernel(put_ref, *refs):
    returned, out_ref = refs[:-1], refs[-1]
    step = put_ref.shape[1] // len(returned)
    values = [r[:step] for r in returned]
    values = jnp.concatenate(values, axis=0) if len(values) > 1 else values[0]
    placed = jnp.dot(put_ref[...], values, preferred_element_type=F32)
    out_ref[...] = placed.astype(BF16)


def cell_of(place):
    return place % ROWS // TILE_H * (TILE_H * TILE_W) + place % TILE_H * TILE_W + place // ROWS


def sources_of(source_ref, tile):
    square = (CELLS, CELLS)
    left = lax.broadcasted_iota(jnp.int32, square, 0)
    right = lax.broadcasted_iota(jnp.int32, square, 1)
    line = source_ref[pl.ds(tile, 1), :]
    column = jnp.sum(jnp.where(cell_of(left) == right, line, 0), axis=1, keepdims=True)
    return column, jnp.sum(jnp.where(left == right, column, 0), axis=0, keepdims=True)


def one_hot(match):
    return match.astype(F32).astype(BF16)


def first_places(source, own, capacity, sender):
    members = source.shape[0]
    first = jnp.where(source // own == lax.axis_index("tile"), source % own, -capacity)
    first = jnp.max(first, axis=1, keepdims=True) // capacity * capacity
    wide = (members, members * capacity)
    spot = lax.broadcasted_iota(jnp.int32, wide, 1)
    match = sender(spot // capacity) == row_index(wide)
    return jnp.sum(jnp.where(match, first + spot % capacity, 0), axis=0, keepdims=True)


def load_all(ins, outs, sems):
    copies = [
        pltpu.make_async_copy(hbm, vmem, sems.at[k]) for k, (hbm, vmem) in enumerate(zip(ins, outs))
    ]
    for copy in copies:
        copy.start()
    return copies


def tile_prep_kernel(across, neighbours, own, capacity, *refs):
    ins, (take_ref, pack_ref, put_ref, grid_ref, *outs) = refs[:6], refs[6:-3]
    source_ref, space, sems = refs[-3:]
    copies = load_all(ins, [source_ref, space] + outs, sems)
    for copy in copies:
        copy.wait()
    tile = lax.axis_index("tile")
    members = source_ref.shape[0]
    place = lax.broadcasted_iota(jnp.int32, (CELLS, members * own), 1)
    for i, (dr, dc) in enumerate(neighbours):
        other = jnp.clip(tile + dr * across + dc, 0, members - 1)
        column, row = sources_of(source_ref, other)
        if (dr, dc) == (0, 0):
            slot = row // own * capacity + row % capacity
            pack_ref[...] = one_hot(row_index(pack_ref.shape) == slot)
        take_ref[i * CELLS : (i + 1) * CELLS] = one_hot(place == column)
    spots = first_places(source_ref[...], own, capacity, lambda sender: sender)
    put_ref[...] = one_hot(row_index(put_ref.shape) == spots)
    grid_ref[...] = space[...].astype(F32)


def pair_prep_kernel(own, capacity, *refs):
    ins, (take_ref, pack_ref, put_ref, *outs) = refs[:5], refs[5:-2]
    source_ref, sems = refs[-2:]
    copies = load_all(ins, [source_ref] + outs, sems)
    copies[0].wait()
    tile = lax.axis_index("tile")
    z, x = tile // 2, tile % 2
    members = source_ref.shape[0]
    place = lax.broadcasted_iota(jnp.int32, (CELLS, members * own), 1)
    outer = jnp.clip(tile + 2 * x - 1, 0, members - 1)
    for i, other in enumerate((2 * z, 2 * z + 1, outer)):
        column, row = sources_of(source_ref, other)
        take_ref[i * CELLS : (i + 1) * CELLS] = one_hot(place == column ^ (2 * z * own))
        if i < 2:
            owner = row // own
            slot = (owner // 2 ^ z) * (2 * capacity) + i * capacity + row % capacity
            slot = jnp.where(owner % 2 == x, slot, -1)
            shape = (pack_ref.shape[0], CELLS)
            pack_ref[:, i * CELLS : (i + 1) * CELLS] = one_hot(row_index(shape) == slot)
    spots = first_places(source_ref[...], own, capacity, lambda k: (k // 2 ^ z) * 2 + k % 2)
    put_ref[...] = one_hot(row_index(put_ref.shape) == spots)
    for copy in copies[1:]:
        copy.wait()


def pair_fold_kernel(*refs):
    taps_ref, pair_ref = refs[-2:]
    mine, theirs = refs[:2], refs[2:4]
    area = pair_ref.shape[0] // 2
    size = mine[0].shape[0]
    wide = 2 * TILE_W
    right = lax.axis_index("tile") % 2
    for at, (head, tail) in ((right, mine), (1 - right, theirs)):
        begin = pl.multiple_of(at * area, area)
        pair_ref[pl.ds(begin, size), :] = head[...].astype(F32)
        begin = pl.multiple_of(at * area + size, 16)
        pair_ref[pl.ds(begin, area - size), :] = tail[size - area :].astype(F32)
    zero = jnp.zeros((ROWS, pair_ref.shape[1]), F32)
    columns = folded_columns(pair_ref, wide, 2 * wide, lambda p: zero, lambda p: zero)
    for tap, value in enumerate(fold_taps(columns)):
        taps_ref[tap] = value


def swapped(block, axis, k):
    return lax.ppermute(block, axis, [(i, i ^ k) for i in range(lax.axis_size(axis))])


def shape(rows, lanes, kind=BF16):
    return jax.ShapeDtypeStruct((rows, lanes), kind)


def chan_swaps(blocks):
    return [swapped(block, "chan", k + 1) for k, block in enumerate(blocks)]


def pair_plan(tokens, cell_source, gain, shift, weight, bias, lines):
    own, lanes = tokens.shape
    members = lax.axis_size("tile")
    capacity = max(2, own // (members // 2))
    slots = members * capacity
    area = lines.shape[0]
    early, *parts = call(
        early_kernel,
        [shape(own + 2 * ROWS + area - SPLIT, lanes), shape(SPLIT, lanes)],
        [tokens, lines],
        [
            pltpu.VMEM((area, lanes), F32),
            pltpu.VMEM((area, lanes), BF16),
            pltpu.SemaphoreType.DMA((2,)),
        ],
        loose=(0, 1),
    )
    peer = swapped(early, "tile", 1)
    others = [swapped(part, "tile", 1) for part in parts]
    ins = [cell_source, weight] + [v.reshape(1, lanes) for v in (gain, shift, bias)]
    take, pack, put, weight, gain, shift, bias = call(
        functools.partial(pair_prep_kernel, own, capacity),
        [
            shape(3 * CELLS, members * own),
            shape(slots, 2 * CELLS),
            shape(own, slots),
        ]
        + [jax.ShapeDtypeStruct(v.shape, v.dtype) for v in ins[1:]],
        ins,
        [pltpu.VMEM(cell_source.shape, jnp.int32), pltpu.SemaphoreType.DMA((len(ins),))],
        loose=range(5),
    )
    (block,) = call(join_kernel, [shape(2 * own + 4 * ROWS, lanes)], [early, peer, put])
    pieces = [block] + [swapped(block, "tile", k) for k in (2, 4, 6)]
    (taps,) = call(
        pair_fold_kernel,
        [jax.ShapeDtypeStruct((9, 2 * CELLS, lanes), F32)],
        parts + [early] + others + [peer],
        [pltpu.VMEM((2 * area, lanes), F32)],
    )
    cell = shape(2 * CELLS, lanes, F32)
    mine, *sends = call(
        pair_adjoint_kernel,
        [cell] + [shape(2 * CELLS, lanes)] * 3,
        [taps, weight] + pieces,
        [pltpu.VMEM((2 * CELLS, CHANNELS), F32), pltpu.VMEM((4 * ROWS, lanes), F32)],
        flops=4 * 27 * CELLS * lanes * CHANNELS,
    )
    sends = chan_swaps(sends)
    hat, slope, scale, cells = call(
        pair_norm_kernel,
        [cell, cell, shape(2, lanes, F32), shape(CELLS + 2 * ROWS, lanes)],
        pieces + [take, gain, shift],
        flops=6 * CELLS * members * own * lanes,
    )
    received = chan_swaps([cells] * 3)
    routed = call(
        back_kernel,
        [shape(2 * capacity + more, lanes) for more in (0, 16, 32, 0)],
        [mine, hat, slope, scale, pack] + sends,
    )
    returned = [routed[0]] + [swapped(r, "tile", 2 * k + 2) for k, r in enumerate(routed[1:])]
    return cells, received, weight, bias, put, returned


def tile_plan(tokens, cell_source, gain, shift, weight, bias, lines):
    own, lanes = tokens.shape
    members = lax.axis_size("tile")
    across = across_tiles()
    multi = members > across
    capacity = max(2, own // (members // 2))
    slots = members * capacity
    high, wide = 2 * TILE_H, 2 * TILE_W
    area = lines.shape[0]
    neighbours = [(0, -1), (0, 0), (0, 1)]
    if multi:
        neighbours = [(r, c) for r in (-1, 0, 1) for c in (-1, 0, 1)]
    gathered = lax.all_gather(tokens, "tile", axis=0, tiled=True)
    others = [along_row(lines[wide - 1 :: wide], 1), along_row(lines[::wide], -1)]
    if multi:
        side = (FRAMES, high, 1, lanes)
        widened = [others[0].reshape(side), lines.reshape(FRAMES, high, wide, lanes)]
        widened = jnp.concatenate(widened + [others[1].reshape(side)], axis=2)
        for edge, step, line in ((widened[:, -1], 1, 0), (widened[:, 0], -1, TILE_H - 1)):
            rim = along_column(edge, step).transpose(1, 0, 2)
            spaced = jnp.zeros((wide + 2, FRAMES, TILE_H, lanes), BF16).at[:, :, line].set(rim)
            others.append(spaced.reshape(wide + 2, ROWS, lanes))
    ins = [cell_source, lines, weight] + [v.reshape(1, lanes) for v in (gain, shift, bias)]
    take, pack, put, grid, weight, gain, shift, bias = call(
        functools.partial(tile_prep_kernel, across, neighbours, own, capacity),
        [
            shape(len(neighbours) * CELLS, members * own),
            shape(slots, CELLS),
            shape(own, slots),
            shape(area, lanes, F32),
        ]
        + [jax.ShapeDtypeStruct(v.shape, v.dtype) for v in ins[2:]],
        ins,
        [
            pltpu.VMEM(cell_source.shape, jnp.int32),
            pltpu.VMEM(lines.shape, BF16),
            pltpu.SemaphoreType.DMA((len(ins),)),
        ],
        loose=range(len(ins)),
    )
    cell = shape(CELLS, lanes, F32)
    mine, *sends = call(
        tile_adjoint_kernel,
        [cell] + [shape(CELLS, lanes)] * 3,
        [grid, weight] + others,
        [pltpu.VMEM((CELLS, CHANNELS), F32), pltpu.VMEM((4 * ROWS, lanes), F32)],
        flops=2 * 27 * CELLS * lanes * CHANNELS,
    )
    sends = chan_swaps(sends)
    size = (CELLS + 2 * ROWS) * (3 if multi else 1)
    hat, slope, scale, cells = call(
        functools.partial(tile_norm_kernel, members, across, neighbours),
        [cell, cell, shape(1, lanes, F32), shape(size, lanes)],
        [gathered, take, gain, shift],
        flops=2 * len(neighbours) * CELLS * members * own * lanes,
    )
    received = chan_swaps([cells] * 3)
    (packed,) = call(back_kernel, [shape(slots, lanes)], [mine, hat, slope, scale, pack] + sends)
    returned = lax.all_to_all(packed, "tile", split_axis=0, concat_axis=0, tiled=True)
    return cells, received, weight, bias, put, [returned]


def local(tokens, cell_source, gain, shift, weight, bias, cotangent):
    own, lanes = tokens.shape
    lines = cotangent.reshape(-1, lanes)
    members = lax.axis_size("tile")
    plan = pair_plan if members == 8 else tile_plan
    cells, received, weight, bias, put, returned = plan(
        tokens, cell_source, gain, shift, weight, bias, lines
    )
    (decoded,) = call(
        functools.partial(conv_kernel, members > across_tiles()),
        [shape(lines.shape[0], lanes)],
        [cells] + received + [weight, bias],
        [pltpu.VMEM(lines.shape, F32)],
        flops=2 * 27 * (CELLS + 2 * ROWS) * lanes * CHANNELS,
    )
    (token_grad,) = call(place_kernel, [shape(own, lanes)], [put] + returned)
    return decoded.reshape(cotangent.shape), token_grad


def solution(mesh):
    in_specs = (
        P("tile", "chan"),
        P(),
        P("chan"),
        P("chan"),
        P(None, None, "chan"),
        P("chan"),
        P("tile", None, None, None, "chan"),
    )
    out_specs = (P("tile", None, None, None, "chan"), P("tile", "chan"))
    return jax.shard_map(local, mesh=mesh, in_specs=in_specs, out_specs=out_specs, check_vma=False)
```

```python
import functools

import jax
import jax.numpy as jnp
from jax import lax
from jax.experimental import pallas as pl
from jax.experimental.pallas import tpu as pltpu
from jax.sharding import PartitionSpec as P

CHANNELS = 512
GROUP = 16
FRAMES = 2
TILE_H = 4
TILE_W = 8
CELLS = FRAMES * TILE_H * TILE_W
ROWS = FRAMES * TILE_H
EPS = 1e-06
VMEM_LIMIT = 12 * 2**20
SPLIT = 240
F32 = jnp.float32
BF16 = jnp.bfloat16
VMEM = pl.BlockSpec(memory_space=pltpu.VMEM)
FAR = pl.BlockSpec(memory_space=pltpu.HBM)
HIGHEST = lax.Precision.HIGHEST


def call(kernel, outs, args, scratch=(), flops=0, loose=()):
    args = [
        pltpu.with_memory_space_constraint(a, pltpu.HBM) if i in loose else a
        for i, a in enumerate(args)
    ]
    moved = sum(a.size * a.dtype.itemsize for a in args)
    moved += sum(o.size * o.dtype.itemsize for o in outs)
    return pl.pallas_call(
        kernel,
        out_shape=outs,
        in_specs=[FAR if i in loose else VMEM for i in range(len(args))],
        out_specs=[VMEM] * len(outs),
        scratch_shapes=list(scratch),
        compiler_params=pltpu.CompilerParams(vmem_limit_bytes=VMEM_LIMIT),
        cost_estimate=pl.CostEstimate(flops=flops, bytes_accessed=moved, transcendentals=0),
    )(*args)


def across_tiles():
    return min(lax.axis_size("tile"), 16)


def along_row(block, step):
    count, across = lax.axis_size("tile"), across_tiles()
    route = [(i, i + step) for i in range(count) if 0 <= i % across + step < across]
    return lax.ppermute(block, "tile", route)


def along_column(block, step):
    count, across = lax.axis_size("tile"), across_tiles()
    route = [(i, i + step * across) for i in range(count) if 0 <= i + step * across < count]
    return lax.ppermute(block, "tile", route)


def row_index(shape):
    return lax.broadcasted_iota(jnp.int32, shape, 0)


def from_row_above(x):
    keep = row_index(x.shape) % TILE_H != 0
    return jnp.where(keep, pltpu.roll(x, 1, 0), 0.0)


def from_row_below(x):
    keep = row_index(x.shape) % TILE_H != TILE_H - 1
    return jnp.where(keep, pltpu.roll(x, x.shape[0] - 1, 0), 0.0)


def folded_columns(grid, cut, wide, left=None, right=None):
    def column(p, x):
        if x < 0:
            return left(p)
        if x >= wide:
            return right(p)
        return grid[pl.ds(x // cut * (FRAMES * 2 * TILE_H * cut) + p * cut + x % cut, ROWS, stride=2 * cut), :]

    return [[column(p, x) for x in range(-1, wide + 1)] for p in range(2)]


def fold(parts, e):
    pairs = [parts[2 * s + 2 - e] + parts[2 * s + 3 - e] for s in range(len(parts) // 2 - 1)]
    return jnp.concatenate(pairs, axis=0)


def fold_taps(columns, rims=()):
    taps = [None] * 9
    for e in range(3):
        even, odd = fold(columns[0], e), fold(columns[1], e)
        below, above = from_row_below(even), from_row_above(odd)
        if rims:
            high = [rims[0][x].astype(F32) for x in range(len(columns[0]))]
            low = [rims[1][x].astype(F32) for x in range(len(columns[0]))]
            below, above = below + fold(low, e), above + fold(high, e)
        taps[e], taps[3 + e], taps[6 + e] = odd + below, even + odd, above + even
    return taps


def operands(taps):
    rows = taps[0].shape[0]
    first = row_index(taps[0].shape) % ROWS < TILE_H
    both = [jnp.where(first, v + pltpu.roll(v, rows - TILE_H, 0), 0.0).astype(BF16) for v in taps]
    return both, [v.astype(BF16) for v in taps]


def adjoint(both, single, w_ref, begin, width):
    total = jnp.zeros((both[0].shape[0], width), F32)
    some = pl.ds(begin, width)
    pairs = [(both[t], t, both[t], t + 9) for t in range(9)]
    pairs += [(single[t], t + 18, single[t + 1], t + 19) for t in range(0, 8, 2)]
    for x, i, y, j in pairs:
        total = total + contract(x, i, y, j, w_ref, some)
    last = w_ref[26, some, :]
    return total + lax.dot_general(
        single[8], last, (((1,), (1,)), ((), ())), preferred_element_type=F32
    )


def share(partial_ref, outs):
    lanes = outs[0].shape[1]
    chan = lax.axis_index("chan")
    for k, out in enumerate(outs):
        begin = pl.multiple_of((chan ^ k) * lanes, 128)
        out[...] = partial_ref[:, pl.ds(begin, lanes)].astype(out.dtype)


def contract(x, i, y, j, w_ref, some):
    left = jnp.concatenate([x, y], axis=1)
    right = jnp.concatenate([w_ref[i, some, :], w_ref[j, some, :]], axis=1)
    return lax.dot_general(left, right, (((1,), (1,)), ((), ())), preferred_element_type=F32)


def group_mean(sums):
    lanes = sums.shape[1]
    left = lax.broadcasted_iota(jnp.int32, (lanes, lanes), 0) // GROUP
    right = lax.broadcasted_iota(jnp.int32, (lanes, lanes), 1) // GROUP
    same = (left == right).astype(F32)
    whole = jnp.dot(sums, same, preferred_element_type=F32, precision=HIGHEST)
    return whole * (1.0 / (CELLS * GROUP))


def column_sums(x):
    return jnp.sum(x, axis=0, keepdims=True)


def silu_parts(hat, gain, shift):
    value = hat * gain + shift
    gate = 1.0 / (1.0 + jnp.exp(-value))
    return value * gate, gate * (1.0 + value * (1.0 - gate)) * gain


def standardized(features):
    means = group_mean(stacked([column_sums(f) for f in features]))
    centred = [f - means[i : i + 1] for i, f in enumerate(features)]
    spreads = group_mean(stacked([column_sums(c * c) for c in centred]))
    scales = lax.rsqrt(spreads + EPS)
    return [c * scales[i : i + 1] for i, c in enumerate(centred)], scales


def tile_adjoint_kernel(grid_ref, w_ref, left_ref, right_ref, *refs):
    rims, outs, (partial_ref, sides) = refs[:-6], refs[-6:-2], refs[-2:]
    wide = 2 * TILE_W
    sides[: 2 * ROWS] = left_ref[...].astype(F32)
    sides[2 * ROWS :] = right_ref[...].astype(F32)
    columns = folded_columns(
        grid_ref,
        wide,
        wide,
        lambda p: sides[pl.ds(p, ROWS, stride=2), :],
        lambda p: sides[pl.ds(2 * ROWS + p, ROWS, stride=2), :],
    )
    partial_ref[...] = adjoint(*operands(fold_taps(columns, rims)), w_ref, 0, CHANNELS)
    share(partial_ref, outs)


def tile_norm_kernel(members, across, neighbours, *refs):
    tokens_ref, take_ref, gain_ref, shift_ref = refs[:4]
    hat_ref, slope_ref, scale_ref, own_ref = refs[4:]
    tile = lax.axis_index("tile")
    tokens = tokens_ref[...]
    lanes = tokens.shape[1]
    gain, shift = gain_ref[...], shift_ref[...]
    there = []
    for dr, dc in neighbours:
        col, row = tile % across + dc, tile // across + dr
        there.append((col >= 0) & (col < across) & (row >= 0) & (row < members // across))
    chosen = take_ref[...]
    features = jnp.dot(chosen, tokens, preferred_element_type=F32)
    features = [features[i * CELLS : (i + 1) * CELLS] for i in range(len(neighbours))]
    hats, scales = standardized(features)
    blocks = {}
    for i, (dr, dc) in enumerate(neighbours):
        hat = hats[i][-ROWS:] if dc == -1 else hats[i][:ROWS] if dc == 1 else hats[i]
        active, slope = silu_parts(hat, gain, shift)
        if (dr, dc) == (0, 0):
            hat_ref[...] = hat
            slope_ref[...] = slope
            scale_ref[...] = scales[i : i + 1]
        else:
            active = jnp.where(there[i], active, 0.0)
        blocks[dr, dc] = active
    parts = [blocks[0, dc] for dc in (-1, 0, 1)]
    if len(neighbours) == 9:
        rows = CELLS + 2 * ROWS
        line = row_index((rows, lanes)) % TILE_H
        for dr, take, keep in ((-1, rows - TILE_H + 1, 0), (1, TILE_H - 1, TILE_H - 1)):
            block = jnp.concatenate([blocks[dr, dc] for dc in (-1, 0, 1)], axis=0)
            parts.append(jnp.where(line == keep, pltpu.roll(block, take, 0), 0.0))
    own_ref[...] = jnp.concatenate(parts, axis=0).astype(BF16)


def half_adjoint(both, single, w_ref, half, partial_ref, outs):
    lanes = outs[0].shape[1]
    begin = pl.multiple_of(half * (2 * lanes), 256)
    partial_ref[...] = adjoint(both, single, w_ref, begin, 2 * lanes)
    like = lax.axis_index("chan") % 2
    for k, out in enumerate(outs):
        begin = pl.multiple_of((like ^ k) * lanes, 128)
        out[...] = partial_ref[:, pl.ds(begin, lanes)].astype(out.dtype)


def near_adjoint_kernel(left_ref, w_ref, mine_ref, send_ref, partial_ref):
    both, single = [[left_ref[i, t] for t in range(9)] for i in range(2)]
    half = lax.axis_index("chan") // 2
    half_adjoint(both, single, w_ref, half, partial_ref, [mine_ref, send_ref])


def far_adjoint_kernel(taps_ref, w_ref, *refs):
    pieces, outs, left_ref, (partial_ref, sides) = refs[:4], refs[4:6], refs[6], refs[7:]
    place = lax.axis_index("tile") // 2
    zero = jnp.zeros((2 * ROWS, taps_ref.shape[2]), BF16)
    left, right = zero, zero
    for k in range(1, 4):
        edges = pieces[k][-4 * ROWS :]
        left = jnp.where(place ^ k == place - 1, edges[2 * ROWS :], left)
        right = jnp.where(place ^ k == place + 1, edges[: 2 * ROWS], right)
    sides[: 2 * ROWS] = left.astype(F32)
    sides[2 * ROWS :] = right.astype(F32)
    rims = []
    for begin in (0, 2 * ROWS):
        even, odd = (sides[pl.ds(begin + p, ROWS, stride=2), :] for p in range(2))
        below, above = from_row_below(even), from_row_above(odd)
        rims.append((odd + below, even + odd, above + even))
    taps = []
    for tap in range(9):
        value, b, e = taps_ref[tap], tap // 3, tap % 3
        if e == 0:
            value = jnp.concatenate([value[:-ROWS], value[-ROWS:] + rims[1][b]], axis=0)
        if e == 2:
            value = jnp.concatenate([value[:ROWS] + rims[0][b], value[ROWS:]], axis=0)
        taps.append(value)
    both, single = operands(taps)
    for t in range(9):
        left_ref[0, t] = both[t]
        left_ref[1, t] = single[t]
    half_adjoint(both, single, w_ref, 1 - lax.axis_index("chan") // 2, partial_ref, outs)


def pair_norm_kernel(*refs):
    pieces, (take_ref, gain_ref, shift_ref) = refs[:4], refs[4:7]
    hat_ref, slope_ref, scale_ref, own_ref = refs[7:]
    tile = lax.axis_index("tile")
    odd = tile % 2 == 1
    tokens = jnp.concatenate([p[: -4 * ROWS] for p in pieces], axis=0)
    features = jnp.dot(take_ref[...], tokens, preferred_element_type=F32)
    hats, scales = standardized([features[i * CELLS : (i + 1) * CELLS] for i in range(3)])
    hat = jnp.concatenate(hats[:2], axis=0)
    active, slope = silu_parts(hat, gain_ref[...], shift_ref[...])
    hat_ref[...] = hat
    slope_ref[...] = slope
    scale_ref[...] = scales[:2]
    outer = jnp.where(odd, hats[2][:ROWS], hats[2][-ROWS:])
    outer, _ = silu_parts(outer, gain_ref[...], shift_ref[...])
    outer = jnp.where((tile == 0) | (tile == 7), 0.0, outer)
    own_ref[:ROWS] = jnp.where(odd, active[CELLS - ROWS : CELLS], outer).astype(BF16)
    own_ref[ROWS:-ROWS] = jnp.where(odd, active[CELLS:], active[:CELLS]).astype(BF16)
    own_ref[-ROWS:] = jnp.where(odd, outer, active[CELLS : CELLS + ROWS]).astype(BF16)


def stacked(rows):
    lanes = rows[0].shape[1]
    pad = -len(rows) % 8
    if pad:
        rows = rows + [jnp.zeros((pad, lanes), F32)]
    return jnp.concatenate(rows, axis=0)


def fetch(copies):
    for copy in copies:
        copy.start()
    for copy in copies:
        copy.wait()


def back_kernel(*refs):
    mine_ref, hat_ref, slope_ref, scale_ref, pack_ref = refs[:5]
    received, outs = refs[5:8], refs[8:]
    grad = mine_ref[...]
    for r in received:
        grad = grad + r[...].astype(F32)
    grad = grad * slope_ref[...]
    hat = hat_ref[...]
    tiles = grad.shape[0] // CELLS
    spans = [slice(i * CELLS, (i + 1) * CELLS) for i in range(tiles)]
    sums = [column_sums(grad[c]) for c in spans] + [column_sums(grad[c] * hat[c]) for c in spans]
    means = group_mean(stacked(sums))
    result = []
    for i, c in enumerate(spans):
        value = grad[c] - means[i : i + 1] - hat[c] * means[tiles + i : tiles + i + 1]
        result.append(scale_ref[i : i + 1] * value)
    result = (jnp.concatenate(result, axis=0) if tiles > 1 else result[0]).astype(BF16)
    packed = jnp.dot(pack_ref[...], result, preferred_element_type=F32).astype(BF16)
    step = packed.shape[0] // len(outs)
    for k, out in enumerate(outs):
        out[:step] = packed[k * step : (k + 1) * step]


def fetch(copies):
    for copy in copies:
        copy.start()
    for copy in copies:
        copy.wait()


def early_kernel(tokens_ref, lines_ref, out_ref, *refs):
    parts, (grid_ref, space, sems) = refs[:-3], refs[-3:]
    own = tokens_ref.shape[0]
    fetch(
        [
            pltpu.make_async_copy(tokens_ref, out_ref.at[pl.ds(0, own)], sems.at[0]),
            pltpu.make_async_copy(lines_ref, space, sems.at[1]),
        ]
    )
    size = parts[0].shape[0]
    parts[0][...] = space[:size]
    out_ref[own + 2 * ROWS :] = space[size:]
    grid_ref[...] = space[...].astype(F32)
    wide = 2 * TILE_W
    first = grid_ref[pl.ds(0, 2 * ROWS, stride=wide), :]
    last = grid_ref[pl.ds(wide - 1, 2 * ROWS, stride=wide), :]
    odd = lax.axis_index("tile") % 2 == 1
    out_ref[own : own + 2 * ROWS] = jnp.where(odd, last, first).astype(BF16)


def join_kernel(mine_ref, peer_ref, after_ref, out_ref):
    own = (out_ref.shape[0] - 4 * ROWS) // 2
    odd = lax.axis_index("tile") % 2 == 1
    mine, peer = mine_ref[...], peer_ref[...]
    even_one, odd_one = jnp.where(odd, peer, mine), jnp.where(odd, mine, peer)
    out_ref[:own] = even_one[:own]
    out_ref[own : 2 * own] = odd_one[:own]
    out_ref[2 * own : 2 * own + 2 * ROWS] = even_one[own : own + 2 * ROWS]
    out_ref[2 * own + 2 * ROWS :] = odd_one[own : own + 2 * ROWS]


def conv_kernel(multi, *refs):
    own_ref, *received, w_ref, bias_ref, out_ref, grid = refs
    chan = lax.axis_index("chan")
    rows = CELLS + 2 * ROWS
    lanes = own_ref.shape[1]
    grid_in = []
    received = [own_ref[...]] + [r[...] for r in received]
    for c in range(4):
        piece = received[3]
        for k in range(3):
            piece = jnp.where(chan ^ k == c, received[k], piece)
        grid_in.append(piece)
    cells = jnp.concatenate(grid_in, axis=1).astype(F32)
    line = row_index(cells.shape) % ROWS < TILE_H
    early = jnp.where(line, cells, pltpu.roll(cells, TILE_H, 0)).astype(BF16)
    cells = cells.astype(BF16)

    def products(taps, begin):
        x = cells[begin : begin + rows]
        y = early[begin : begin + rows]
        made = {}
        for at in range(0, len(taps), 2):
            pair = taps[at : at + 2]
            acc = None
            for a, left in ((0, y), (9, y), (18, x)):
                right = jnp.concatenate([w_ref[a + t] for t in pair], axis=1)
                term = jnp.dot(left, right, preferred_element_type=F32)
                acc = term if acc is None else acc + term
            for n, t in enumerate(pair):
                made[t] = acc[:, n * lanes : (n + 1) * lanes]
        return made

    def spread(made, b, q):
        first, middle, last = (made[3 * b + e] for e in range(3))
        if q == 0:
            return first[:CELLS] + middle[ROWS:-ROWS] + last[ROWS:-ROWS]
        return first[ROWS:-ROWS] + middle[ROWS:-ROWS] + last[2 * ROWS :]

    made = products(list(range(9)), 0)
    if multi:
        made_above = products([0, 1, 2], rows)
        made_below = products([6, 7, 8], 2 * rows)
    wide = 2 * TILE_W
    for q in range(2):
        top, middle, bottom = (spread(made, b, q) for b in range(3))
        above, below = from_row_above(top), from_row_below(bottom)
        if multi:
            above = above + spread(made_above, 0, q)
            below = below + spread(made_below, 2, q)
        for p, value in enumerate((above + middle + bottom, top + middle + below)):
            value = value + bias_ref[...]
            for j in range(TILE_W):
                grid[pl.ds(p * wide + 2 * j + q, ROWS, stride=2 * wide), :] = value[
                    j * ROWS : (j + 1) * ROWS
                ]
    out_ref[...] = grid[...].astype(BF16)


def place_kernel(put_ref, *refs):
    returned, out_ref = refs[:-1], refs[-1]
    step = put_ref.shape[1] // len(returned)
    values = [r[:step] for r in returned]
    values = jnp.concatenate(values, axis=0) if len(values) > 1 else values[0]
    placed = jnp.dot(put_ref[...], values, preferred_element_type=F32)
    out_ref[...] = placed.astype(BF16)


def cell_of(place):
    return place % ROWS // TILE_H * (TILE_H * TILE_W) + place % TILE_H * TILE_W + place // ROWS


def sources_of(source_ref, tile):
    square = (CELLS, CELLS)
    left = lax.broadcasted_iota(jnp.int32, square, 0)
    right = lax.broadcasted_iota(jnp.int32, square, 1)
    line = source_ref[pl.ds(tile, 1), :]
    column = jnp.sum(jnp.where(cell_of(left) == right, line, 0), axis=1, keepdims=True)
    return column, jnp.sum(jnp.where(left == right, column, 0), axis=0, keepdims=True)


def one_hot(match):
    return match.astype(F32).astype(BF16)


def first_places(source, own, capacity, sender):
    members = source.shape[0]
    first = jnp.where(source // own == lax.axis_index("tile"), source % own, -capacity)
    first = jnp.max(first, axis=1, keepdims=True) // capacity * capacity
    wide = (members, members * capacity)
    spot = lax.broadcasted_iota(jnp.int32, wide, 1)
    match = sender(spot // capacity) == row_index(wide)
    return jnp.sum(jnp.where(match, first + spot % capacity, 0), axis=0, keepdims=True)


def load_all(ins, outs, sems):
    copies = [
        pltpu.make_async_copy(hbm, vmem, sems.at[k]) for k, (hbm, vmem) in enumerate(zip(ins, outs))
    ]
    for copy in copies:
        copy.start()
    return copies


def tile_prep_kernel(across, neighbours, own, capacity, *refs):
    ins, (take_ref, pack_ref, put_ref, grid_ref, *outs) = refs[:6], refs[6:-3]
    source_ref, space, sems = refs[-3:]
    copies = load_all(ins, [source_ref, space] + outs, sems)
    for copy in copies:
        copy.wait()
    tile = lax.axis_index("tile")
    members = source_ref.shape[0]
    place = lax.broadcasted_iota(jnp.int32, (CELLS, members * own), 1)
    for i, (dr, dc) in enumerate(neighbours):
        other = jnp.clip(tile + dr * across + dc, 0, members - 1)
        column, row = sources_of(source_ref, other)
        if (dr, dc) == (0, 0):
            slot = row // own * capacity + row % capacity
            pack_ref[...] = one_hot(row_index(pack_ref.shape) == slot)
        take_ref[i * CELLS : (i + 1) * CELLS] = one_hot(place == column)
    spots = first_places(source_ref[...], own, capacity, lambda sender: sender)
    put_ref[...] = one_hot(row_index(put_ref.shape) == spots)
    grid_ref[...] = space[...].astype(F32)


def pair_prep_kernel(own, capacity, *refs):
    lines_ref, refs = refs[0], refs[1:]
    ins, (take_ref, pack_ref, put_ref, after_ref, *outs) = refs[:4], refs[4:-2]
    after_ref[...] = lines_ref[...]
    source_ref, sems = refs[-2:]
    copies = load_all(ins, [source_ref] + outs, sems)
    copies[0].wait()
    tile = lax.axis_index("tile")
    z, x = tile // 2, tile % 2
    members = source_ref.shape[0]
    place = lax.broadcasted_iota(jnp.int32, (CELLS, members * own), 1)
    outer = jnp.clip(tile + 2 * x - 1, 0, members - 1)
    for i, other in enumerate((2 * z, 2 * z + 1, outer)):
        column, row = sources_of(source_ref, other)
        take_ref[i * CELLS : (i + 1) * CELLS] = one_hot(place == column ^ (2 * z * own))
        if i < 2:
            owner = row // own
            slot = (owner // 2 ^ z) * (2 * capacity) + i * capacity + row % capacity
            slot = jnp.where(owner % 2 == x, slot, -1)
            shape = (pack_ref.shape[0], CELLS)
            pack_ref[:, i * CELLS : (i + 1) * CELLS] = one_hot(row_index(shape) == slot)
    spots = first_places(source_ref[...], own, capacity, lambda k: (k // 2 ^ z) * 2 + k % 2)
    put_ref[...] = one_hot(row_index(put_ref.shape) == spots)
    for copy in copies[1:]:
        copy.wait()


def weight_copies(weight_ref, w_ref, sems):
    return [
        pltpu.make_async_copy(weight_ref.at[pl.ds(3 * k, 3)], w_ref.at[pl.ds(3 * k, 3)], sems.at[k])
        for k in range(9)
    ]


def pair_fold_kernel(*refs):
    weight_ref, taps_ref, w_ref, pair_ref, sems = refs[4:]
    weights = weight_copies(weight_ref, w_ref, sems)
    for copy in weights:
        copy.start()
    mine, theirs = refs[:2], refs[2:4]
    area = pair_ref.shape[0] // 2
    size = mine[0].shape[0]
    wide = 2 * TILE_W
    right = lax.axis_index("tile") % 2
    for at, (head, tail) in ((right, mine), (1 - right, theirs)):
        begin = pl.multiple_of(at * area, area)
        pair_ref[pl.ds(begin, size), :] = head[...].astype(F32)
        begin = pl.multiple_of(at * area + size, 16)
        pair_ref[pl.ds(begin, area - size), :] = tail[size - area :].astype(F32)
    zero = jnp.zeros((ROWS, pair_ref.shape[1]), F32)
    columns = folded_columns(pair_ref, wide, 2 * wide, lambda p: zero, lambda p: zero)
    for tap, value in enumerate(fold_taps(columns)):
        taps_ref[tap] = value
    for copy in weights:
        copy.wait()


def swapped(block, axis, k):
    return lax.ppermute(block, axis, [(i, i ^ k) for i in range(lax.axis_size(axis))])


def shape(rows, lanes, kind=BF16):
    return jax.ShapeDtypeStruct((rows, lanes), kind)


def chan_swaps(blocks):
    return [swapped(block, "chan", k + 1) for k, block in enumerate(blocks)]


def pair_plan(tokens, cell_source, gain, shift, weight, bias, lines):
    own, lanes = tokens.shape
    members = lax.axis_size("tile")
    capacity = max(2, own // (members // 2))
    slots = members * capacity
    area = lines.shape[0]
    early, *parts = call(
        early_kernel,
        [shape(own + 2 * ROWS + area - SPLIT, lanes), shape(SPLIT, lanes)],
        [tokens, lines],
        [
            pltpu.VMEM((area, lanes), F32),
            pltpu.VMEM((area, lanes), BF16),
            pltpu.SemaphoreType.DMA((2,)),
        ],
        loose=(0, 1),
    )
    peer = swapped(early, "tile", 1)
    ins = [cell_source] + [v.reshape(1, lanes) for v in (gain, shift, bias)]
    take, pack, put, parts[0], gain, shift, bias = call(
        functools.partial(pair_prep_kernel, own, capacity),
        [
            shape(3 * CELLS, members * own),
            shape(slots, 2 * CELLS),
            shape(own, slots),
            shape(SPLIT, lanes),
        ]
        + [jax.ShapeDtypeStruct(v.shape, v.dtype) for v in ins[1:]],
        parts[:1] + ins,
        [pltpu.VMEM(cell_source.shape, jnp.int32), pltpu.SemaphoreType.DMA((len(ins),))],
        loose=range(1, 5),
    )
    others = [swapped(part, "tile", 1) for part in parts]
    (block,) = call(join_kernel, [shape(2 * own + 4 * ROWS, lanes)], [early, peer, put])
    pieces = [block] + [swapped(block, "tile", k) for k in (2, 4, 6)]
    taps, weight = call(
        pair_fold_kernel,
        [
            jax.ShapeDtypeStruct((9, 2 * CELLS, lanes), F32),
            jax.ShapeDtypeStruct(weight.shape, BF16),
        ],
        parts + [early] + others + [peer, weight],
        [pltpu.VMEM((2 * area, lanes), F32), pltpu.SemaphoreType.DMA((9,))],
        loose=(4,),
    )
    cell = shape(2 * CELLS, lanes, F32)
    part = pltpu.VMEM((2 * CELLS, 2 * lanes), F32)
    work = 2 * 27 * CELLS * lanes * CHANNELS
    straight, crossed, left = call(
        far_adjoint_kernel,
        [shape(2 * CELLS, lanes)] * 2 + [jax.ShapeDtypeStruct((2, 9, 2 * CELLS, lanes), BF16)],
        [taps, weight] + pieces,
        [part, pltpu.VMEM((4 * ROWS, lanes), F32)],
        flops=work,
    )
    mine, twin = call(
        near_adjoint_kernel,
        [cell, shape(2 * CELLS, lanes)],
        [left, weight],
        [part],
        flops=work,
    )
    sends = chan_swaps([twin, straight, crossed])
    hat, slope, scale, cells = call(
        pair_norm_kernel,
        [cell, cell, shape(2, lanes, F32), shape(CELLS + 2 * ROWS, lanes)],
        pieces + [take, gain, shift],
        flops=6 * CELLS * members * own * lanes,
    )
    received = chan_swaps([cells] * 3)
    routed = call(
        back_kernel,
        [shape(2 * capacity + more, lanes) for more in (0, 16, 32, 0)],
        [mine, hat, slope, scale, pack] + sends,
    )
    returned = [routed[0]] + [swapped(r, "tile", 2 * k + 2) for k, r in enumerate(routed[1:])]
    return cells, received, weight, bias, put, returned


def tile_plan(tokens, cell_source, gain, shift, weight, bias, lines):
    own, lanes = tokens.shape
    members = lax.axis_size("tile")
    across = across_tiles()
    multi = members > across
    capacity = max(2, own // (members // 2))
    slots = members * capacity
    high, wide = 2 * TILE_H, 2 * TILE_W
    area = lines.shape[0]
    neighbours = [(0, -1), (0, 0), (0, 1)]
    if multi:
        neighbours = [(r, c) for r in (-1, 0, 1) for c in (-1, 0, 1)]
    gathered = lax.all_gather(tokens, "tile", axis=0, tiled=True)
    others = [along_row(lines[wide - 1 :: wide], 1), along_row(lines[::wide], -1)]
    if multi:
        side = (FRAMES, high, 1, lanes)
        widened = [others[0].reshape(side), lines.reshape(FRAMES, high, wide, lanes)]
        widened = jnp.concatenate(widened + [others[1].reshape(side)], axis=2)
        for edge, step, line in ((widened[:, -1], 1, 0), (widened[:, 0], -1, TILE_H - 1)):
            rim = along_column(edge, step).transpose(1, 0, 2)
            spaced = jnp.zeros((wide + 2, FRAMES, TILE_H, lanes), BF16).at[:, :, line].set(rim)
            others.append(spaced.reshape(wide + 2, ROWS, lanes))
    ins = [cell_source, lines, weight] + [v.reshape(1, lanes) for v in (gain, shift, bias)]
    take, pack, put, grid, weight, gain, shift, bias = call(
        functools.partial(tile_prep_kernel, across, neighbours, own, capacity),
        [
            shape(len(neighbours) * CELLS, members * own),
            shape(slots, CELLS),
            shape(own, slots),
            shape(area, lanes, F32),
        ]
        + [jax.ShapeDtypeStruct(v.shape, v.dtype) for v in ins[2:]],
        ins,
        [
            pltpu.VMEM(cell_source.shape, jnp.int32),
            pltpu.VMEM(lines.shape, BF16),
            pltpu.SemaphoreType.DMA((len(ins),)),
        ],
        loose=range(len(ins)),
    )
    cell = shape(CELLS, lanes, F32)
    mine, *sends = call(
        tile_adjoint_kernel,
        [cell] + [shape(CELLS, lanes)] * 3,
        [grid, weight] + others,
        [pltpu.VMEM((CELLS, CHANNELS), F32), pltpu.VMEM((4 * ROWS, lanes), F32)],
        flops=2 * 27 * CELLS * lanes * CHANNELS,
    )
    sends = chan_swaps(sends)
    size = (CELLS + 2 * ROWS) * (3 if multi else 1)
    hat, slope, scale, cells = call(
        functools.partial(tile_norm_kernel, members, across, neighbours),
        [cell, cell, shape(1, lanes, F32), shape(size, lanes)],
        [gathered, take, gain, shift],
        flops=2 * len(neighbours) * CELLS * members * own * lanes,
    )
    received = chan_swaps([cells] * 3)
    (packed,) = call(back_kernel, [shape(slots, lanes)], [mine, hat, slope, scale, pack] + sends)
    returned = lax.all_to_all(packed, "tile", split_axis=0, concat_axis=0, tiled=True)
    return cells, received, weight, bias, put, [returned]


def local(tokens, cell_source, gain, shift, weight, bias, cotangent):
    own, lanes = tokens.shape
    lines = cotangent.reshape(-1, lanes)
    members = lax.axis_size("tile")
    plan = pair_plan if members == 8 else tile_plan
    cells, received, weight, bias, put, returned = plan(
        tokens, cell_source, gain, shift, weight, bias, lines
    )
    (decoded,) = call(
        functools.partial(conv_kernel, members > across_tiles()),
        [shape(lines.shape[0], lanes)],
        [cells] + received + [weight, bias],
        [pltpu.VMEM(lines.shape, F32)],
        flops=2 * 27 * (CELLS + 2 * ROWS) * lanes * CHANNELS,
    )
    (token_grad,) = call(place_kernel, [shape(own, lanes)], [put] + returned)
    return decoded.reshape(cotangent.shape), token_grad


def solution(mesh):
    in_specs = (
        P("tile", "chan"),
        P(),
        P("chan"),
        P("chan"),
        P(None, None, "chan"),
        P("chan"),
        P("tile", None, None, None, "chan"),
    )
    out_specs = (P("tile", None, None, None, "chan"), P("tile", "chan"))
    return jax.shard_map(local, mesh=mesh, in_specs=in_specs, out_specs=out_specs, check_vma=False)
```
